32 devices in a mesh: page: 8 (over z, x), band: 4 (over y, core).
Axes of the slice: x: 2, y: 2, z: 4, core: 2. Of those that a mesh axis runs over, the one named last changes fastest.
Arguments:
- hidden: bfloat16 [16, 4, 128, 768], P('page', 'band'), may hold values from -6 to 6
- boxes: int32 [4, 16, 4, 128], P(None, 'page', 'band'), may hold values from 0 to 2599, as said below
- page_size: int32 [2, 16], P(None, 'page'), may hold values from 600 to 2599, as said below
- band_count: int32 [16, 4], P('page', 'band'), may hold values from 1 to 128, as said below
- layout_tables: bfloat16 [4, 1024, 768], P(None, ('page', 'band')), may hold values from -1.75 to 1.75
- attn_in: bfloat16 [2, 768, 2304], P(None, ('page', 'band')), may hold values from -0.21875 to 0.21875
- attn_bias: bfloat16 [2, 2, 768], P(None, None, ('page', 'band')), may hold values from -3 to 3
- attn_out: bfloat16 [2, 768, 768], P(None, ('page', 'band')), may hold values from -1.25 to 1.25
- out_bias: bfloat16 [2, 768], P(None, ('page', 'band')), may hold values from -1.75 to 1.75
- norm_gain: bfloat16 [2, 2, 768], P(None, None, ('page', 'band')), may hold values from 0.5 to 1.5
- norm_bias: bfloat16 [2, 2, 768], P(None, None, ('page', 'band')), may hold values from -1.75 to 1.75
- ffn_in: bfloat16 [2, 768, 3072], P(None, ('page', 'band')), may hold values from -0.21875 to 0.21875
- ffn_in_bias: bfloat16 [2, 3072], P(None, ('page', 'band')), may hold values from -3 to 3
- ffn_out: bfloat16 [2, 3072, 768], P(None, ('page', 'band')), may hold values from -0.109375 to 0.109375
- ffn_out_bias: bfloat16 [2, 768], P(None, ('page', 'band')), may hold values from -1.75 to 1.75
- out_grad: bfloat16 [16, 4, 128, 768], P('page', 'band'), may hold values from -6 to 6
Outputs:
- output: float32 [16, 4, 128, 768], P('page', 'band')
- input_grad: float32 [16, 4, 128, 768], P('page', 'band')
- grad_layout_tables: float32 [4, 1024, 768], P(None, ('page', 'band'))
- grad_attn_in: float32 [2, 768, 2304], P(None, ('page', 'band'))
- grad_attn_bias: float32 [2, 2, 768], P(None, None, ('page', 'band'))
- grad_attn_out: float32 [2, 768, 768], P(None, ('page', 'band'))
- grad_out_bias: float32 [2, 768], P(None, ('page', 'band'))
- grad_norm_gain: float32 [2, 2, 768], P(None, None, ('page', 'band'))
- grad_norm_bias: float32 [2, 2, 768], P(None, None, ('page', 'band'))
- grad_ffn_in: float32 [2, 768, 3072], P(None, ('page', 'band'))
- grad_ffn_in_bias: float32 [2, 3072], P(None, ('page', 'band'))
- grad_ffn_out: float32 [2, 3072, 768], P(None, ('page', 'band'))
- grad_ffn_out_bias: float32 [2, 768], P(None, ('page', 'band'))
The draws below stay inside these ranges and needn't reach their ends.
Inputs may be any that keep to these rules, and one draw needn't show every extreme that they name: `band_count`: in every page one band holds 128 live tokens; live tokens fill the first slots of their band. `boxes`: left <= right <= the page's width and top <= bottom <= the page's height. `page_size`: widths from 600 to 1999, heights from 800 to 2599.
All inputs are finite; a program needn't handle non-finite values.
Results may differ from the reference program's by a relative error of at most 0.02.
Values may be sent and summed in bfloat16 or wider, within the bound.
No kernel may reach another device: no remote copies, remote signals or barrier semaphores. Data moves between devices by JAX's collectives and lax.ppermute only.
A program may use at most 256 MiB of HBM per device.

```python
import jax
import jax.numpy as jnp
from jax import lax

D = 768
HEADS = 12
HEAD_DIM = 64
FF = 3072
POS = 1024
GRID = 1000
LAYERS = 2
SLOTS = 512
CAP = 128
PAGES_DEV = 2
PAGES = 16
N_BAND = 4


def page_dims(key):
    base_key = jax.random.fold_in(key, 17)
    widths = jax.random.randint(jax.random.fold_in(base_key, 1), (PAGES,), 600, 2000)
    heights = jax.random.randint(jax.random.fold_in(base_key, 2), (PAGES,), 800, 2600)
    widths = widths.at[0].set(600)
    heights = heights.at[0].set(2599)
    return (widths, heights)


def draw_page_size(key, part):
    widths, heights = page_dims(key)
    return jnp.stack([widths, heights]).astype(jnp.int32)


def draw_boxes(key, part):
    widths, heights = page_dims(key)
    box_shape = (PAGES, N_BAND, CAP)
    page_wide = widths[:, None, None]
    page_tall = heights[:, None, None]
    box_left = jax.random.randint(jax.random.fold_in(key, 31), box_shape, 0, page_wide)
    box_right = jnp.minimum(box_left + jax.random.randint(jax.random.fold_in(key, 32), box_shape, 10, 400), page_wide)
    band_step = page_tall // N_BAND
    band_start = jnp.arange(N_BAND, dtype=jnp.int32)[None, :, None] * band_step
    box_top = band_start + jax.random.randint(jax.random.fold_in(key, 33), box_shape, 0, band_step)
    box_bottom = jnp.minimum(box_top + jax.random.randint(jax.random.fold_in(key, 34), box_shape, 8, 60), page_tall)
    box_left = box_left.at[:, N_BAND - 1, CAP - 1].set(0)
    box_right = box_right.at[:, N_BAND - 1, CAP - 1].set(widths)
    box_bottom = box_bottom.at[:, N_BAND - 1, CAP - 1].set(heights)
    return jnp.stack([box_left, box_top, box_right, box_bottom]).astype(jnp.int32)


def draw_band_count(key, part):
    full_band = jax.random.randint(jax.random.fold_in(key, 41), (PAGES,), 0, N_BAND)
    others = jax.random.randint(jax.random.fold_in(key, 42), (PAGES, N_BAND), 1, max(2, CAP * 7 // 8))
    band_number = jnp.arange(N_BAND, dtype=jnp.int32)[None, :]
    return jnp.where(band_number == full_band[:, None], CAP, others).astype(jnp.int32)


def steps_of(rng, extent, split, low, high):
    def one(dim, shards_of):
        steps = jax.random.uniform(jax.random.fold_in(jax.random.fold_in(rng, 6), dim), (shards_of,), jnp.float32, low / len(split), high / len(split))
        return jnp.repeat(jnp.exp(steps), extent[dim] // shards_of).reshape((-1,) + (1,) * (len(extent) - dim - 1))

    factor_of = one(*split[0])
    for cut in split[1:]:
        factor_of = factor_of * one(*cut)
    return factor_of


def scatter_about(rng, dims, width, most, split=(), kind=jnp.bfloat16):
    loudness = steps_of(rng, dims, split, -0.22, 0.18) if split else 1.0
    drawn = jax.random.normal(rng, dims, jnp.float32) * width * loudness
    return jnp.minimum(jnp.maximum(drawn, -most), most).astype(kind)


def setup_inputs(seed: int = 0) -> dict:
    arg_keys = jax.random.split(jax.random.key(seed), 17)
    hidden = scatter_about(arg_keys[0], (PAGES, N_BAND, CAP, D), 1.0, 6.0, ((0, 8), (1, 4)))
    boxes = draw_boxes(jax.random.fold_in(arg_keys[16], 71), 0)
    page_size = draw_page_size(jax.random.fold_in(arg_keys[16], 71), 0)
    band_count = draw_band_count(jax.random.fold_in(arg_keys[16], 71), 0)
    layout_tables = scatter_about(arg_keys[4], (4, POS, D), 0.3, 1.75, ((1, 32),))
    attn_in = scatter_about(arg_keys[5], (LAYERS, D, 3 * D), D ** -0.5, 0.21875, ((1, 32),))
    attn_bias = scatter_about(arg_keys[6], (LAYERS, 2, D), 0.5, 3.0, ((2, 32),))
    attn_out = scatter_about(arg_keys[7], (LAYERS, D, D), (D // 32) ** -0.5, 1.25, ((1, 32),))
    out_bias = scatter_about(arg_keys[8], (LAYERS, D), 0.3, 1.75, ((1, 32),))
    norm_gain = jnp.clip(1.0 + 0.1 * jax.random.normal(arg_keys[9], (LAYERS, 2, D), jnp.float32), 0.5, 1.5).astype(jnp.bfloat16)
    norm_bias = scatter_about(arg_keys[10], (LAYERS, 2, D), 0.3, 1.75, ((2, 32),))
    ffn_in = scatter_about(arg_keys[11], (LAYERS, D, FF), D ** -0.5, 0.21875, ((1, 32),))
    ffn_in_bias = scatter_about(arg_keys[12], (LAYERS, FF), 0.5, 3.0, ((1, 32),))
    ffn_out = scatter_about(arg_keys[13], (LAYERS, FF, D), FF ** -0.5, 0.109375, ((1, 32),))
    ffn_out_bias = scatter_about(arg_keys[14], (LAYERS, D), 0.3, 1.75, ((1, 32),))
    out_grad = scatter_about(arg_keys[15], (PAGES, N_BAND, CAP, D), 1.0, 6.0, ((0, 8), (1, 4)))
    return {"hidden": hidden, "boxes": boxes, "page_size": page_size, "band_count": band_count, "layout_tables": layout_tables, "attn_in": attn_in, "attn_bias": attn_bias, "attn_out": attn_out, "out_bias": out_bias, "norm_gain": norm_gain, "norm_bias": norm_bias, "ffn_in": ffn_in, "ffn_in_bias": ffn_in_bias, "ffn_out": ffn_out, "ffn_out_bias": ffn_out_bias, "out_grad": out_grad}


@jax.custom_vjp
def low(v):
    return lax.optimization_barrier(v.astype(jnp.bfloat16)).astype(jnp.float32)

@jax.custom_vjp
def low_back(v):
    return v

def low_keep(v):
    return (low(v), None)

def low_pass(kept, grad):
    return (grad,)

def back_keep(v):
    return (v, None)

def back_low(kept, grad):
    return (low(grad),)
low.defvjp(low_keep, low_pass)
low_back.defvjp(back_keep, back_low)
exact_prec = lax.Precision.HIGHEST
norm_eps = 1e-12
table_pick = (0, 1, 0, 1, 2, 3)

def layer_norm(hidden_rows, gain_row, shift_row):
    row_mean = lax.optimization_barrier(jnp.mean(hidden_rows, axis=-1, keepdims=True))
    centred = hidden_rows - row_mean
    row_var = lax.optimization_barrier(jnp.mean(centred * centred, axis=-1, keepdims=True))
    return centred * lax.rsqrt(row_var + norm_eps) * gain_row + shift_row

def gelu_exact(values):
    return jax.nn.gelu(values, approximate=False)

def layout_index(boxes, page_size, band_count):
    widths = page_size[0][:, None, None]
    heights = page_size[1][:, None, None]
    box_left = boxes[0] * GRID // widths
    box_top = boxes[1] * GRID // heights
    box_right = boxes[2] * GRID // widths
    box_bottom = boxes[3] * GRID // heights
    box_index = jnp.stack([box_left, box_top, box_right, box_bottom, box_bottom - box_top, box_right - box_left])
    slot_index = lax.broadcasted_iota(jnp.int32, box_left.shape, 2)
    live_mask = slot_index < band_count[:, :, None]
    return (box_index.reshape(6, PAGES, SLOTS), live_mask.reshape(PAGES, SLOTS))

def page_attention(packed):
    queries, keys_page, values_page, live_page = packed
    scores = jnp.einsum('qhd,khd->hqk', queries, keys_page, precision=exact_prec) * HEAD_DIM ** (-0.5)
    scores = low_back(jnp.where(live_page[None, None, :], scores, -1000000000.0))
    row_peak = lax.optimization_barrier(jnp.max(scores, axis=-1, keepdims=True))
    exponent = jnp.exp(scores - row_peak)
    attn_probs = low(exponent / lax.optimization_barrier(jnp.sum(exponent, axis=-1, keepdims=True)))
    return jnp.einsum('hqk,khd->qhd', attn_probs, values_page, precision=exact_prec)

def encoder_layer(layer_rows, live_mask, weights):
    in_proj, in_bias, out_proj, out_shift, norm_gains, shifts, up_proj, up_shift, down_proj, down_shift = weights
    joint_proj = jnp.einsum('gsd,de->gse', low(layer_rows), in_proj, precision=exact_prec)
    queries = low(low_back(joint_proj[..., :D] + in_bias[0]))
    keys_all = low(low_back(joint_proj[..., D:2 * D]))
    values_all = low(low_back(joint_proj[..., 2 * D:] + in_bias[1]))
    head_shape = (layer_rows.shape[0], SLOTS, HEADS, HEAD_DIM)
    attend = jax.checkpoint(page_attention)
    attn_mixed = lax.map(attend, (queries.reshape(head_shape), keys_all.reshape(head_shape), values_all.reshape(head_shape), live_mask))
    attn_mixed = low(low_back(attn_mixed.reshape(layer_rows.shape)))
    branch = low_back(jnp.einsum('gse,ed->gsd', attn_mixed, out_proj, precision=exact_prec) + out_shift)
    first_out = layer_norm(layer_rows + branch, norm_gains[0], shifts[0])
    up_rows = low_back(jnp.einsum('gsd,df->gsf', low(first_out), up_proj, precision=exact_prec) + up_shift)
    activated = low(gelu_exact(up_rows))
    down_rows = low_back(jnp.einsum('gsf,fd->gsd', activated, down_proj, precision=exact_prec) + down_shift)
    return layer_norm(first_out + down_rows, norm_gains[1], shifts[1])

def group_forward(params, hidden_rows, box_index, live_mask):
    tables = params[0]
    layer_rows = hidden_rows
    for lookup_number in range(6):
        layer_rows = layer_rows + tables[table_pick[lookup_number]][box_index[lookup_number]]
    for layer_number in range(LAYERS):
        layer_rows = encoder_layer(layer_rows, live_mask, tuple((member[layer_number] for member in params[1:])))
    return layer_rows * live_mask[..., None].astype(jnp.float32)

def reference(hidden, boxes, page_size, band_count, layout_tables, attn_in, attn_bias, attn_out, out_bias, norm_gain, norm_bias, ffn_in, ffn_in_bias, ffn_out, ffn_out_bias, out_grad):
    params = tuple((member.astype(jnp.float32) for member in (layout_tables, attn_in, attn_bias, attn_out, out_bias, norm_gain, norm_bias, ffn_in, ffn_in_bias, ffn_out, ffn_out_bias)))
    box_index, live_mask = layout_index(boxes, page_size, band_count)
    groups = PAGES // PAGES_DEV
    hidden_groups = hidden.astype(jnp.float32).reshape(groups, PAGES_DEV, SLOTS, D)
    grad_groups = out_grad.astype(jnp.float32).reshape(groups, PAGES_DEV, SLOTS, D)
    index_groups = box_index.reshape(6, groups, PAGES_DEV, SLOTS).transpose(1, 0, 2, 3)
    live_groups = live_mask.reshape(groups, PAGES_DEV, SLOTS)

    def group_step(totals, packed):
        hidden_rows, grad_rows, index_rows, live_rows = packed
        result, pull_back = jax.vjp(lambda weights, inputs: group_forward(weights, inputs, index_rows, live_rows), params, hidden_rows)
        grad_params, grad_inputs = pull_back(grad_rows)
        return (jax.tree.map(jnp.add, totals, grad_params), (result, grad_inputs))
    zero_grads = jax.tree.map(jnp.zeros_like, params)
    totals, (result, input_grad) = lax.scan(group_step, zero_grads, (hidden_groups, grad_groups, index_groups, live_groups))
    out_shape = (PAGES, N_BAND, CAP, D)
    return (result.reshape(out_shape), input_grad.reshape(out_shape), totals[0], totals[1], totals[2], totals[3], totals[4], totals[5], totals[6], totals[7], totals[8], totals[9], totals[10])
```

```python
import functools

import jax
import jax.numpy as jnp
from jax import lax
from jax.experimental import pallas as pl
from jax.experimental.pallas import tpu as pltpu
from jax.sharding import PartitionSpec as P

D = 768
HEADS = 12
HEAD_DIM = 64
HALF = D // 2
PAIRS = HEADS // 4
FF = 3072
POS = 1024
GRID = 1000
LAYERS = 2
CORES = 2
LANES = 128
EPS = 1e-12
DEAD = -1000000000.0
SCALE = HEAD_DIM ** (-0.5)
VMEM = 40 * 1024 * 1024
F32 = jnp.float32
BF16 = jnp.bfloat16

ROW_ATTN, ROW_OUT, ROW_GAIN, ROW_SHIFT, ROW_DOWN = 0, 4, 6, 10, 14
SMALL_ROWS = 16


def dot(a, b, dims=((1,), (0,))):
    return lax.dot_general(a, b, (dims, ((), ())), preferred_element_type=F32)


NT = ((1,), (1,))
TN = ((0,), (0,))


def sds(shape, dtype):
    return jax.ShapeDtypeStruct(shape, dtype)


def whole(shape):
    return pl.BlockSpec(shape, lambda *_: (0,) * len(shape))


def cost(flops, nbytes, trans=0):
    return pl.CostEstimate(flops=flops, bytes_accessed=nbytes, transcendentals=trans)


def params():
    return pltpu.CompilerParams(vmem_limit_bytes=VMEM)


def embed_kernel(idx, t0, t1, t2, t3, out):
    rows = t0.shape[0]
    place = lax.broadcasted_iota(jnp.int32, (idx.shape[0], rows), 1)

    def hot(*cols):
        total = None
        for col in cols:
            one = jnp.where(place == idx[:, col : col + 1], 1.0, 0.0)
            total = one if total is None else total + one
        return total.astype(BF16)

    out[...] = (
        dot(hot(0, 2), t0[...])
        + dot(hot(1, 3), t1[...])
        + dot(hot(4), t2[...])
        + dot(hot(5), t3[...])
    )


def embed(idx, tables):
    tokens = idx.shape[0]
    block = 128
    rows = tables[0].shape[0]
    return pl.pallas_call(
        embed_kernel,
        name="embed",
        out_shape=sds((tokens, D), F32),
        grid=(tokens // block,),
        in_specs=[pl.BlockSpec((block, 8), lambda i: (i, 0))] + [whole((rows, D))] * 4,
        out_specs=pl.BlockSpec((block, D), lambda i: (i, 0)),
        compiler_params=params(),
        cost_estimate=cost(8 * tokens * rows * D, 8 * rows * D + 4 * tokens * D),
    )(idx, *tables)


def table_kernel(idx, own, sib, o0, o1, o2, o3):
    half = own.shape[0]
    block = o0.shape[0]
    first = pl.program_id(0) * block
    place = lax.broadcasted_iota(jnp.int32, (block, 2 * half), 0) + first

    def hot(*rows):
        total = None
        for row in rows:
            one = jnp.where(place == idx[row : row + 1, :], 1.0, 0.0)
            total = one if total is None else total + one
        return total.astype(BF16)

    for out, rows in ((o0, (0, 2)), (o1, (1, 3)), (o2, (4,)), (o3, (5,))):
        mark = hot(*rows)
        out[...] = (dot(mark[:, :half], own[...]) + dot(mark[:, half:], sib[...])).astype(BF16)


def table_grads(idx, own, sib, rows):
    half = own.shape[0]
    block = 256
    return pl.pallas_call(
        table_kernel,
        name="table_grads",
        out_shape=[sds((rows, D), BF16)] * 4,
        grid=(rows // block,),
        in_specs=[whole((8, 2 * half)), whole((half, D)), whole((half, D))],
        out_specs=[pl.BlockSpec((block, D), lambda i: (i, 0))] * 4,
        compiler_params=params(),
        cost_estimate=cost(16 * half * rows * D, 8 * rows * D),
    )(idx, own, sib)


def attn_fwd_kernel(core, xo, xs, wq, wk, wv, small, mask, q, k, v, mo, ms, *, layer):
    half = xo.shape[0]
    for first, rows in ((0, xo), (half, xs)):
        x = rows[...]
        q[first : first + half, :] = (
            dot(x, wq[...]) + small[ROW_ATTN + 2 * layer : ROW_ATTN + 2 * layer + 1, :]
        ).astype(BF16)
        k[first : first + half, :] = dot(x, wk[...]).astype(BF16)
        v[first : first + half, :] = (
            dot(x, wv[...]) + small[ROW_ATTN + 2 * layer + 1 : ROW_ATTN + 2 * layer + 2, :]
        ).astype(BF16)
    keys, values = k[...], v[...]
    low_lanes = lax.broadcasted_iota(jnp.int32, (1, LANES), 1) < HEAD_DIM
    for first, out in ((0, mo), (half, ms)):
        queries = q[first : first + half, :].astype(F32) * SCALE
        parts = []
        for head in range(2):
            lanes = low_lanes if head == 0 else jnp.logical_not(low_lanes)
            one = jnp.where(lanes, queries, 0.0).astype(BF16)
            scores = dot(one, keys, NT) + mask[...]
            expo = jnp.exp(scores - jnp.max(scores, axis=-1, keepdims=True))
            total = jnp.sum(expo, axis=-1, keepdims=True)
            parts.append(dot(expo.astype(BF16), values) / total)
        out[...] = jnp.where(low_lanes, parts[0], parts[1]).astype(BF16)


def attn_fwd(core, xo, xs, wq, wk, wv, small, mask, layer):
    half = xo.shape[0]
    tokens = 2 * half
    col = lambda p, core: (0, p)
    weight = pl.BlockSpec((D, LANES), col)
    rows = pl.BlockSpec((tokens, LANES), col)
    return pl.pallas_call(
        functools.partial(attn_fwd_kernel, layer=layer),
        name="attn_fwd",
        out_shape=[sds((tokens, HALF), BF16)] * 3 + [sds((half, HALF), BF16)] * 2,
        grid_spec=pltpu.PrefetchScalarGridSpec(
            num_scalar_prefetch=1,
            grid=(PAIRS,),
            in_specs=[
                whole((half, D)),
                whole((half, D)),
                weight,
                weight,
                weight,
                pl.BlockSpec((SMALL_ROWS, LANES), lambda p, core: (0, core[0] * PAIRS + p)),
                whole((1, tokens)),
            ],
            out_specs=[rows] * 3 + [pl.BlockSpec((half, LANES), col)] * 2,
        ),
        compiler_params=params(),
        cost_estimate=cost(
            2 * tokens * D * 3 * HALF + 4 * PAIRS * 2 * tokens * tokens * LANES,
            2 * (tokens * D + 3 * D * HALF + 4 * tokens * HALF),
            PAIRS * 2 * tokens * tokens,
        ),
    )(core, xo, xs, wq, wk, wv, small, mask)


def attn_bwd_kernel(
    core, dao, das, wo, q, k, v, mo, ms, xo, xs, wq, wk, wv, mask,
    dwq, dwk, dwv, dwo, sums, dxo, dxs, acc, dq_s, dk_s, dv_s,
):
    half = xo.shape[0]
    step = pl.program_id(0)
    keys, values = k[...], v[...]
    low_lanes = lax.broadcasted_iota(jnp.int32, (1, LANES), 1) < HEAD_DIM
    grad_keys = [None, None]
    grad_values = [None, None]
    for part, da in ((0, dao), (1, das)):
        first = part * half
        span = slice(first, first + half)
        grad_mix = dot(da[...], wo[...], NT)
        queries = q[span, :].astype(F32) * SCALE
        grad_queries = []
        for head in range(2):
            lanes = low_lanes if head == 0 else jnp.logical_not(low_lanes)
            one = jnp.where(lanes, queries, 0.0).astype(BF16)
            scores = dot(one, keys, NT) + mask[...]
            expo = jnp.exp(scores - jnp.max(scores, axis=-1, keepdims=True))
            probs = expo * (1.0 / jnp.sum(expo, axis=-1, keepdims=True))
            grad_one = jnp.where(lanes, grad_mix, 0.0).astype(BF16)
            grad_probs = dot(grad_one, values, NT)
            weighted = probs * grad_probs
            delta = jnp.sum(weighted, axis=-1, keepdims=True)
            grad_scores = (weighted - probs * delta).astype(BF16)
            grad_queries.append(dot(grad_scores, keys))
            key_part = dot(grad_scores, one, TN)
            value_part = dot(probs.astype(BF16), grad_one, TN)
            if part == 0:
                grad_keys[head], grad_values[head] = key_part, value_part
            else:
                grad_keys[head] = grad_keys[head] + key_part
                grad_values[head] = grad_values[head] + value_part
        dq_s[span, :] = (jnp.where(low_lanes, grad_queries[0], grad_queries[1]) * SCALE).astype(BF16)
    dk_s[...] = (grad_keys[0] + grad_keys[1]).astype(BF16)
    dv_s[...] = (grad_values[0] + grad_values[1]).astype(BF16)
    sums[...] = jnp.zeros_like(sums)
    sums[0:1, :] = jnp.sum(dq_s[...].astype(F32), axis=0, keepdims=True)
    sums[1:2, :] = jnp.sum(dv_s[...].astype(F32), axis=0, keepdims=True)
    for out, grad in ((dwq, dq_s), (dwk, dk_s), (dwv, dv_s)):
        out[...] = (dot(xo[...], grad[:half, :], TN) + dot(xs[...], grad[half:, :], TN)).astype(BF16)
    out_rows = dot(mo[...], dao[...], TN) + dot(ms[...], das[...], TN)
    dwo[0] = out_rows[:, :HALF].astype(BF16)
    dwo[1] = out_rows[:, HALF:].astype(BF16)
    total = dot(dq_s[...], wq[...], NT) + dot(dk_s[...], wk[...], NT) + dot(dv_s[...], wv[...], NT)

    @pl.when(step == 0)
    def _():
        acc[...] = total

    @pl.when(step > 0)
    def _():
        acc[...] += total

    @pl.when(step == PAIRS - 1)
    def _():
        dxo[...] = acc[:half, :]
        dxs[...] = acc[half:, :].astype(BF16)


def attn_bwd(core, dao, das, wo, q, k, v, mo, ms, xo, xs, wq, wk, wv, mask):
    half = xo.shape[0]
    tokens = 2 * half
    col = lambda p, core: (0, p)
    weight = pl.BlockSpec((D, LANES), col)
    rows = pl.BlockSpec((tokens, LANES), col)
    part = pl.BlockSpec((half, LANES), col)
    return pl.pallas_call(
        attn_bwd_kernel,
        name="attn_bwd",
        out_shape=[sds((D, HALF), BF16)] * 3
        + [
            sds((CORES, HALF, HALF), BF16),
            sds((8, HALF), F32),
            sds((half, D), F32),
            sds((half, D), BF16),
        ],
        grid_spec=pltpu.PrefetchScalarGridSpec(
            num_scalar_prefetch=1,
            grid=(PAIRS,),
            in_specs=[
                whole((half, D)),
                whole((half, D)),
                pl.BlockSpec((LANES, D), lambda p, core: (core[0] * PAIRS + p, 0)),
                rows,
                rows,
                rows,
                part,
                part,
                whole((half, D)),
                whole((half, D)),
                weight,
                weight,
                weight,
                whole((1, tokens)),
            ],
            out_specs=[weight] * 3
            + [
                pl.BlockSpec((CORES, LANES, HALF), lambda p, core: (0, p, 0)),
                pl.BlockSpec((8, LANES), col),
                whole((half, D)),
                whole((half, D)),
            ],
            scratch_shapes=[pltpu.VMEM((tokens, D), F32)] + [pltpu.VMEM((tokens, LANES), BF16)] * 3,
        ),
        compiler_params=params(),
        cost_estimate=cost(
            8 * tokens * D * 3 * HALF // 2 + 10 * PAIRS * 2 * tokens * tokens * LANES,
            2 * (4 * tokens * D + 8 * D * HALF + 4 * tokens * HALF),
            PAIRS * 2 * tokens * tokens,
        ),
    )(core, dao, das, wo, q, k, v, mo, ms, xo, xs, wq, wk, wv, mask)


def norm_rows(h, gain, shift, y, yb, n, rstd):
    mean = jnp.mean(h, axis=-1, keepdims=True)
    centred = h - mean
    scale = lax.rsqrt(jnp.mean(centred * centred, axis=-1, keepdims=True) + EPS)
    normal = centred * scale
    out = normal * gain + shift
    y[...] = out
    yb[...] = out.astype(BF16)
    n[...] = normal
    rstd[...] = scale


def norm_outs(half):
    return [sds((half, D), F32), sds((half, D), BF16), sds((half, D), F32), sds((half, 1), F32)]


def out_norm_kernel(core, mine, theirs, wo, base, small, y, yb, n, rstd, *, layer):
    first = core[0] * HALF
    mine_rows = pl.ds(pl.multiple_of(first, HALF), HALF)
    their_rows = pl.ds(pl.multiple_of(HALF - first, HALF), HALF)
    h = (
        base[...]
        + dot(mine[...], wo[mine_rows, :])
        + dot(theirs[...], wo[their_rows, :])
        + small[ROW_OUT + layer : ROW_OUT + layer + 1, :]
    )
    row = 2 * layer
    norm_rows(
        h, small[ROW_GAIN + row : ROW_GAIN + row + 1, :], small[ROW_SHIFT + row : ROW_SHIFT + row + 1, :],
        y, yb, n, rstd,
    )


def out_norm(core, mine, theirs, wo, base, small, layer):
    half = base.shape[0]
    return pl.pallas_call(
        functools.partial(out_norm_kernel, layer=layer),
        name="out_norm",
        out_shape=norm_outs(half),
        in_specs=[pl.BlockSpec(memory_space=pltpu.SMEM)] + [pl.BlockSpec(memory_space=pltpu.VMEM)] * 5,
        out_specs=[pl.BlockSpec(memory_space=pltpu.VMEM)] * 4,
        compiler_params=params(),
        cost_estimate=cost(2 * half * D * D, 2 * D * D + 16 * half * D),
    )(core, mine, theirs, wo, base, small)


def add_norm_kernel(base, part, recv, small, y, yb, n, rstd, *, layer):
    h = base[...] + part[...] + recv[...].astype(F32) + small[ROW_DOWN + layer : ROW_DOWN + layer + 1, :]
    row = 2 * layer + 1
    norm_rows(
        h, small[ROW_GAIN + row : ROW_GAIN + row + 1, :], small[ROW_SHIFT + row : ROW_SHIFT + row + 1, :],
        y, yb, n, rstd,
    )


def add_norm(base, part, recv, small, layer):
    half = base.shape[0]
    return pl.pallas_call(
        functools.partial(add_norm_kernel, layer=layer),
        name="add_norm",
        out_shape=norm_outs(half),
        in_specs=[pl.BlockSpec(memory_space=pltpu.VMEM)] * 4,
        out_specs=[pl.BlockSpec(memory_space=pltpu.VMEM)] * 4,
        compiler_params=params(),
        cost_estimate=cost(20 * half * D, 20 * half * D),
    )(base, part, recv, small)


def norm_bwd_kernel(*refs, row, summed):
    if summed:
        base, part, recv, n, rstd, small, gh, ghb, sums = refs
        gz = base[...] + part[...] + recv[...].astype(F32)
    else:
        base, live, n, rstd, small, gh, ghb, sums = refs
        gz = base[...].astype(F32) * live[...]
    normal = n[...]
    e = gz * small[ROW_GAIN + row : ROW_GAIN + row + 1, :]
    mean = jnp.mean(e, axis=-1, keepdims=True)
    slope = jnp.mean(e * normal, axis=-1, keepdims=True)
    grad = (e - mean - normal * slope) * rstd[...]
    low = grad.astype(BF16)
    gh[...] = grad
    ghb[...] = low
    sums[...] = jnp.zeros_like(sums)
    sums[0:1, :] = jnp.sum(gz * normal, axis=0, keepdims=True)
    sums[1:2, :] = jnp.sum(gz, axis=0, keepdims=True)
    sums[2:3, :] = jnp.sum(low.astype(F32), axis=0, keepdims=True)


def norm_bwd(sources, n, rstd, small, row):
    half = n.shape[0]
    operands = tuple(sources) + (n, rstd, small)
    return pl.pallas_call(
        functools.partial(norm_bwd_kernel, row=row, summed=len(sources) == 3),
        name="norm_bwd",
        out_shape=[sds((half, D), F32), sds((half, D), BF16), sds((8, D), F32)],
        in_specs=[pl.BlockSpec(memory_space=pltpu.VMEM)] * len(operands),
        out_specs=[pl.BlockSpec(memory_space=pltpu.VMEM)] * 3,
        compiler_params=params(),
        cost_estimate=cost(20 * half * D, 20 * half * D),
    )(*operands)


FF_BLOCK = 256
FF_STEPS = FF // CORES // FF_BLOCK
UNIT_STEPS = FF_STEPS // 2


def first_unit(j):
    return jnp.minimum(j, UNIT_STEPS - 1)


def second_unit(j):
    return jnp.maximum(j - UNIT_STEPS, 0)


def ffn_fwd_kernel(yo, ys, w1a, w1b, bias, w2a, w2b, act, slope, po, ps, acc, *, layer):
    half = yo.shape[0]
    j = pl.program_id(0)
    early = j < UNIT_STEPS
    w1 = jnp.where(early, w1a[...], w1b[...])
    w2 = jnp.where(early, w2a[...], w2b[...])
    for first, rows in ((0, yo), (half, ys)):
        span = slice(first, first + half)
        up = dot(rows[...], w1) + bias[layer : layer + 1, :]
        cdf = 0.5 * (1.0 + lax.erf(up * (2.0**-0.5)))
        low = (up * cdf).astype(BF16)
        act[span, :] = low
        slope[span, :] = (cdf + up * (jnp.exp(-0.5 * up * up) * 0.3989422804014327)).astype(BF16)
        total = dot(low, w2)

        @pl.when(j == 0)
        def _():
            acc[span, :] = total

        @pl.when(j > 0)
        def _():
            acc[span, :] += total

    @pl.when(j == FF_STEPS - 1)
    def _():
        po[...] = acc[:half, :]
        ps[...] = acc[half:, :].astype(BF16)


def ffn_fwd(yo, ys, w1a, w1b, bias, w2a, w2b, layer):
    half = yo.shape[0]
    tokens = 2 * half
    width = FF // CORES
    return pl.pallas_call(
        functools.partial(ffn_fwd_kernel, layer=layer),
        name="ffn_fwd",
        out_shape=[sds((tokens, width), BF16)] * 2 + [sds((half, D), F32), sds((half, D), BF16)],
        grid=(FF_STEPS,),
        in_specs=[
            whole((half, D)),
            whole((half, D)),
            pl.BlockSpec((D, FF_BLOCK), lambda j: (0, first_unit(j))),
            pl.BlockSpec((D, FF_BLOCK), lambda j: (0, second_unit(j))),
            pl.BlockSpec((LAYERS, FF_BLOCK), lambda j: (0, j)),
            pl.BlockSpec((FF_BLOCK, D), lambda j: (first_unit(j), 0)),
            pl.BlockSpec((FF_BLOCK, D), lambda j: (second_unit(j), 0)),
        ],
        out_specs=[pl.BlockSpec((tokens, FF_BLOCK), lambda j: (0, j))] * 2 + [whole((half, D))] * 2,
        scratch_shapes=[pltpu.VMEM((tokens, D), F32)],
        compiler_params=params(),
        cost_estimate=cost(4 * tokens * D * width, 4 * D * width + 4 * tokens * width, tokens * width),
    )(yo, ys, w1a, w1b, bias, w2a, w2b)


def ffn_bwd_kernel(
    dfo, dfs, w1a, w1b, w2a, w2b, act, slope, yo, ys, dw1a, dw1b, dw2a, dw2b, sums, po, ps, acc, du
):
    half = yo.shape[0]
    j = pl.program_id(0)
    early = j < UNIT_STEPS
    w1 = jnp.where(early, w1a[...], w1b[...])
    w2 = jnp.where(early, w2a[...], w2b[...])
    for first, rows in ((0, dfo), (half, dfs)):
        span = slice(first, first + half)
        low = (slope[span, :].astype(F32) * dot(rows[...], w2, NT)).astype(BF16)
        du[span, :] = low
        total = dot(low, w1, NT)

        @pl.when(j == 0)
        def _():
            acc[span, :] = total

        @pl.when(j > 0)
        def _():
            acc[span, :] += total

    sums[...] = jnp.zeros_like(sums)
    sums[0:1, :] = jnp.sum(du[...].astype(F32), axis=0, keepdims=True)
    grad1 = (dot(yo[...], du[:half, :], TN) + dot(ys[...], du[half:, :], TN)).astype(BF16)
    grad2 = (dot(act[:half, :], dfo[...], TN) + dot(act[half:, :], dfs[...], TN)).astype(BF16)

    @pl.when(early)
    def _():
        dw1a[...] = grad1
        dw2a[...] = grad2

    @pl.when(jnp.logical_not(early))
    def _():
        dw1b[...] = grad1
        dw2b[...] = grad2

    @pl.when(j == FF_STEPS - 1)
    def _():
        po[...] = acc[:half, :]
        ps[...] = acc[half:, :].astype(BF16)


def ffn_bwd(dfo, dfs, w1a, w1b, w2a, w2b, act, slope, yo, ys):
    half = yo.shape[0]
    tokens = 2 * half
    width = FF // CORES
    col_a = pl.BlockSpec((D, FF_BLOCK), lambda j: (0, first_unit(j)))
    col_b = pl.BlockSpec((D, FF_BLOCK), lambda j: (0, second_unit(j)))
    row_a = pl.BlockSpec((FF_BLOCK, D), lambda j: (first_unit(j), 0))
    row_b = pl.BlockSpec((FF_BLOCK, D), lambda j: (second_unit(j), 0))
    rows = pl.BlockSpec((tokens, FF_BLOCK), lambda j: (0, j))
    return pl.pallas_call(
        ffn_bwd_kernel,
        name="ffn_bwd",
        out_shape=[sds((D, width // 2), BF16)] * 2
        + [sds((width // 2, D), BF16)] * 2
        + [sds((8, width), F32), sds((half, D), F32), sds((half, D), BF16)],
        grid=(FF_STEPS,),
        in_specs=[whole((half, D))] * 2 + [col_a, col_b, row_a, row_b, rows, rows] + [whole((half, D))] * 2,
        out_specs=[col_a, col_b, row_a, row_b, pl.BlockSpec((8, FF_BLOCK), lambda j: (0, j))]
        + [whole((half, D))] * 2,
        scratch_shapes=[pltpu.VMEM((tokens, D), F32), pltpu.VMEM((tokens, FF_BLOCK), BF16)],
        compiler_params=params(),
        cost_estimate=cost(8 * tokens * D * width, 8 * D * width + 4 * tokens * width),
    )(dfo, dfs, w1a, w1b, w2a, w2b, act, slope, yo, ys)


def shuffle_kernel(table, *refs, moves, count, placed):
    for out, to, source, at in moves:
        if placed:
            refs[count + out][table[to]] = refs[source][at]
        else:
            refs[count + out][to] = refs[source][table[at]]


def shuffle(table, sources, shapes, moves, placed):
    nbytes = sum(4 * source.size for source in sources)
    return pl.pallas_call(
        functools.partial(shuffle_kernel, moves=moves, count=len(sources), placed=placed),
        name="shuffle",
        out_shape=shapes,
        in_specs=[pl.BlockSpec(memory_space=pltpu.SMEM)]
        + [pl.BlockSpec(memory_space=pltpu.VMEM)] * len(sources),
        out_specs=[pl.BlockSpec(memory_space=pltpu.VMEM)] * len(shapes),
        compiler_params=params(),
        cost_estimate=cost(0, nbytes),
    )(table, *sources)


class Places:
    def __init__(self, pages, bands):
        self.ny = bands // CORES
        self.nx = self.ny if pages % self.ny == 0 else 1
        self.nz = pages // self.nx
        self.chips = pages * self.ny
        page, band = lax.axis_index("page"), lax.axis_index("band")
        self.z, self.x = page // self.nx, page % self.nx
        self.y, self.core = band // CORES, band % CORES
        self.sizes = (self.nz, self.nx, self.ny, CORES)

    def shift(self, value, axis, steps):
        pairs = []
        nz, nx, ny, nc = self.sizes
        for device in range(nz * nx * ny * nc):
            place = [device // (nx * ny * nc), device // (ny * nc) % nx, device // nc % ny, device % nc]
            place[axis] = (place[axis] + steps) % self.sizes[axis]
            pairs.append((device, ((place[0] * nx + place[1]) * ny + place[2]) * nc + place[3]))
        return lax.ppermute(value, ("page", "band"), pairs)

    def swap(self, value):
        return self.shift(value, 3, 1)

    def spread(self, value, axis):
        return [value] + [self.shift(value, axis, k) for k in range(1, self.sizes[axis])]

    def chip_of(self, kz, kx, ky):
        z, x, y = (self.z - kz) % self.nz, (self.x - kx) % self.nx, (self.y - ky) % self.ny
        return (z * self.nx + x) * self.ny + y

    def gather(self, first, second):
        count = len(first)
        local = jnp.stack(list(first) + list(second))
        rows, cols = local.shape[1:]
        along_z = self.spread(local, 0)
        sources, moves, table = [], [], []
        for axes, start, stop in (((1, 2), 0, count), ((2, 1), count, local.shape[0])):
            part = jnp.stack([piece[start:stop] for piece in along_z])
            part = jnp.stack(self.spread(part, axes[0]))
            for far, piece in enumerate(self.spread(part, axes[1])):
                number = 0
                for near in range(self.sizes[axes[0]]):
                    kx, ky = (near, far) if axes[0] == 1 else (far, near)
                    for kz in range(self.nz):
                        for unit in range(start, stop):
                            moves.append((unit, len(table), len(sources), number))
                            number += 1
                        table.append(self.chip_of(kz, kx, ky))
                sources.append(piece.reshape((-1, rows, cols)))
        outs = shuffle(
            jnp.stack(table), sources, [sds((self.chips, rows, cols), BF16)] * local.shape[0], moves, True
        )
        return [out.reshape(-1, cols) for out in outs]

    def reduce(self, first, second, turns=None):
        turns = turns or {}
        units = list(first) + list(second)
        cols = units[0].shape[-1]
        rows = units[0].shape[0] // self.chips
        count = len(first)
        shapes, moves, table = [], [], []
        for axes, start, stop in (((2, 1), 0, count), ((1, 2), count, len(units))):
            inner = self.sizes[axes[1]]
            for far in range(self.sizes[axes[0]]):
                number = 0
                for near in range(inner):
                    kx, ky = (near, far) if axes[0] == 2 else (far, near)
                    for kz in range(self.nz):
                        chip = self.chip_of(kz, kx, ky)
                        for unit in range(start, stop):
                            moves.append((len(shapes), number, unit, len(table)))
                            table.append((chip + turns[unit]) % self.chips if unit in turns else chip)
                            number += 1
                shapes.append(sds((number, rows, cols), BF16))
        terms = shuffle(
            jnp.stack(table), [unit.reshape(self.chips, rows, cols) for unit in units], shapes, moves, False
        )
        lows = []
        for axes, start, stop in (((2, 1), 0, count), ((1, 2), count, len(units))):
            outer, inner = self.sizes[axes[0]], self.sizes[axes[1]]
            mine, terms = terms[:outer], terms[outer:]
            total = mine[0].astype(F32)
            for k in range(1, outer):
                total = total + self.shift(mine[k], axes[0], -k).astype(F32)
            low = total.astype(BF16).reshape(inner, self.nz, stop - start, rows, cols)
            total = low[0].astype(F32)
            for k in range(1, inner):
                total = total + self.shift(low[k], axes[1], -k).astype(F32)
            lows.append(total.astype(BF16))
        low = jnp.concatenate(lows, axis=1)
        total = low[0].astype(F32)
        for k in range(1, self.nz):
            total = total + self.shift(low[k], 0, -k).astype(F32)
        return total


def pick(stacked, index, axis=0):
    return lax.dynamic_index_in_dim(stacked, index, axis, keepdims=False)


def by_core(core, mine, theirs, axis):
    return jnp.where(core == 0, jnp.stack([mine, theirs], axis), jnp.stack([theirs, mine], axis))


def body(
    hidden,
    boxes,
    page_size,
    band_count,
    layout_tables,
    attn_in,
    attn_bias,
    attn_out,
    out_bias,
    norm_gain,
    norm_bias,
    ffn_in,
    ffn_in_bias,
    ffn_out,
    ffn_out_bias,
    out_grad,
    *,
    pages,
    bands,
):
    at = Places(pages, bands)
    core = at.core
    core_id = core.astype(jnp.int32).reshape(1)
    devices = pages * bands
    ny, chips = at.ny, at.chips
    cap = hidden.shape[2]
    rows_dev = attn_in.shape[1]
    table_rows = layout_tables.shape[1]
    ff_dev = ffn_out.shape[1]

    def to_chip(stacked):
        own = [pick(stacked, at.y)]
        for k in range(1, ny):
            own.append(at.shift(pick(stacked, (at.y + k) % ny), 2, k))
        return own

    def from_chip(rows):
        parts = rows.reshape((ny, cap) + rows.shape[1:])
        back = [parts[0]]
        for k in range(1, ny):
            back.append(at.shift(parts[k].astype(BF16), 2, -k).astype(F32))
        back = jnp.stack(back)
        return jnp.stack([pick(back, (page - at.y) % ny) for page in range(ny)])[:, None]

    widths, heights = page_size[0][:, None], page_size[1][:, None]
    left = boxes[0, :, 0] * GRID // widths
    top = boxes[1, :, 0] * GRID // heights
    right = boxes[2, :, 0] * GRID // widths
    bottom = boxes[3, :, 0] * GRID // heights
    live = (lax.broadcasted_iota(jnp.int32, left.shape, 1) < band_count).astype(jnp.int32)
    facts = jnp.stack([left, top, right, bottom, bottom - top, right - left, live, live], axis=1)
    facts_own = jnp.concatenate(to_chip(facts), axis=-1)
    facts_all = jnp.concatenate([facts_own, at.swap(facts_own)], axis=-1)
    owner = facts_all // table_rows
    index = jnp.where(
        owner % CORES == core, owner // CORES * table_rows + facts_all % table_rows, -1
    )
    mask = jnp.where(facts_all[6:7] > 0, 0.0, DEAD).astype(F32)
    live_own = facts_own[6].astype(F32)[:, None]
    hidden_own = jnp.concatenate(to_chip(hidden[:, 0]), axis=0)
    grad_own = jnp.concatenate(to_chip(out_grad[:, 0]), axis=0)

    segment = jnp.concatenate(
        [
            attn_bias.reshape(-1),
            out_bias.reshape(-1),
            norm_gain.reshape(-1),
            norm_bias.reshape(-1),
            ffn_out_bias.reshape(-1),
            ffn_in_bias.reshape(-1),
        ]
    )
    split = SMALL_ROWS * rows_dev
    smalls = lax.all_to_all(
        jnp.broadcast_to(segment, (devices, segment.shape[0])), ("page", "band"), 0, 0, tiled=True
    ).astype(F32)
    small = smalls[:, :split].reshape(devices, SMALL_ROWS, rows_dev).swapaxes(0, 1).reshape(SMALL_ROWS, D)
    up_bias = pick(smalls[:, split:].reshape(chips, CORES, LAYERS, 2, ff_dev // 2), core, 1)
    up_bias = up_bias.transpose(1, 2, 0, 3).reshape(LAYERS, FF // CORES)

    tables = at.gather(layout_tables[:2], layout_tables[2:])
    columns = jnp.concatenate(
        [
            attn_in.reshape(LAYERS, rows_dev, 3, CORES, HALF),
            attn_out.reshape(LAYERS, rows_dev, 1, CORES, HALF),
        ],
        axis=2,
    ).transpose(3, 0, 2, 1, 4)
    ups = ffn_in.reshape(LAYERS, rows_dev, chips, CORES, 2, ff_dev // 2).transpose(3, 0, 4, 1, 2, 5)
    ups = ups.reshape(CORES, LAYERS, 2, rows_dev, D)

    def chip_rows(by_columns):
        both = by_core(core, pick(by_columns, core), at.swap(pick(by_columns, 1 - core)), 2)
        return both.reshape(both.shape[:2] + (CORES * rows_dev, both.shape[-1]))

    columns = chip_rows(columns)
    ups = chip_rows(ups)
    downs = ffn_out.reshape(LAYERS, 2, ff_dev // 2, D)
    weights = []
    for layer in range(LAYERS):
        wq, wk, wv, wo_mine = at.gather(columns[layer, :2], columns[layer, 2:])
        w1a, w2a, w1b, w2b = at.gather(
            (ups[layer, 0], downs[layer, 0]), (ups[layer, 1], downs[layer, 1])
        )
        wo = by_core(core, wo_mine, at.swap(wo_mine), 1).reshape(D, D)
        weights.append((wq, wk, wv, wo, w1a, w1b, w2a, w2b))

    half = ny * cap
    looked_up = embed(index.T, tables)
    x = hidden_own.astype(F32) + looked_up[:half] + at.swap(looked_up[half:].astype(BF16)).astype(F32)
    x_low = x.astype(BF16)
    saved = []
    for layer in range(LAYERS):
        wq, wk, wv, wo, w1a, w1b, w2a, w2b = weights[layer]
        x_other = at.swap(x_low)
        q, k, v, mix_own, mix_other = attn_fwd(core_id, x_low, x_other, wq, wk, wv, small, mask, layer)
        y1, y1_low, n1, r1 = out_norm(core_id, mix_own, at.swap(mix_other), wo, x, small, layer)
        y1_other = at.swap(y1_low)
        act, slope, part, part_other = ffn_fwd(y1_low, y1_other, w1a, w1b, up_bias, w2a, w2b, layer)
        saved.append(
            (x_low, x_other, q, k, v, mix_own, mix_other, n1, r1, y1_low, y1_other, act, slope)
        )
        x, x_low, n2, r2 = add_norm(y1, part, at.swap(part_other), small, layer)
        saved[layer] += (n2, r2)
    output = from_chip(x * live_own)

    sources = (grad_own, live_own)
    small_grads = [None] * LAYERS
    results = [None] * LAYERS
    for layer in reversed(range(LAYERS)):
        wq, wk, wv, wo, w1a, w1b, w2a, w2b = weights[layer]
        x_low, x_other, q, k, v, mix_own, mix_other, n1, r1, y1_low, y1_other, act, slope, n2, r2 = saved[layer]
        gh2, df, sums2 = norm_bwd(sources, n2, r2, small, 2 * layer + 1)
        df_other = at.swap(df)
        dw1a, dw1b, dw2a, dw2b, up_sums, part, part_other = ffn_bwd(
            df, df_other, w1a, w1b, w2a, w2b, act, slope, y1_low, y1_other
        )
        ffn_result = at.reduce((dw1a, dw2a), (dw1b, dw2b))
        gh1, da, sums1 = norm_bwd((gh2, part, at.swap(part_other)), n1, r1, small, 2 * layer)
        da_other = at.swap(da)
        dwq, dwk, dwv, dwo, attn_sums, part, part_other = attn_bwd(
            core_id, da, da_other, wo, q, k, v, mix_own, mix_other, x_low, x_other, wq, wk, wv, mask
        )
        sources = (gh1, part, at.swap(part_other))
        dwo = jnp.concatenate([pick(dwo, core), at.swap(pick(dwo, 1 - core))])
        attn_result = at.reduce((dwq, dwk), (dwv, dwo), {3: core * (chips // 2)})
        results[layer] = (attn_result, ffn_result)
        small_grads[layer] = (sums1, sums2, attn_sums, up_sums)
    grad_x = sources[0] + sources[1] + sources[2].astype(F32)
    input_grad = from_chip(grad_x)
    grad_low = grad_x.astype(BF16)
    table_parts = table_grads(index, grad_low, at.swap(grad_low), chips * table_rows)
    grad_tables = at.reduce(table_parts[:2], table_parts[2:])

    zeros = jnp.zeros((2, HALF), F32)
    vectors = []
    for layer in range(LAYERS):
        mine = small_grads[layer][2][:2]
        vectors.append(by_core(core, mine, zeros, 1).reshape(2, D))
    vectors.append(jnp.stack([small_grads[layer][0][2] for layer in range(LAYERS)]))
    for row in range(2):
        for layer in range(LAYERS):
            vectors.append(jnp.stack([small_grads[layer][norm][row] for norm in range(2)]))
    vectors.append(jnp.stack([small_grads[layer][1][2] for layer in range(LAYERS)]))
    vectors = jnp.concatenate(vectors).reshape(SMALL_ROWS, devices, rows_dev).swapaxes(0, 1)
    ups_grad = jnp.stack([small_grads[layer][3][0] for layer in range(LAYERS)])
    ups_grad = ups_grad.reshape(LAYERS, 2, chips, ff_dev // 2).transpose(2, 0, 1, 3)
    ups_grad = by_core(core, ups_grad, jnp.zeros_like(ups_grad), 1)
    segments = jnp.concatenate(
        [vectors.reshape(devices, split), ups_grad.reshape(devices, LAYERS * ff_dev)], axis=1
    )
    segment = jnp.sum(lax.all_to_all(segments, ("page", "band"), 0, 0, tiled=True), axis=0)
    rows = segment[:split].reshape(SMALL_ROWS, rows_dev)

    grads = [[], [], [], []]
    for layer in range(LAYERS):
        attn_result, ffn_result = results[layer]

        def my_rows(result):
            units, cols = result.shape[0], result.shape[-1]
            by_owner = result.reshape(units, CORES, rows_dev, cols)
            return by_core(core, pick(by_owner, core, 1), at.swap(pick(by_owner, 1 - core, 1)), 2)

        both = my_rows(attn_result).swapaxes(0, 1)
        grads[0].append(both[:, :3].reshape(rows_dev, 3 * D))
        grads[1].append(both[:, 3].reshape(rows_dev, D))
        both = my_rows(jnp.stack([ffn_result[0], ffn_result[2]]))
        both = both.reshape(2, rows_dev, CORES, chips, ff_dev // 2).transpose(1, 3, 2, 0, 4)
        grads[2].append(both.reshape(rows_dev, FF))
        grads[3].append(jnp.concatenate([ffn_result[1], ffn_result[3]]))
    grads = [jnp.stack(pair) for pair in grads]

    return (
        output,
        input_grad,
        grad_tables,
        grads[0],
        rows[ROW_ATTN:ROW_OUT].reshape(LAYERS, 2, rows_dev),
        grads[1],
        rows[ROW_OUT:ROW_GAIN],
        rows[ROW_GAIN:ROW_SHIFT].reshape(LAYERS, 2, rows_dev),
        rows[ROW_SHIFT:ROW_DOWN].reshape(LAYERS, 2, rows_dev),
        grads[2],
        segment[split:].reshape(LAYERS, ff_dev),
        grads[3],
        rows[ROW_DOWN:SMALL_ROWS],
    )


def solution(mesh):
    both = ("page", "band")
    tokens = P("page", "band", None, None)
    middle = P(None, both, None)
    last = P(None, both)
    third = P(None, None, both)
    return jax.shard_map(
        functools.partial(body, pages=mesh.shape["page"], bands=mesh.shape["band"]),
        mesh=mesh,
        in_specs=(
            tokens,
            P(None, "page", "band", None),
            P(None, "page"),
            P("page", "band"),
            middle,
            middle,
            third,
            middle,
            last,
            third,
            third,
            middle,
            last,
            middle,
            last,
            tokens,
        ),
        out_specs=(
            tokens,
            tokens,
            middle,
            middle,
            third,
            middle,
            last,
            third,
            third,
            middle,
            last,
            middle,
            last,
        ),
        check_vma=False,
    )
```

```python
import functools

import jax
import jax.numpy as jnp
from jax import lax
from jax.experimental import pallas as pl
from jax.experimental.pallas import tpu as pltpu
from jax.sharding import PartitionSpec as P

D = 768
HEADS = 12
HEAD_DIM = 64
HALF = D // 2
PAIRS = HEADS // 4
FF = 3072
POS = 1024
GRID = 1000
LAYERS = 2
CORES = 2
LANES = 128
EPS = 1e-12
DEAD = -1000000000.0
SCALE = HEAD_DIM ** (-0.5)
VMEM = 60 * 1024 * 1024
F32 = jnp.float32
BF16 = jnp.bfloat16

ROW_ATTN, ROW_OUT, ROW_GAIN, ROW_SHIFT, ROW_DOWN = 0, 4, 6, 10, 14
SMALL_ROWS = 16


def dot(a, b, dims=((1,), (0,))):
    return lax.dot_general(a, b, (dims, ((), ())), preferred_element_type=F32)


def halves(core):
    first = core[0] * HALF
    return pl.ds(pl.multiple_of(first, LANES), HALF), pl.ds(pl.multiple_of(HALF - first, LANES), HALF)


NT = ((1,), (1,))
TN = ((0,), (0,))


def sds(shape, dtype):
    return jax.ShapeDtypeStruct(shape, dtype)


def whole(shape):
    return pl.BlockSpec(shape, lambda *_: (0,) * len(shape))


def cost(flops, nbytes, trans=0):
    return pl.CostEstimate(flops=flops, bytes_accessed=nbytes, transcendentals=trans)


def params():
    return pltpu.CompilerParams(vmem_limit_bytes=VMEM)


def embed_kernel(idx, t0, t1, t2, t3, out):
    rows = t0.shape[0]
    place = lax.broadcasted_iota(jnp.int32, (idx.shape[0], rows), 1)

    def hot(*cols):
        total = None
        for col in cols:
            one = jnp.where(place == idx[:, col : col + 1], 1.0, 0.0)
            total = one if total is None else total + one
        return total.astype(BF16)

    out[...] = (
        dot(hot(0, 2), t0[...])
        + dot(hot(1, 3), t1[...])
        + dot(hot(4), t2[...])
        + dot(hot(5), t3[...])
    )


def embed(idx, tables):
    tokens = idx.shape[0]
    block = 128
    rows = tables[0].shape[0]
    return pl.pallas_call(
        embed_kernel,
        name="embed",
        out_shape=sds((tokens, D), F32),
        grid=(tokens // block,),
        in_specs=[pl.BlockSpec((block, 8), lambda i: (i, 0))] + [whole((rows, D))] * 4,
        out_specs=pl.BlockSpec((block, D), lambda i: (i, 0)),
        compiler_params=params(),
        cost_estimate=cost(8 * tokens * rows * D, 8 * rows * D + 4 * tokens * D),
    )(idx, *tables)


def table_kernel(idx, own, sib, o0, o1, o2, o3):
    half = own.shape[0]
    block = o0.shape[0]
    first = pl.program_id(0) * block
    place = lax.broadcasted_iota(jnp.int32, (block, 2 * half), 0) + first

    def hot(*rows):
        total = None
        for row in rows:
            one = jnp.where(place == idx[row : row + 1, :], 1.0, 0.0)
            total = one if total is None else total + one
        return total.astype(BF16)

    for out, rows in ((o0, (0, 2)), (o1, (1, 3)), (o2, (4,)), (o3, (5,))):
        mark = hot(*rows)
        out[...] = (dot(mark[:, :half], own[...]) + dot(mark[:, half:], sib[...])).astype(BF16)


def table_grads(idx, own, sib, rows):
    half = own.shape[0]
    block = 256
    return pl.pallas_call(
        table_kernel,
        name="table_grads",
        out_shape=[sds((rows, D), BF16)] * 4,
        grid=(rows // block,),
        in_specs=[whole((8, 2 * half)), whole((half, D)), whole((half, D))],
        out_specs=[pl.BlockSpec((block, D), lambda i: (i, 0))] * 4,
        compiler_params=params(),
        cost_estimate=cost(16 * half * rows * D, 8 * rows * D),
    )(idx, own, sib)


def attn_fwd_kernel(core, xo, xs, wq, wk, wv, small, mask, q, k, v, mo, ms, *, layer):
    half = xo.shape[0]
    for first, rows in ((0, xo), (half, xs)):
        x = rows[...]
        q[first : first + half, :] = (
            dot(x, wq[...]) + small[ROW_ATTN + 2 * layer : ROW_ATTN + 2 * layer + 1, :]
        ).astype(BF16)
        k[first : first + half, :] = dot(x, wk[...]).astype(BF16)
        v[first : first + half, :] = (
            dot(x, wv[...]) + small[ROW_ATTN + 2 * layer + 1 : ROW_ATTN + 2 * layer + 2, :]
        ).astype(BF16)
    keys, values = k[...], v[...]
    low_lanes = lax.broadcasted_iota(jnp.int32, (1, LANES), 1) < HEAD_DIM
    for first, out in ((0, mo), (half, ms)):
        queries = q[first : first + half, :].astype(F32) * SCALE
        parts = []
        for head in range(2):
            lanes = low_lanes if head == 0 else jnp.logical_not(low_lanes)
            one = jnp.where(lanes, queries, 0.0).astype(BF16)
            scores = dot(one, keys, NT) + mask[...]
            expo = jnp.exp(scores - jnp.max(scores, axis=-1, keepdims=True))
            total = jnp.sum(expo, axis=-1, keepdims=True)
            parts.append(dot(expo.astype(BF16), values) / total)
        out[...] = jnp.where(low_lanes, parts[0], parts[1]).astype(BF16)


def weight_block(part):
    return pl.BlockSpec((D, LANES), lambda p, core: (0, part * PAIRS + p))


def attn_fwd(core, xo, xs, wa, small, mask, layer):
    half = xo.shape[0]
    tokens = 2 * half
    col = lambda p, core: (0, p)
    rows = pl.BlockSpec((tokens, LANES), col)
    return pl.pallas_call(
        functools.partial(attn_fwd_kernel, layer=layer),
        name="attn_fwd",
        out_shape=[sds((tokens, HALF), BF16)] * 3 + [sds((half, HALF), BF16)] * 2,
        grid_spec=pltpu.PrefetchScalarGridSpec(
            num_scalar_prefetch=1,
            grid=(PAIRS,),
            in_specs=[
                whole((half, D)),
                whole((half, D)),
                weight_block(0),
                weight_block(1),
                weight_block(2),
                pl.BlockSpec((SMALL_ROWS, LANES), lambda p, core: (0, core[0] * PAIRS + p)),
                whole((1, tokens)),
            ],
            out_specs=[rows] * 3 + [pl.BlockSpec((half, LANES), col)] * 2,
        ),
        compiler_params=params(),
        cost_estimate=cost(
            2 * tokens * D * 3 * HALF + 4 * PAIRS * 2 * tokens * tokens * LANES,
            2 * (tokens * D + 3 * D * HALF + 4 * tokens * HALF),
            PAIRS * 2 * tokens * tokens,
        ),
    )(core, xo, xs, wa, wa, wa, small, mask)


def attn_bwd_kernel(
    core, dao, das, wom, wot, q, k, v, mo, ms, xo, xs, wq, wk, wv, mask,
    dwq, dwk, dwv, dwo, sums, dxo, dxs, acc, all_s, turned,
):
    half = xo.shape[0]
    step = pl.program_id(0)
    mine_cols, their_cols = halves(core)
    dq_s, dk_s, dv_s = [all_s.at[:, part * LANES : (part + 1) * LANES] for part in range(3)]

    @pl.when(step == 0)
    def _():
        turned[:, :half] = xo[...].T
        turned[:, half:] = xs[...].T

    keys, values = k[...], v[...]
    low_lanes = lax.broadcasted_iota(jnp.int32, (1, LANES), 1) < HEAD_DIM
    grad_keys = [None, None]
    grad_values = [None, None]
    for part, da in ((0, dao), (1, das)):
        first = part * half
        span = slice(first, first + half)
        grad_mix = dot(da[:, mine_cols], wom[...], NT) + dot(da[:, their_cols], wot[...], NT)
        queries = q[span, :].astype(F32) * SCALE
        grad_queries = []
        for head in range(2):
            lanes = low_lanes if head == 0 else jnp.logical_not(low_lanes)
            one = jnp.where(lanes, queries, 0.0).astype(BF16)
            scores = dot(one, keys, NT) + mask[...]
            expo = jnp.exp(scores - jnp.max(scores, axis=-1, keepdims=True))
            probs = expo * (1.0 / jnp.sum(expo, axis=-1, keepdims=True))
            grad_one = jnp.where(lanes, grad_mix, 0.0).astype(BF16)
            grad_probs = dot(grad_one, values, NT)
            weighted = probs * grad_probs
            delta = jnp.sum(weighted, axis=-1, keepdims=True)
            grad_scores = (weighted - probs * delta).astype(BF16)
            grad_queries.append(dot(grad_scores, keys))
            key_part = dot(grad_scores, one, TN)
            value_part = dot(probs.astype(BF16), grad_one, TN)
            if part == 0:
                grad_keys[head], grad_values[head] = key_part, value_part
            else:
                grad_keys[head] = grad_keys[head] + key_part
                grad_values[head] = grad_values[head] + value_part
        dq_s[span, :] = (jnp.where(low_lanes, grad_queries[0], grad_queries[1]) * SCALE).astype(BF16)
    dk_s[...] = (grad_keys[0] + grad_keys[1]).astype(BF16)
    dv_s[...] = (grad_values[0] + grad_values[1]).astype(BF16)
    sums[...] = jnp.zeros_like(sums)
    sums[0:1, :] = jnp.sum(dq_s[...].astype(F32), axis=0, keepdims=True)
    sums[1:2, :] = jnp.sum(dv_s[...].astype(F32), axis=0, keepdims=True)
    for part, out in enumerate((dwq, dwk, dwv)):
        out[...] = dot(turned[...], all_s[:, part * LANES : (part + 1) * LANES]).astype(BF16)
    out_rows = dot(mo[...], dao[...], TN) + dot(ms[...], das[...], TN)
    dwo[0] = out_rows[:, :HALF].astype(BF16)
    dwo[1] = out_rows[:, HALF:].astype(BF16)
    total = dot(dq_s[...], wq[...], NT) + dot(dk_s[...], wk[...], NT) + dot(dv_s[...], wv[...], NT)

    @pl.when(step == 0)
    def _():
        acc[...] = total

    @pl.when(step > 0)
    def _():
        acc[...] += total

    @pl.when(step == PAIRS - 1)
    def _():
        dxo[...] = acc[:half, :]
        dxs[...] = acc[half:, :].astype(BF16)


def attn_bwd(core, dao, das, wom, wot, q, k, v, mo, ms, xo, xs, wa, mask):
    half = xo.shape[0]
    tokens = 2 * half
    col = lambda p, core: (0, p)
    weight = pl.BlockSpec((D, LANES), col)
    rows = pl.BlockSpec((tokens, LANES), col)
    part = pl.BlockSpec((half, LANES), col)
    out_rows = pl.BlockSpec((LANES, HALF), lambda p, core: (core[0] * PAIRS + p, 0))
    return pl.pallas_call(
        attn_bwd_kernel,
        name="attn_bwd",
        out_shape=[sds((D, HALF), BF16)] * 3
        + [
            sds((CORES, HALF, HALF), BF16),
            sds((8, HALF), F32),
            sds((half, D), F32),
            sds((half, D), BF16),
        ],
        grid_spec=pltpu.PrefetchScalarGridSpec(
            num_scalar_prefetch=1,
            grid=(PAIRS,),
            in_specs=[
                whole((half, D)),
                whole((half, D)),
                out_rows,
                out_rows,
                rows,
                rows,
                rows,
                part,
                part,
                whole((half, D)),
                whole((half, D)),
                weight_block(0),
                weight_block(1),
                weight_block(2),
                whole((1, tokens)),
            ],
            out_specs=[weight] * 3
            + [
                pl.BlockSpec((CORES, LANES, HALF), lambda p, core: (0, p, 0)),
                pl.BlockSpec((8, LANES), col),
                whole((half, D)),
                whole((half, D)),
            ],
            scratch_shapes=[
                pltpu.VMEM((tokens, D), F32),
                pltpu.VMEM((tokens, 3 * LANES), BF16),
                pltpu.VMEM((D, tokens), BF16),
            ],
        ),
        compiler_params=params(),
        cost_estimate=cost(
            8 * tokens * D * 3 * HALF // 2 + 10 * PAIRS * 2 * tokens * tokens * LANES,
            2 * (4 * tokens * D + 8 * D * HALF + 4 * tokens * HALF),
            PAIRS * 2 * tokens * tokens,
        ),
    )(core, dao, das, wom, wot, q, k, v, mo, ms, xo, xs, wa, wa, wa, mask)


def norm_rows(h, gain, shift, y, yb, n, rstd):
    mean = jnp.mean(h, axis=-1, keepdims=True)
    centred = h - mean
    scale = lax.rsqrt(jnp.mean(centred * centred, axis=-1, keepdims=True) + EPS)
    normal = centred * scale
    out = normal * gain + shift
    y[...] = out
    yb[...] = out.astype(BF16)
    n[...] = normal
    rstd[...] = scale


def norm_outs(half):
    return [sds((half, D), F32), sds((half, D), BF16), sds((half, D), F32), sds((half, 1), F32)]


def out_norm_kernel(core, mine, theirs, wom, wot, base, small, y, yb, n, rstd, *, layer):
    mine_rows, their_rows = halves(core)
    near = dot(mine[...], wom[mine_rows, :]) + dot(theirs[...], wom[their_rows, :])
    far = dot(mine[...], wot[mine_rows, :]) + dot(theirs[...], wot[their_rows, :])
    first = core[0] == 0
    mixed = jnp.concatenate([jnp.where(first, near, far), jnp.where(first, far, near)], axis=1)
    h = base[...] + mixed + small[ROW_OUT + layer : ROW_OUT + layer + 1, :]
    row = 2 * layer
    norm_rows(
        h, small[ROW_GAIN + row : ROW_GAIN + row + 1, :], small[ROW_SHIFT + row : ROW_SHIFT + row + 1, :],
        y, yb, n, rstd,
    )


def out_norm(core, mine, theirs, wom, wot, base, small, layer):
    half = base.shape[0]
    return pl.pallas_call(
        functools.partial(out_norm_kernel, layer=layer),
        name="out_norm",
        out_shape=norm_outs(half),
        in_specs=[pl.BlockSpec(memory_space=pltpu.SMEM)] + [pl.BlockSpec(memory_space=pltpu.VMEM)] * 6,
        out_specs=[pl.BlockSpec(memory_space=pltpu.VMEM)] * 4,
        compiler_params=params(),
        cost_estimate=cost(2 * half * D * D, 2 * D * D + 16 * half * D),
    )(core, mine, theirs, wom, wot, base, small)


def add_norm_kernel(base, part, recv, small, y, yb, n, rstd, *, layer):
    h = base[...] + part[...] + recv[...].astype(F32) + small[ROW_DOWN + layer : ROW_DOWN + layer + 1, :]
    row = 2 * layer + 1
    norm_rows(
        h, small[ROW_GAIN + row : ROW_GAIN + row + 1, :], small[ROW_SHIFT + row : ROW_SHIFT + row + 1, :],
        y, yb, n, rstd,
    )


def add_norm(base, part, recv, small, layer):
    half = base.shape[0]
    return pl.pallas_call(
        functools.partial(add_norm_kernel, layer=layer),
        name="add_norm",
        out_shape=norm_outs(half),
        in_specs=[pl.BlockSpec(memory_space=pltpu.VMEM)] * 4,
        out_specs=[pl.BlockSpec(memory_space=pltpu.VMEM)] * 4,
        compiler_params=params(),
        cost_estimate=cost(20 * half * D, 20 * half * D),
    )(base, part, recv, small)


def norm_bwd_kernel(*refs, row, summed):
    if summed:
        base, part, recv, n, rstd, small, gh, ghb, sums = refs
        gz = base[...] + part[...] + recv[...].astype(F32)
    else:
        base, live, n, rstd, small, gh, ghb, sums = refs
        gz = base[...].astype(F32) * live[...]
    normal = n[...]
    e = gz * small[ROW_GAIN + row : ROW_GAIN + row + 1, :]
    mean = jnp.mean(e, axis=-1, keepdims=True)
    slope = jnp.mean(e * normal, axis=-1, keepdims=True)
    grad = (e - mean - normal * slope) * rstd[...]
    low = grad.astype(BF16)
    gh[...] = grad
    ghb[...] = low
    sums[...] = jnp.zeros_like(sums)
    sums[0:1, :] = jnp.sum(gz * normal, axis=0, keepdims=True)
    sums[1:2, :] = jnp.sum(gz, axis=0, keepdims=True)
    sums[2:3, :] = jnp.sum(low.astype(F32), axis=0, keepdims=True)


def norm_bwd(sources, n, rstd, small, row):
    half = n.shape[0]
    operands = tuple(sources) + (n, rstd, small)
    return pl.pallas_call(
        functools.partial(norm_bwd_kernel, row=row, summed=len(sources) == 3),
        name="norm_bwd",
        out_shape=[sds((half, D), F32), sds((half, D), BF16), sds((8, D), F32)],
        in_specs=[pl.BlockSpec(memory_space=pltpu.VMEM)] * len(operands),
        out_specs=[pl.BlockSpec(memory_space=pltpu.VMEM)] * 3,
        compiler_params=params(),
        cost_estimate=cost(20 * half * D, 20 * half * D),
    )(*operands)


FF_BLOCK = 256
FF_STEPS = FF // CORES // FF_BLOCK


def ffn_fwd_kernel(yo, ys, w1, bias, w2, act, slope, po, ps, acc, *, layer):
    half = yo.shape[0]
    j = pl.program_id(0)
    for first, rows in ((0, yo), (half, ys)):
        span = slice(first, first + half)
        up = dot(rows[...], w1[...]) + bias[layer : layer + 1, :]
        cdf = 0.5 * (1.0 + lax.erf(up * (2.0**-0.5)))
        low = (up * cdf).astype(BF16)
        act[span, :] = low
        slope[span, :] = (cdf + up * (jnp.exp(-0.5 * up * up) * 0.3989422804014327)).astype(BF16)
        total = dot(low, w2[...])

        @pl.when(j == 0)
        def _():
            acc[span, :] = total

        @pl.when(j > 0)
        def _():
            acc[span, :] += total

    @pl.when(j == FF_STEPS - 1)
    def _():
        po[...] = acc[:half, :]
        ps[...] = acc[half:, :].astype(BF16)


DOWN_STEPS = D // FF_BLOCK


def ffn_specs(tokens, col):
    return (
        pl.BlockSpec((D, FF_BLOCK), lambda j: (0, col // FF_BLOCK + j)),
        pl.BlockSpec((FF_BLOCK, D), lambda j: (j % DOWN_STEPS, col // D + 2 + j // DOWN_STEPS)),
        pl.BlockSpec((tokens, FF_BLOCK), lambda j: (0, j)),
    )


def ffn_fwd(yo, ys, wf, col, bias, layer):
    half = yo.shape[0]
    tokens = 2 * half
    width = FF // CORES
    cols, down, rows = ffn_specs(tokens, col)
    return pl.pallas_call(
        functools.partial(ffn_fwd_kernel, layer=layer),
        name="ffn_fwd",
        out_shape=[sds((tokens, width), BF16)] * 2 + [sds((half, D), F32), sds((half, D), BF16)],
        grid=(FF_STEPS,),
        in_specs=[
            whole((half, D)),
            whole((half, D)),
            cols,
            pl.BlockSpec((LAYERS, FF_BLOCK), lambda j: (0, j)),
            down,
        ],
        out_specs=[rows] * 2 + [whole((half, D))] * 2,
        scratch_shapes=[pltpu.VMEM((tokens, D), F32)],
        compiler_params=params(),
        cost_estimate=cost(4 * tokens * D * width, 4 * D * width + 4 * tokens * width, tokens * width),
    )(yo, ys, wf, bias, wf)


def ffn_bwd_kernel(dfo, dfs, w1, w2, act, slope, yo, ys, dw1, dw2, sums, po, ps, acc, du, turned):
    half = yo.shape[0]
    j = pl.program_id(0)

    @pl.when(j == 0)
    def _():
        turned[:, :half] = yo[...].T
        turned[:, half:] = ys[...].T

    for first, rows in ((0, dfo), (half, dfs)):
        span = slice(first, first + half)
        low = (slope[span, :].astype(F32) * dot(rows[...], w2[...], NT)).astype(BF16)
        du[span, :] = low
        total = dot(low, w1[...], NT)

        @pl.when(j == 0)
        def _():
            acc[span, :] = total

        @pl.when(j > 0)
        def _():
            acc[span, :] += total

    sums[...] = jnp.zeros_like(sums)
    sums[0:1, :] = jnp.sum(du[...].astype(F32), axis=0, keepdims=True)
    dw1[...] = dot(turned[...], du[...]).astype(BF16)
    dw2[...] = (dot(act[:half, :], dfo[...], TN) + dot(act[half:, :], dfs[...], TN)).astype(BF16)

    @pl.when(j == FF_STEPS - 1)
    def _():
        po[...] = acc[:half, :]
        ps[...] = acc[half:, :].astype(BF16)


def ffn_bwd(dfo, dfs, wf, col, act, slope, yo, ys):
    half = yo.shape[0]
    tokens = 2 * half
    width = FF // CORES
    cols, down, rows = ffn_specs(tokens, col)
    return pl.pallas_call(
        ffn_bwd_kernel,
        name="ffn_bwd",
        out_shape=[
            sds((2, D, D), BF16),
            sds((2, D, D), BF16),
            sds((8, width), F32),
            sds((half, D), F32),
            sds((half, D), BF16),
        ],
        grid=(FF_STEPS,),
        in_specs=[whole((half, D))] * 2 + [cols, down, rows, rows] + [whole((half, D))] * 2,
        out_specs=[
            pl.BlockSpec((None, D, FF_BLOCK), lambda j: (j // DOWN_STEPS, 0, j % DOWN_STEPS)),
            pl.BlockSpec((None, FF_BLOCK, D), lambda j: (j // DOWN_STEPS, j % DOWN_STEPS, 0)),
            pl.BlockSpec((8, FF_BLOCK), lambda j: (0, j)),
        ]
        + [whole((half, D))] * 2,
        scratch_shapes=[
            pltpu.VMEM((tokens, D), F32),
            pltpu.VMEM((tokens, FF_BLOCK), BF16),
            pltpu.VMEM((D, tokens), BF16),
        ],
        compiler_params=params(),
        cost_estimate=cost(8 * tokens * D * width, 8 * D * width + 4 * tokens * width),
    )(dfo, dfs, wf, wf, act, slope, yo, ys)


def shuffle_kernel(table, *refs, moves, count):
    for out, to, to_col, source, at, at_col, width in moves:
        to = table[to[0]] if isinstance(to, list) else to
        at = table[at[0]] if isinstance(at, list) else at
        refs[count + out][to, :, to_col : to_col + width] = refs[source][at, :, at_col : at_col + width]


def shuffle(table, sources, shapes, moves):
    nbytes = sum(4 * source.size for source in sources)
    return pl.pallas_call(
        functools.partial(shuffle_kernel, moves=moves, count=len(sources)),
        name="shuffle",
        out_shape=shapes,
        in_specs=[pl.BlockSpec(memory_space=pltpu.SMEM)]
        + [pl.BlockSpec(memory_space=pltpu.VMEM)] * len(sources),
        out_specs=[pl.BlockSpec(memory_space=pltpu.VMEM)] * len(shapes),
        compiler_params=params(),
        cost_estimate=cost(0, nbytes),
    )(table, *sources)


def pack_kernel(core, qkv, out, up, mine, send):
    chips = FF // (2 * CORES * FF_CHUNK)
    ups = up[0].astype(F32)
    parts = []
    for parity in range(CORES):
        starts = [
            ((chip * CORES + parity) * 2 + part) * FF_CHUNK for part in range(2) for chip in range(chips)
        ]
        parts.append(jnp.concatenate([ups[:, start : start + FF_CHUNK] for start in starts], axis=1))
    even = core[0] == 0
    for ref, cols, ff in (
        (mine, halves(core)[0], jnp.where(even, parts[0], parts[1])),
        (send, halves(core)[1], jnp.where(even, parts[1], parts[0])),
    ):
        for part in range(3):
            whole_part = qkv.at[0, :, part * D : (part + 1) * D]
            ref[:, part * HALF : (part + 1) * HALF] = whole_part[:, cols]
        ref[:, 3 * HALF : 4 * HALF] = out.at[0][:, cols]
        ref[:, 4 * HALF :] = ff.astype(BF16)


FF_CHUNK = 48
PACKED = 4 * HALF + FF // CORES


def layer_block(shape, layer):
    return pl.BlockSpec((1,) + shape, lambda *_: (layer, 0, 0))


def pack(core, attn_in, attn_out, ffn_in, layer):
    rows = attn_in.shape[1]
    return pl.pallas_call(
        pack_kernel,
        name="pack",
        out_shape=[sds((rows, PACKED), BF16)] * 2,
        grid=(1,),
        in_specs=[
            pl.BlockSpec(memory_space=pltpu.SMEM),
            layer_block((rows, 3 * D), layer),
            layer_block((rows, D), layer),
            layer_block((rows, FF), layer),
        ],
        out_specs=[whole((rows, PACKED))] * 2,
        compiler_params=params(),
        cost_estimate=cost(0, 8 * rows * PACKED),
    )(core, attn_in, attn_out, ffn_in)


def join_kernel(core, mine, recv, down, *outs):
    rows = mine.shape[0]
    even = core[0] == 0
    near, far = mine[...].astype(F32), recv[...].astype(F32)
    both = jnp.concatenate([jnp.where(even, near, far), jnp.where(even, far, near)], axis=0).astype(BF16)
    downs = [down[0, part * CORES * rows : (part + 1) * CORES * rows, :] for part in range(2)]
    attn, ffn = outs
    for unit in range(2):
        attn[unit] = both[:, unit * D : (unit + 1) * D]
        ffn[2 * unit] = both[:, (2 + unit) * D : (3 + unit) * D]
        ffn[2 * unit + 1] = downs[unit]


def join(core, mine, recv, ffn_out, layer, shapes):
    rows = mine.shape[0]
    down = ffn_out.shape[1]
    return pl.pallas_call(
        join_kernel,
        name="join",
        out_shape=[sds(shape, BF16) for shape in shapes],
        grid=(1,),
        in_specs=[
            pl.BlockSpec(memory_space=pltpu.SMEM),
            whole((rows, PACKED)),
            whole((rows, PACKED)),
            layer_block((down, D), layer),
        ],
        out_specs=[whole(shape) for shape in shapes],
        compiler_params=params(),
        cost_estimate=cost(0, 8 * rows * PACKED),
    )(core, mine, recv, ffn_out)


def split_kernel(core, *refs):
    mine, send = refs[-2:]
    rows = mine.shape[0]
    even = core[0] == 0
    for part, block in enumerate(refs[:-2]):
        top, bottom = block[:rows, :], block[rows:, :]
        mine[:, part * D : (part + 1) * D] = jnp.where(even, top, bottom)
        send[:, part * D : (part + 1) * D] = jnp.where(even, bottom, top)


def split(core, units):
    rows = units[0].shape[0] // CORES
    return pl.pallas_call(
        split_kernel,
        name="split",
        out_shape=[sds((rows, PACKED), F32)] * 2,
        in_specs=[pl.BlockSpec(memory_space=pltpu.SMEM)] + [pl.BlockSpec(memory_space=pltpu.VMEM)] * len(units),
        out_specs=[pl.BlockSpec(memory_space=pltpu.VMEM)] * 2,
        compiler_params=params(),
        cost_estimate=cost(0, 16 * rows * PACKED),
    )(core, *units)


def merge_kernel(core, *refs):
    qkv, out, up, down = refs[4 * LAYERS :]
    chips = FF // (2 * CORES * FF_CHUNK)
    even = core[0] == 0
    for layer in range(LAYERS):
        mine, recv, first_down, second_down = refs[4 * layer : 4 * layer + 4]
        near, far = mine[...], recv[...]
        first, second = jnp.where(even, near, far), jnp.where(even, far, near)
        for part in range(3):
            span = slice(part * HALF, (part + 1) * HALF)
            qkv[layer, :, part * D : part * D + HALF] = first[:, span]
            qkv[layer, :, part * D + HALF : (part + 1) * D] = second[:, span]
        out[layer, :, :HALF] = first[:, 3 * HALF : 4 * HALF]
        out[layer, :, HALF:] = second[:, 3 * HALF : 4 * HALF]
        chunks = []
        for chip in range(chips):
            for source in (first, second):
                for part in range(2):
                    start = 4 * HALF + part * D + chip * FF_CHUNK
                    chunks.append(source[:, start : start + FF_CHUNK])
        up[layer] = jnp.concatenate(chunks, axis=1)
        rows = first_down.shape[0]
        down[layer, :rows, :] = first_down[...]
        down[layer, rows:, :] = second_down[...]


def merge(core, parts):
    rows = parts[0].shape[0]
    down = 2 * parts[2].shape[0]
    return pl.pallas_call(
        merge_kernel,
        name="merge",
        out_shape=[
            sds((LAYERS, rows, 3 * D), F32),
            sds((LAYERS, rows, D), F32),
            sds((LAYERS, rows, FF), F32),
            sds((LAYERS, down, D), F32),
        ],
        in_specs=[pl.BlockSpec(memory_space=pltpu.SMEM)] + [pl.BlockSpec(memory_space=pltpu.VMEM)] * len(parts),
        out_specs=[pl.BlockSpec(memory_space=pltpu.VMEM)] * 4,
        compiler_params=params(),
        cost_estimate=cost(0, 32 * rows * PACKED),
    )(core, *parts)


class Places:
    def __init__(self, pages, bands):
        self.ny = bands // CORES
        self.nx = self.ny if pages % self.ny == 0 else 1
        self.nz = pages // self.nx
        self.chips = pages * self.ny
        page, band = lax.axis_index("page"), lax.axis_index("band")
        self.z, self.x = page // self.nx, page % self.nx
        self.y, self.core = band // CORES, band % CORES
        self.sizes = (self.nz, self.nx, self.ny, CORES)

    def move(self, value, axis, step, flip=False):
        pairs = []
        nz, nx, ny, nc = self.sizes
        for device in range(nz * nx * ny * nc):
            place = [device // (nx * ny * nc), device // (ny * nc) % nx, device // nc % ny, device % nc]
            place[axis] = place[axis] ^ step if flip else (place[axis] + step) % self.sizes[axis]
            pairs.append((device, ((place[0] * nx + place[1]) * ny + place[2]) * nc + place[3]))
        return lax.ppermute(value, ("page", "band"), pairs)

    def exchange(self, wants):
        keys = []
        for axis, step, _ in wants:
            key = (axis, step if axis == 0 else step % self.sizes[axis])
            keys.append(key)
        got = [None] * len(wants)
        for key in dict.fromkeys(keys):
            numbers = [i for i, other in enumerate(keys) if other == key]
            flat = [wants[i][2].reshape(-1, wants[i][2].shape[-1]) for i in numbers]
            moved = self.move(jnp.concatenate(flat) if len(flat) > 1 else flat[0], *key, flip=key[0] == 0)
            first = 0
            for i, part in zip(numbers, flat):
                got[i] = moved[first : first + part.shape[0]].reshape(wants[i][2].shape)
                first += part.shape[0]
        return got

    def swap(self, value):
        return self.move(value, 3, 1)

    def chip_of(self, kz, kx, ky):
        z, x, y = self.z ^ kz, (self.x - kx) % self.nx, (self.y - ky) % self.ny
        return (z * self.nx + x) * self.ny + y

    def flips(self):
        return [1 << bit for bit in reversed(range(self.nz.bit_length() - 1))]


def tie(values, *others):
    return lax.optimization_barrier((values, others))[0]


class Gather:
    def __init__(self, at, local, shapes, place):
        self.at, self.local = at, local
        self.half = local.shape[0] // 2
        self.shapes, self.place = shapes, place
        self.stages = [functools.partial(self.flip, step) for step in at.flips()]
        self.stages += [self.first, self.second]
        self.held = local[None]
        self.spots = [0]

    def flip(self, step, got):
        if got:
            self.held = jnp.concatenate([self.held] + list(got))
        self.spots = self.spots + [spot ^ step for spot in self.spots]
        return [(0, step, self.held)]

    def near(self, axis, part):
        return [(axis, k, part) for k in range(1, self.at.sizes[axis])]

    def first(self, got):
        held = jnp.concatenate([self.held] + list(got))
        self.sent = [held[:, : self.half], held[:, self.half :]]
        return self.near(1, self.sent[0]) + self.near(2, self.sent[1])

    def second(self, got):
        cut = self.at.nx - 1
        self.sent = [jnp.stack([part] + got) for part, got in zip(self.sent, (got[:cut], got[cut:]))]
        return self.near(2, self.sent[0]) + self.near(1, self.sent[1])

    def finish(self, got):
        at = self.at
        rows, cols = self.local.shape[1:]
        sources, moves, table = [], [], []
        cut = at.ny - 1
        for axes, part, other, start in (
            ((1, 2), self.sent[0], got[:cut], 0),
            ((2, 1), self.sent[1], got[cut:], self.half),
        ):
            for far, piece in enumerate([part] + list(other)):
                number = 0
                for near in range(at.sizes[axes[0]]):
                    kx, ky = (near, far) if axes[0] == 1 else (far, near)
                    for kz in self.spots:
                        chip = at.chip_of(kz, kx, ky)
                        for unit in range(start, start + self.half):
                            for out, step, offset, to_col, at_col, width in self.place[unit]:
                                moves.append(
                                    (out, [len(table)], to_col, len(sources), number, at_col, width)
                                )
                                table.append(chip * step + offset)
                            number += 1
                sources.append(piece.reshape((-1, rows, cols)))
        outs = shuffle(jnp.stack(table), sources, [sds(shape, BF16) for shape in self.shapes], moves)
        return [out.reshape(-1, out.shape[-1]) for out in outs]


class Reduce:
    def __init__(self, at, first, second):
        self.at, self.halves = at, (first, second)
        self.stages = [self.first, self.second]
        self.stages += [functools.partial(self.flip, number) for number in range(len(at.flips()))]

    def picked(self, groups, axis, index):
        at = self.at
        rows = []
        for group in groups:
            parts = []
            for part in group:
                blocks = part.reshape(at.nz, at.nx, at.ny, part.shape[0] // at.chips, part.shape[1])
                parts.append(pick(blocks, index, axis))
            rows.append(jnp.concatenate(parts, axis=-1) if len(parts) > 1 else parts[0])
        return jnp.concatenate(rows, axis=2) if len(rows) > 1 else rows[0]

    def first(self, got):
        at = self.at
        wants = [(2, -k, self.picked(self.halves[0], 2, (at.y - k) % at.ny)) for k in range(1, at.ny)]
        return wants + [
            (1, -k, self.picked(self.halves[1], 1, (at.x - k) % at.nx)) for k in range(1, at.nx)
        ]

    def second(self, got):
        at = self.at
        cut = at.ny - 1
        self.lows = []
        for mine, other in (
            (self.picked(self.halves[0], 2, at.y), got[:cut]),
            (self.picked(self.halves[1], 1, at.x), got[cut:]),
        ):
            self.lows.append(self.total(mine, other).astype(BF16))
        wants = [(1, -k, pick(self.lows[0], (at.x - k) % at.nx, 1)) for k in range(1, at.nx)]
        return wants + [(2, -k, pick(self.lows[1], (at.y - k) % at.ny, 1)) for k in range(1, at.ny)]

    def total(self, mine, other):
        mine = mine.astype(F32)
        for term in other:
            mine = mine + term.astype(F32)
        return mine

    def flip(self, number, got):
        at = self.at
        bit = 1 << number
        if number == 0:
            cut = at.nx - 1
            first = self.total(pick(self.lows[0], at.x, 1), got[:cut])
            second = self.total(pick(self.lows[1], at.y, 1), got[cut:])
            self.cut = first.shape[1]
            low = jnp.concatenate([first, second], axis=1).astype(BF16)
        else:
            low = self.total(self.low, got).astype(BF16)
        low = low.reshape((low.shape[0] // 2, 2) + low.shape[1:])
        side = at.z // bit % 2
        self.low = pick(low, side, 1)
        return [(0, bit, pick(low, 1 - side, 1))]

    def finish(self, got):
        total = self.total(self.low, got)[0]
        return total[: self.cut], total[self.cut :]


class Line:
    def __init__(self, at):
        self.at, self.chunks, self.age, self.got = at, [], [], []

    def add(self, chunk):
        self.chunks.append(chunk)
        self.age.append(0)
        self.got.append([])

    def step(self, *others, extra=None):
        wants, spans = [], []
        for number, chunk in enumerate(self.chunks):
            if self.age[number] < len(chunk.stages):
                new = chunk.stages[self.age[number]](self.got[number])
                spans.append((number, len(wants), len(wants) + len(new)))
                wants += new
                self.age[number] += 1
        values, others = lax.optimization_barrier(([want[2] for want in wants], others))
        wants = [want[:2] + (value,) for want, value in zip(wants, values)]
        self.spans, self.moved = spans, self.at.exchange(wants)
        return others

    def close(self, *others):
        self.moved, others = lax.optimization_barrier((self.moved, others))
        for number, start, stop in self.spans:
            self.got[number] = self.moved[start:stop]
        return others

    def busy(self):
        return not all(self.done(chunk) for chunk in self.chunks)

    def done(self, chunk):
        number = self.chunks.index(chunk)
        return self.age[number] == len(chunk.stages)

    def fresh(self, chunk):
        return self.done(chunk) and any(span[0] == self.chunks.index(chunk) for span in self.spans)

    def result(self, chunk):
        return chunk.finish(self.got[self.chunks.index(chunk)])


def blocks_kernel(scalars, *refs, count, jobs):
    def rows(place, height):
        start, slopes = place
        for number, slope in slopes:
            start = start + scalars[number] * slope
        return pl.ds(pl.multiple_of(start, 16) if slopes else start, height)

    for out, to, height, terms in jobs:
        total = None
        for parts, place in terms:
            values = [refs[ref][rows(place, height), :] for ref in parts]
            value = values[0] if len(values) == 1 else jnp.concatenate(values, axis=1)
            if len(terms) > 1:
                value = value.astype(F32)
            total = value if total is None else total + value
        ref = refs[count + out]
        ref[to : to + height, :] = total.astype(ref.dtype)


class Stream:
    def __init__(self, parts, first_y, rows, base=0):
        self.parts, self.first_y, self.rows, self.base = parts, first_y, rows, base
        self.age = 0
        self.keep = self.recv = self.total = None


class Pipe:
    def __init__(self, at):
        self.at, self.groups = at, []
        self.bits = at.nz.bit_length() - 1
        self.last = 2 + self.bits
        scalars = [at.x, at.y] + [at.z // (1 << bit) % 2 for bit in range(self.bits)]
        self.scalars = jnp.stack(scalars).astype(jnp.int32)

    def add(self, streams):
        self.groups.append(streams)

    def pieces(self, stream, rows):
        nz = self.at.nz
        first = 1 if stream.first_y else 0
        strides = (2, 1)

        def chip(z, coords):
            start, slopes = stream.base + 4 * z * rows, []
            for axis, (fixed, slope) in enumerate(coords):
                start += fixed * strides[axis] * rows
                if slope:
                    slopes.append((axis, slope * strides[axis] * rows))
            return start, slopes

        def spot(fixed, number, slope, scale, base=0):
            return (base + fixed * scale, [(number, slope * scale)])

        other, same = (1, -1), (0, 1)
        sent, kept = [], []
        if stream.age == 0:
            for z in range(nz):
                for far in range(2):
                    coords = [None, None]
                    coords[first], coords[1 - first] = other, (far, 0)
                    sent.append([(stream.parts, chip(z, coords))])
        elif stream.age == 1:
            ref, base = stream.recv
            for out, side in ((sent, other), (kept, same)):
                for z in range(nz):
                    coords = [None, None]
                    coords[first], coords[1 - first] = same, side
                    place = spot(2 * z + side[0], 1 - first, side[1], rows, base)
                    out.append([(stream.parts, chip(z, coords)), ([ref], place)])
        elif stream.age < self.last:
            bit = stream.age - 2
            ref, base = stream.recv
            for out, side in ((sent, other), (kept, same)):
                for high in range(nz >> (bit + 1)):
                    fixed = 2 * high + side[0]
                    keep = spot(fixed, 2 + bit, side[1], rows)
                    out.append([([stream.keep], keep), ([ref], spot(fixed, 2 + bit, side[1], rows, base))])
        else:
            ref, base = stream.recv
            kept.append([([stream.keep], (0, [])), ([ref], (base, []))])
        return sent, kept

    def step(self, *others, extra=None):
        arrays, shapes, jobs = [], [], []
        heights, keeps, self.sent = {}, [], []

        def number(array):
            for i, known in enumerate(arrays):
                if known is array:
                    return i
            arrays.append(array)
            return len(arrays) - 1

        todo = []
        for streams in self.groups:
            for stream in streams:
                if stream.age > self.last:
                    continue
                rows = stream.rows
                sent, kept = self.pieces(stream, rows)
                axis = (2, 1) if stream.first_y else (1, 2)
                key = axis[stream.age] if stream.age < 2 else -stream.age
                start = heights.get(key, 0)
                if sent:
                    heights[key] = start + len(sent) * rows
                    self.sent.append((stream, key, start))
                todo.append((stream, key, start, sent, kept, rows))
        if extra is not None:
            span = (heights.get(2, 0), extra.shape[0])
            heights[2] = sum(span)
        order = list(heights)
        shapes = [sds((heights[key], D), BF16) for key in order]
        if extra is not None:
            jobs.append((order.index(2), span[0], span[1], [([number(extra)], (0, []))]))
        for stream, key, start, sent, kept, rows in todo:
            for block, terms in enumerate(sent):
                terms = [([number(part) for part in parts], place) for parts, place in terms]
                jobs.append((order.index(key), start + block * rows, rows, terms))
            if kept:
                last = stream.age == self.last
                keeps.append((stream, len(shapes)))
                for block, terms in enumerate(kept):
                    terms = [([number(part) for part in parts], place) for parts, place in terms]
                    jobs.append((len(shapes), block * rows, rows, terms))
                shapes.append(sds((len(kept) * rows, D), F32 if last else BF16))
        outs = pl.pallas_call(
            functools.partial(blocks_kernel, count=len(arrays), jobs=jobs),
            name="blocks",
            out_shape=shapes,
            in_specs=[pl.BlockSpec(memory_space=pltpu.SMEM)]
            + [pl.BlockSpec(memory_space=pltpu.VMEM)] * len(arrays),
            out_specs=[pl.BlockSpec(memory_space=pltpu.VMEM)] * len(shapes),
            compiler_params=params(),
            cost_estimate=cost(0, sum(3 * array.size for array in arrays)),
        )(self.scalars, *arrays)
        for stream, out in keeps:
            stream.keep = outs[out]
            if stream.age == self.last:
                stream.total = outs[out]
        for stream, *_ in todo:
            stream.age += 1
        payloads, others = lax.optimization_barrier((outs[: len(order)], others))
        self.moved = {}
        self.span = None if extra is None else span
        for key, payload in zip(order, payloads):
            if key > 0:
                self.moved[key] = self.at.move(payload, key, 1)
            else:
                self.moved[key] = self.at.move(payload, 0, 1 << (-key - 2), flip=True)
        return others

    def close(self, *others):
        self.moved, others = lax.optimization_barrier((self.moved, others))
        for stream, key, start in self.sent:
            stream.recv = (self.moved[key], start)
        if self.span is not None:
            self.extra = [self.moved[2][self.span[0] : sum(self.span)]]
        return others

    def busy(self):
        return any(stream.age <= self.last for streams in self.groups for stream in streams)


def pick(stacked, index, axis=0):
    return lax.dynamic_index_in_dim(stacked, index, axis, keepdims=False)


def by_core(core, mine, theirs, axis):
    return jnp.where(core == 0, jnp.stack([mine, theirs], axis), jnp.stack([theirs, mine], axis))


def body(
    hidden,
    boxes,
    page_size,
    band_count,
    layout_tables,
    attn_in,
    attn_bias,
    attn_out,
    out_bias,
    norm_gain,
    norm_bias,
    ffn_in,
    ffn_in_bias,
    ffn_out,
    ffn_out_bias,
    out_grad,
    *,
    pages,
    bands,
):
    at = Places(pages, bands)
    core = at.core
    core_id = core.astype(jnp.int32).reshape(1)
    devices = pages * bands
    ny, chips = at.ny, at.chips
    cap = hidden.shape[2]
    rows_dev = attn_in.shape[1]
    table_rows = layout_tables.shape[1]
    ff_dev = ffn_out.shape[1]
    chip_rows = CORES * rows_dev
    tiled = rows_dev % 8 == 0 and ff_dev == 2 * FF_CHUNK and at.nx == ny == 2

    def local_weights(layer):
        if tiled:
            mine, send = pack(core_id, attn_in, attn_out, ffn_in, layer)
            shapes = ((2, chip_rows, D), (4, chip_rows, D))
            return join(core_id, mine, at.swap(send), ffn_out, layer, shapes)
        columns = jnp.concatenate(
            [attn_in[layer].reshape(rows_dev, 3, CORES, HALF), attn_out[layer].reshape(rows_dev, 1, CORES, HALF)],
            axis=1,
        ).transpose(2, 0, 1, 3)
        ups = ffn_in[layer].reshape(rows_dev, chips, CORES, 2, ff_dev // 2).transpose(2, 0, 3, 1, 4)
        packed = jnp.concatenate(
            [columns.reshape(CORES, rows_dev, 4 * HALF), ups.reshape(CORES, rows_dev, FF // CORES)], axis=2
        )
        both = by_core(core, pick(packed, core), at.swap(pick(packed, 1 - core)), 0)
        both = both.reshape(chip_rows, PACKED)
        down = ffn_out[layer].reshape(2, chip_rows, D)
        both = both.reshape(chip_rows, 4, D).swapaxes(0, 1)
        return both[:2], jnp.stack([both[2], down[0], both[3], down[1]])

    attn_place = ([(0, 1, 0, 0, 0, D)], [(0, 1, 0, D, 0, D), (1, 1, 0, 0, HALF, HALF)])
    attn_shapes = ((chips, chip_rows, 2 * D), (chips, chip_rows, HALF))
    ffn_place = [[(0, 1, 0, col * D, 0, D)] for col in (0, 2, 1, 3)]
    ffn_shapes = ((chips, chip_rows, 4 * D),)
    table_place = [[(table, 1, 0, 0, 0, D)] for table in range(4)]
    table_shapes = ((chips, table_rows, D),) * 4

    def to_chip(stacked):
        own = [pick(stacked, at.y)]
        for k in range(1, ny):
            own.append(at.move(pick(stacked, (at.y + k) % ny), 2, k))
        return own

    def send_back(rows):
        parts = rows.reshape((ny, cap) + rows.shape[1:])
        return [at.move(parts[k].astype(BF16), 2, -k) for k in range(1, ny)]

    def from_chip(rows, back):
        back = [rows[:cap]] + [part.astype(F32) for part in back]
        back = jnp.stack(back)
        return jnp.stack([pick(back, (page - at.y) % ny) for page in range(ny)])[:, None]

    def token_facts(hidden, boxes, page_size, band_count):
        widths, heights = page_size[0][:, None], page_size[1][:, None]
        left = boxes[0, :, 0] * GRID // widths
        top = boxes[1, :, 0] * GRID // heights
        right = boxes[2, :, 0] * GRID // widths
        bottom = boxes[3, :, 0] * GRID // heights
        live = (lax.broadcasted_iota(jnp.int32, left.shape, 1) < band_count).astype(jnp.int32)
        facts = jnp.stack([left, top, right, bottom, bottom - top, right - left, live, live], axis=1)
        facts_own = jnp.concatenate(to_chip(facts), axis=-1)
        facts_all = jnp.concatenate([facts_own, at.swap(facts_own)], axis=-1)
        owner = facts_all // table_rows
        index = jnp.where(
            owner % CORES == core, owner // CORES * table_rows + facts_all % table_rows, -1
        )
        mask = jnp.where(facts_all[6:7] > 0, 0.0, DEAD).astype(F32)
        live_own = facts_own[6].astype(F32)[:, None]
        hidden_own = jnp.concatenate(to_chip(hidden[:, 0]), axis=0)
        return index, mask, live_own, hidden_own

    cut = SMALL_ROWS * rows_dev

    def small_params(attn_bias, out_bias, norm_gain, norm_bias, ffn_out_bias, ffn_in_bias):
        segment = jnp.concatenate(
            [
                attn_bias.reshape(-1),
                out_bias.reshape(-1),
                norm_gain.reshape(-1),
                norm_bias.reshape(-1),
                ffn_out_bias.reshape(-1),
                ffn_in_bias.reshape(-1),
            ]
        )
        smalls = lax.all_to_all(
            jnp.broadcast_to(segment, (devices, segment.shape[0])), ("page", "band"), 0, 0, tiled=True
        ).astype(F32)
        small = smalls[:, :cut].reshape(devices, SMALL_ROWS, rows_dev).swapaxes(0, 1).reshape(SMALL_ROWS, D)
        up_bias = pick(smalls[:, cut:].reshape(chips, CORES, LAYERS, 2, ff_dev // 2), core, 1)
        up_bias = up_bias.transpose(1, 2, 0, 3).reshape(LAYERS, FF // CORES)
        return small, up_bias

    saved = [[], []]
    weights = [[], []]

    def look_up(state):
        tables = line.result(chunks[0])
        looked_up = embed(index.T, tables)
        mine = hidden_own.astype(F32) + looked_up[:half]
        x = mine + at.swap(looked_up[half:].astype(BF16)).astype(F32)
        return x, x.astype(BF16)

    def attend(layer, state):
        x, x_low = state
        wa, wom = line.result(chunks[1 + 2 * layer])
        wot, x_other = at.swap(wom), at.swap(x_low)
        weights[layer] += [wa, wom, wot]
        q, k, v, mix_own, mix_other = attn_fwd(core_id, x_low, x_other, wa, small, mask, layer)
        y1, y1_low, n1, r1 = out_norm(core_id, mix_own, at.swap(mix_other), wom, wot, x, small, layer)
        saved[layer] += [x_low, x_other, q, k, v, mix_own, mix_other, n1, r1]
        return y1, y1_low

    def feed(layer, state):
        y1, y1_low = state
        (wf,) = line.result(chunks[2 + 2 * layer])
        y1_other = at.swap(y1_low)
        weights[layer] += [wf, 0]
        act, slope, part, part_other = ffn_fwd(y1_low, y1_other, wf, 0, up_bias, layer)
        x, x_low, n2, r2 = add_norm(y1, part, at.swap(part_other), small, layer)
        saved[layer] += [y1_low, y1_other, act, slope, n2, r2]
        return x, x_low

    half = ny * cap
    line = Line(at)
    chunks = [Gather(at, layout_tables, table_shapes, table_place)]
    parts = [look_up]
    line.add(chunks[0])
    line.step()
    locals0 = local_weights(0)
    token_args = (hidden, boxes, page_size, band_count)
    small_args = (attn_bias, out_bias, norm_gain, norm_bias, ffn_out_bias, ffn_in_bias)
    locals0, token_args = line.close(locals0, token_args)
    state = ()
    running = None
    waiting = []
    for layer in range(LAYERS):
        waiting += [(layer, 0), (layer, 1)]
        parts += [functools.partial(attend, layer), functools.partial(feed, layer)]
    local = locals0
    while waiting or running is not None or not line.done(chunks[-1]):
        if waiting:
            layer, number = waiting.pop(0)
            if layer > 0 and number == 0:
                local = local_weights(layer)
            chunks.append(
                Gather(at, local[number], (attn_shapes, ffn_shapes)[number], (attn_place, ffn_place)[number])
            )
            line.add(chunks[-1])
        if all(line.done(chunk) for chunk in chunks):
            state = running(state)
            break
        state = line.step(*state)
        if running is not None:
            state = running(state)
        if len(chunks) == 2:
            tokens, small_args, late = line.close(
                token_facts(*token_args), small_args, (attn_in, attn_out, ffn_in)
            )
            index, mask, live_own, hidden_own = tokens
            attn_in, attn_out, ffn_in = late
        elif len(chunks) == 3:
            small, up_bias = line.close(*small_params(*small_args))
        else:
            state = line.close(*state)
        ready = [number for number, chunk in enumerate(chunks) if line.fresh(chunk)]
        running = parts[ready[0]] if ready else None
    x = state[0]

    small_grads = [None] * LAYERS

    def backward_ffn(layer, sources):
        wf, col = weights[layer][3:]
        y1_low, y1_other, act, slope, n2, r2 = saved[layer][9:]
        gh2, df, sums2 = norm_bwd(sources, n2, r2, small, 2 * layer + 1)
        dw1, dw2, up_sums, part, part_other = ffn_bwd(df, at.swap(df), wf, col, act, slope, y1_low, y1_other)
        small_grads[layer] = [sums2, up_sums]
        return (gh2, part, at.swap(part_other)), dw1, dw2

    def backward_attn(layer, sources):
        wa, wom, wot = weights[layer][:3]
        x_low, x_other, q, k, v, mix_own, mix_other, n1, r1 = saved[layer][:9]
        gh1, da, sums1 = norm_bwd(sources, n1, r1, small, 2 * layer)
        dwq, dwk, dwv, dwo, attn_sums, part, part_other = attn_bwd(
            core_id, da, at.swap(da), wom, wot, q, k, v, mix_own, mix_other, x_low, x_other, wa, mask
        )
        small_grads[layer] = [sums1] + small_grads[layer] + [attn_sums]
        return (gh1, part, at.swap(part_other)), (dwq, dwk, dwv), (pick(dwo, core), at.swap(pick(dwo, 1 - core)))

    def attn_groups(dqkv, dwo):
        dwq, dwk, dwv = dqkv
        return [dwq, dwk], [dwv, by_core(core, *dwo, 0).reshape(D, HALF)]

    grad_own = jnp.concatenate(to_chip(tie(out_grad[:, 0], saved[0][0])), axis=0)
    line = Pipe(at) if tiled else Line(at)

    def ffn_chunk(dw1, dw2):
        if tiled:
            flat = [dw.reshape(2 * D, D) for dw in (dw1, dw2)]
            streams = [Stream([unit], part == 0, chip_rows, part * D) for part in range(2) for unit in flat]
            line.add(streams)
            return streams
        chunk = Reduce(at, [[dw1[0]], [dw2[0]]], [[dw1[1]], [dw2[1]]])
        line.add(chunk)
        return chunk

    def attn_chunk(dqkv, dwo):
        first, second = attn_groups(dqkv, dwo)
        if tiled:
            streams = [Stream(first, True, chip_rows), Stream(second, False, chip_rows)]
            line.add(streams)
            return streams
        chunk = Reduce(at, [first], [second])
        line.add(chunk)
        return chunk

    def table_chunk(tables):
        if tiled:
            streams = [Stream([table], number < 2, table_rows) for number, table in enumerate(tables)]
            line.add(streams)
            return streams
        chunk = Reduce(at, [[table] for table in tables[:2]], [[table] for table in tables[2:]])
        line.add(chunk)
        return chunk

    sources, dw1, dw2 = backward_ffn(1, (grad_own, live_own))
    ffn1 = ffn_chunk(dw1, dw2)
    output = x * live_own
    sources = line.step(*sources, extra=output[cap:] if tiled else None)
    sources, dqkv, dwo = backward_attn(1, sources)
    sources = line.close(*sources)
    output = from_chip(output, line.extra if tiled else send_back(output))
    att1 = attn_chunk(dqkv, dwo)
    sources = line.step(*sources)
    sources, dw1, dw2 = backward_ffn(0, sources)
    sources = line.close(*sources)
    ffn0 = ffn_chunk(dw1, dw2)
    sources = line.step(*sources)
    sources, dqkv, dwo = backward_attn(0, sources)
    sources = line.close(*sources)
    att0 = attn_chunk(dqkv, dwo)
    sources = line.step(*sources)
    grad_x = sources[0] + sources[1] + sources[2].astype(F32)
    grad_low = grad_x.astype(BF16)
    table_parts = table_grads(index, grad_low, at.swap(grad_low), chips * table_rows)
    table_parts = line.close(*table_parts)
    tab = table_chunk(table_parts)
    line.step(extra=grad_x[cap:] if tiled else None)
    line.close()
    input_grad = from_chip(grad_x, line.extra if tiled else send_back(grad_x))
    zeros = jnp.zeros((2, HALF), F32)
    vectors = []
    for layer in range(LAYERS):
        mine = small_grads[layer][3][:2]
        vectors.append(by_core(core, mine, zeros, 1).reshape(2, D))
    vectors.append(jnp.stack([small_grads[layer][0][2] for layer in range(LAYERS)]))
    for row in range(2):
        for layer in range(LAYERS):
            vectors.append(jnp.stack([small_grads[layer][norm][row] for norm in range(2)]))
    vectors.append(jnp.stack([small_grads[layer][1][2] for layer in range(LAYERS)]))
    vectors = lax.optimization_barrier(jnp.concatenate(vectors)).reshape(SMALL_ROWS, devices, rows_dev).swapaxes(0, 1)
    ups_grad = jnp.stack([small_grads[layer][2][0] for layer in range(LAYERS)])
    ups_grad = ups_grad.reshape(LAYERS, 2, chips, ff_dev // 2).transpose(2, 0, 1, 3)
    ups_grad = by_core(core, ups_grad, jnp.zeros_like(ups_grad), 1)
    segments = jnp.concatenate(
        [vectors.reshape(devices, cut), ups_grad.reshape(devices, LAYERS * ff_dev)], axis=1
    )
    segments = lax.all_to_all(segments, ("page", "band"), 0, 0, tiled=True)

    while line.busy():
        line.step()
        line.close()
    segments = tie(segments, tab[0].total if tiled else line.moved)
    segment = jnp.sum(segments, axis=0)
    rows = segment[:cut].reshape(SMALL_ROWS, rows_dev)
    if tiled:
        grad_tables = jnp.stack([stream.total for stream in tab])
        results = [
            [stream.total for stream in attn[:2] + ffn] for attn, ffn in ((att0, ffn0), (att1, ffn1))
        ]
    else:
        sums = [line.result(chunk) for chunk in (att0, ffn0, att1, ffn1)]
        grad_tables = jnp.stack(line.result(tab)).reshape(4, table_rows, D)
        results = []
        for attn_sum, ffn_sum in ((sums[0], sums[1]), (sums[2], sums[3])):
            attn = jnp.stack(attn_sum)
            ffn = jnp.stack(ffn_sum).reshape(4, chip_rows, D)
            results.append((attn, ffn, ffn))

    if tiled:
        parts = []
        for layer in range(LAYERS):
            qk, vo, up_a, down_a, up_b, down_b = results[layer]
            mine, send = split(core_id, (qk, vo, up_a, up_b))
            parts += [mine, at.swap(send), down_a, down_b]
        grads = merge(core_id, parts)
    else:
        grads = [[], [], [], []]
        for layer in range(LAYERS):
            attn_sum, up_sum, down_sum = results[layer]
            both = jnp.stack([attn_sum[0], attn_sum[1], up_sum[0], up_sum[2]])
            by_owner = both.reshape(4, CORES, rows_dev, D)
            mine, theirs = pick(by_owner, core, 1), at.swap(pick(by_owner, 1 - core, 1))
            both = by_core(core, mine, theirs, 0).transpose(2, 0, 1, 3)
            attn = both[:, :, :2].reshape(rows_dev, CORES, 4, HALF).swapaxes(1, 2)
            grads[0].append(attn[:, :3].reshape(rows_dev, 3 * D))
            grads[1].append(attn[:, 3].reshape(rows_dev, D))
            ups = both[:, :, 2:].reshape(rows_dev, CORES, 2, chips, ff_dev // 2).transpose(0, 3, 1, 2, 4)
            grads[2].append(ups.reshape(rows_dev, FF))
            grads[3].append(jnp.concatenate([down_sum[1], down_sum[3]]))
        grads = [jnp.stack(pair) for pair in grads]

    return (
        output,
        input_grad,
        grad_tables,
        grads[0],
        rows[ROW_ATTN:ROW_OUT].reshape(LAYERS, 2, rows_dev),
        grads[1],
        rows[ROW_OUT:ROW_GAIN],
        rows[ROW_GAIN:ROW_SHIFT].reshape(LAYERS, 2, rows_dev),
        rows[ROW_SHIFT:ROW_DOWN].reshape(LAYERS, 2, rows_dev),
        grads[2],
        segment[cut:].reshape(LAYERS, ff_dev),
        grads[3],
        rows[ROW_DOWN:SMALL_ROWS],
    )


def solution(mesh):
    both = ("page", "band")
    tokens = P("page", "band", None, None)
    middle = P(None, both, None)
    last = P(None, both)
    third = P(None, None, both)
    return jax.shard_map(
        functools.partial(body, pages=mesh.shape["page"], bands=mesh.shape["band"]),
        mesh=mesh,
        in_specs=(
            tokens,
            P(None, "page", "band", None),
            P(None, "page"),
            P("page", "band"),
            middle,
            middle,
            third,
            middle,
            last,
            third,
            third,
            middle,
            last,
            middle,
            last,
            tokens,
        ),
        out_specs=(
            tokens,
            tokens,
            middle,
            middle,
            third,
            middle,
            last,
            third,
            third,
            middle,
            last,
            middle,
            last,
        ),
        check_vma=False,
    )
```

```python
import functools

import jax
import jax.numpy as jnp
from jax import lax
from jax.experimental import pallas as pl
from jax.experimental.pallas import tpu as pltpu
from jax.sharding import PartitionSpec as P

D = 768
HEADS = 12
HEAD_DIM = 64
HALF = D // 2
PAIRS = HEADS // 4
FF = 3072
POS = 1024
GRID = 1000
LAYERS = 2
CORES = 2
LANES = 128
EPS = 1e-12
DEAD = -1000000000.0
SCALE = HEAD_DIM ** (-0.5)
VMEM = 60 * 1024 * 1024
F32 = jnp.float32
BF16 = jnp.bfloat16

ROW_ATTN, ROW_OUT, ROW_GAIN, ROW_SHIFT, ROW_DOWN = 0, 4, 6, 10, 14
SMALL_ROWS = 16


def dot(a, b, dims=((1,), (0,))):
    return lax.dot_general(a, b, (dims, ((), ())), preferred_element_type=F32)


def halves(core):
    first = core[0] * HALF
    return pl.ds(pl.multiple_of(first, LANES), HALF), pl.ds(pl.multiple_of(HALF - first, LANES), HALF)


NT = ((1,), (1,))
TN = ((0,), (0,))


def sds(shape, dtype):
    return jax.ShapeDtypeStruct(shape, dtype)


def whole(shape):
    return pl.BlockSpec(shape, lambda *_: (0,) * len(shape))


def cost(flops, nbytes, trans=0):
    return pl.CostEstimate(flops=flops, bytes_accessed=nbytes, transcendentals=trans)


def params():
    return pltpu.CompilerParams(vmem_limit_bytes=VMEM)


def embed_kernel(idx, t0, t1, t2, t3, out):
    rows = t0.shape[0]
    place = lax.broadcasted_iota(jnp.int32, (idx.shape[0], rows), 1)

    def hot(*cols):
        total = None
        for col in cols:
            one = jnp.where(place == idx[:, col : col + 1], 1.0, 0.0)
            total = one if total is None else total + one
        return total.astype(BF16)

    out[...] = (
        dot(hot(0, 2), t0[...])
        + dot(hot(1, 3), t1[...])
        + dot(hot(4), t2[...])
        + dot(hot(5), t3[...])
    )


def embed(idx, tables):
    tokens = idx.shape[0]
    block = 128
    rows = tables[0].shape[0]
    return pl.pallas_call(
        embed_kernel,
        name="embed",
        out_shape=sds((tokens, D), F32),
        grid=(tokens // block,),
        in_specs=[pl.BlockSpec((block, 8), lambda i: (i, 0))] + [whole((rows, D))] * 4,
        out_specs=pl.BlockSpec((block, D), lambda i: (i, 0)),
        compiler_params=params(),
        cost_estimate=cost(8 * tokens * rows * D, 8 * rows * D + 4 * tokens * D),
    )(idx, *tables)


def table_kernel(idx, own, sib, o0, o1, o2, o3):
    half = own.shape[0]
    block = o0.shape[0]
    first = pl.program_id(0) * block
    place = lax.broadcasted_iota(jnp.int32, (block, 2 * half), 0) + first

    def hot(*rows):
        total = None
        for row in rows:
            one = jnp.where(place == idx[row : row + 1, :], 1.0, 0.0)
            total = one if total is None else total + one
        return total.astype(BF16)

    for out, rows in ((o0, (0, 2)), (o1, (1, 3)), (o2, (4,)), (o3, (5,))):
        mark = hot(*rows)
        out[...] = (dot(mark[:, :half], own[...]) + dot(mark[:, half:], sib[...])).astype(BF16)


def table_grads(idx, own, sib, rows):
    half = own.shape[0]
    block = 256
    return pl.pallas_call(
        table_kernel,
        name="table_grads",
        out_shape=[sds((rows, D), BF16)] * 4,
        grid=(rows // block,),
        in_specs=[whole((8, 2 * half)), whole((half, D)), whole((half, D))],
        out_specs=[pl.BlockSpec((block, D), lambda i: (i, 0))] * 4,
        compiler_params=params(),
        cost_estimate=cost(16 * half * rows * D, 8 * rows * D),
    )(idx, own, sib)


def attn_fwd_kernel(core, xo, xs, wq, wk, wv, small, mask, q, k, v, mo, ms, *, layer):
    half = xo.shape[0]
    joined = jnp.concatenate([wq[...], wk[...], wv[...]], axis=1)
    row = ROW_ATTN + 2 * layer
    for first, rows in ((0, xo), (half, xs)):
        span = slice(first, first + half)
        qkv = dot(rows[...], joined)
        q[span, :] = (qkv[:, :LANES] + small[row : row + 1, :]).astype(BF16)
        k[span, :] = qkv[:, LANES : 2 * LANES].astype(BF16)
        v[span, :] = (qkv[:, 2 * LANES :] + small[row + 1 : row + 2, :]).astype(BF16)
    keys, values = k[...], v[...]
    low_lanes = lax.broadcasted_iota(jnp.int32, (1, LANES), 1) < HEAD_DIM
    for first, out in ((0, mo), (half, ms)):
        queries = q[first : first + half, :].astype(F32) * SCALE
        parts = []
        for head in range(2):
            lanes = low_lanes if head == 0 else jnp.logical_not(low_lanes)
            one = jnp.where(lanes, queries, 0.0).astype(BF16)
            scores = dot(one, keys, NT) + mask[...]
            expo = jnp.exp(scores - jnp.max(scores, axis=-1, keepdims=True))
            total = jnp.sum(expo, axis=-1, keepdims=True)
            parts.append(dot(expo.astype(BF16), values) / total)
        out[...] = jnp.where(low_lanes, parts[0], parts[1]).astype(BF16)


def weight_block(part):
    return pl.BlockSpec((D, LANES), lambda p, core: (0, part * PAIRS + p))


def attn_fwd(core, xo, xs, wa, small, mask, layer):
    half = xo.shape[0]
    tokens = 2 * half
    col = lambda p, core: (0, p)
    rows = pl.BlockSpec((tokens, LANES), col)
    return pl.pallas_call(
        functools.partial(attn_fwd_kernel, layer=layer),
        name="attn_fwd",
        out_shape=[sds((tokens, HALF), BF16)] * 3 + [sds((half, HALF), BF16)] * 2,
        grid_spec=pltpu.PrefetchScalarGridSpec(
            num_scalar_prefetch=1,
            grid=(PAIRS,),
            in_specs=[
                whole((half, D)),
                whole((half, D)),
                weight_block(0),
                weight_block(1),
                weight_block(2),
                pl.BlockSpec((SMALL_ROWS, LANES), lambda p, core: (0, core[0] * PAIRS + p)),
                whole((1, tokens)),
            ],
            out_specs=[rows] * 3 + [pl.BlockSpec((half, LANES), col)] * 2,
        ),
        compiler_params=params(),
        cost_estimate=cost(
            2 * tokens * D * 3 * HALF + 4 * PAIRS * 2 * tokens * tokens * LANES,
            2 * (tokens * D + 3 * D * HALF + 4 * tokens * HALF),
            PAIRS * 2 * tokens * tokens,
        ),
    )(core, xo, xs, wa, wa, wa, small, mask)


def attn_bwd_kernel(
    core, dao, das, wom, wot, q, k, v, mo, ms, xo, xs, wq, wk, wv, mask,
    dwq, dwk, dwv, dwo, sums, dxo, dxs, acc, all_s, turned,
):
    half = xo.shape[0]
    step = pl.program_id(0)
    mine_cols, their_cols = halves(core)
    dq_s, dk_s, dv_s = [all_s.at[:, part * LANES : (part + 1) * LANES] for part in range(3)]

    @pl.when(step == 0)
    def _():
        turned[:, :half] = xo[...].T
        turned[:, half:] = xs[...].T

    keys, values = k[...], v[...]
    low_lanes = lax.broadcasted_iota(jnp.int32, (1, LANES), 1) < HEAD_DIM
    grad_keys = [None, None]
    grad_values = [None, None]
    for part, da in ((0, dao), (1, das)):
        first = part * half
        span = slice(first, first + half)
        grad_mix = dot(da[:, mine_cols], wom[...], NT) + dot(da[:, their_cols], wot[...], NT)
        queries = q[span, :].astype(F32) * SCALE
        grad_queries = []
        for head in range(2):
            lanes = low_lanes if head == 0 else jnp.logical_not(low_lanes)
            one = jnp.where(lanes, queries, 0.0).astype(BF16)
            scores = dot(one, keys, NT) + mask[...]
            expo = jnp.exp(scores - jnp.max(scores, axis=-1, keepdims=True))
            probs = expo * (1.0 / jnp.sum(expo, axis=-1, keepdims=True))
            grad_one = jnp.where(lanes, grad_mix, 0.0).astype(BF16)
            grad_probs = dot(grad_one, values, NT)
            weighted = probs * grad_probs
            delta = jnp.sum(weighted, axis=-1, keepdims=True)
            grad_scores = (weighted - probs * delta).astype(BF16)
            grad_queries.append(dot(grad_scores, keys))
            key_part = dot(grad_scores, one, TN)
            value_part = dot(probs.astype(BF16), grad_one, TN)
            if part == 0:
                grad_keys[head], grad_values[head] = key_part, value_part
            else:
                grad_keys[head] = grad_keys[head] + key_part
                grad_values[head] = grad_values[head] + value_part
        dq_s[span, :] = (jnp.where(low_lanes, grad_queries[0], grad_queries[1]) * SCALE).astype(BF16)
    dk_s[...] = (grad_keys[0] + grad_keys[1]).astype(BF16)
    dv_s[...] = (grad_values[0] + grad_values[1]).astype(BF16)
    sums[...] = jnp.zeros_like(sums)
    sums[0:1, :] = jnp.sum(dq_s[...].astype(F32), axis=0, keepdims=True)
    sums[1:2, :] = jnp.sum(dv_s[...].astype(F32), axis=0, keepdims=True)
    weight_grads = dot(turned[...], all_s[...]).astype(BF16)
    for part, out in enumerate((dwq, dwk, dwv)):
        out[...] = weight_grads[:, part * LANES : (part + 1) * LANES]
    out_rows = dot(mo[...], dao[...], TN) + dot(ms[...], das[...], TN)
    dwo[0] = out_rows[:, :HALF].astype(BF16)
    dwo[1] = out_rows[:, HALF:].astype(BF16)
    total = dot(all_s[...], jnp.concatenate([wq[...], wk[...], wv[...]], axis=1), NT)

    @pl.when(step == 0)
    def _():
        acc[...] = total

    @pl.when(step > 0)
    def _():
        acc[...] += total

    @pl.when(step == PAIRS - 1)
    def _():
        dxo[...] = acc[:half, :]
        dxs[...] = acc[half:, :].astype(BF16)


def attn_bwd(core, dao, das, wom, wot, q, k, v, mo, ms, xo, xs, wa, mask):
    half = xo.shape[0]
    tokens = 2 * half
    col = lambda p, core: (0, p)
    weight = pl.BlockSpec((D, LANES), col)
    rows = pl.BlockSpec((tokens, LANES), col)
    part = pl.BlockSpec((half, LANES), col)
    out_rows = pl.BlockSpec((LANES, HALF), lambda p, core: (core[0] * PAIRS + p, 0))
    return pl.pallas_call(
        attn_bwd_kernel,
        name="attn_bwd",
        out_shape=[sds((D, HALF), BF16)] * 3
        + [
            sds((CORES, HALF, HALF), BF16),
            sds((8, HALF), F32),
            sds((half, D), F32),
            sds((half, D), BF16),
        ],
        grid_spec=pltpu.PrefetchScalarGridSpec(
            num_scalar_prefetch=1,
            grid=(PAIRS,),
            in_specs=[
                whole((half, D)),
                whole((half, D)),
                out_rows,
                out_rows,
                rows,
                rows,
                rows,
                part,
                part,
                whole((half, D)),
                whole((half, D)),
                weight_block(0),
                weight_block(1),
                weight_block(2),
                whole((1, tokens)),
            ],
            out_specs=[weight] * 3
            + [
                pl.BlockSpec((CORES, LANES, HALF), lambda p, core: (0, p, 0)),
                pl.BlockSpec((8, LANES), col),
                whole((half, D)),
                whole((half, D)),
            ],
            scratch_shapes=[
                pltpu.VMEM((tokens, D), F32),
                pltpu.VMEM((tokens, 3 * LANES), BF16),
                pltpu.VMEM((D, tokens), BF16),
            ],
        ),
        compiler_params=params(),
        cost_estimate=cost(
            8 * tokens * D * 3 * HALF // 2 + 10 * PAIRS * 2 * tokens * tokens * LANES,
            2 * (4 * tokens * D + 8 * D * HALF + 4 * tokens * HALF),
            PAIRS * 2 * tokens * tokens,
        ),
    )(core, dao, das, wom, wot, q, k, v, mo, ms, xo, xs, wa, wa, wa, mask)


def norm_rows(h, gain, shift, y, yb, n, rstd):
    mean = jnp.mean(h, axis=-1, keepdims=True)
    centred = h - mean
    scale = lax.rsqrt(jnp.mean(centred * centred, axis=-1, keepdims=True) + EPS)
    normal = centred * scale
    out = normal * gain + shift
    y[...] = out
    yb[...] = out.astype(BF16)
    n[...] = normal
    rstd[...] = scale


def norm_outs(half):
    return [sds((half, D), F32), sds((half, D), BF16), sds((half, D), F32), sds((half, 1), F32)]


def out_norm_kernel(core, mine, theirs, wom, wot, base, small, y, yb, n, rstd, *, layer):
    mine_rows, their_rows = halves(core)
    near = dot(mine[...], wom[mine_rows, :]) + dot(theirs[...], wom[their_rows, :])
    far = dot(mine[...], wot[mine_rows, :]) + dot(theirs[...], wot[their_rows, :])
    first = core[0] == 0
    mixed = jnp.concatenate([jnp.where(first, near, far), jnp.where(first, far, near)], axis=1)
    h = base[...] + mixed + small[ROW_OUT + layer : ROW_OUT + layer + 1, :]
    row = 2 * layer
    norm_rows(
        h, small[ROW_GAIN + row : ROW_GAIN + row + 1, :], small[ROW_SHIFT + row : ROW_SHIFT + row + 1, :],
        y, yb, n, rstd,
    )


def out_norm(core, mine, theirs, wom, wot, base, small, layer):
    half = base.shape[0]
    return pl.pallas_call(
        functools.partial(out_norm_kernel, layer=layer),
        name="out_norm",
        out_shape=norm_outs(half),
        in_specs=[pl.BlockSpec(memory_space=pltpu.SMEM)] + [pl.BlockSpec(memory_space=pltpu.VMEM)] * 6,
        out_specs=[pl.BlockSpec(memory_space=pltpu.VMEM)] * 4,
        compiler_params=params(),
        cost_estimate=cost(2 * half * D * D, 2 * D * D + 16 * half * D),
    )(core, mine, theirs, wom, wot, base, small)


def add_norm_kernel(base, part, recv, small, y, yb, n, rstd, *, layer):
    h = base[...] + part[...] + recv[...].astype(F32) + small[ROW_DOWN + layer : ROW_DOWN + layer + 1, :]
    row = 2 * layer + 1
    norm_rows(
        h, small[ROW_GAIN + row : ROW_GAIN + row + 1, :], small[ROW_SHIFT + row : ROW_SHIFT + row + 1, :],
        y, yb, n, rstd,
    )


def add_norm(base, part, recv, small, layer):
    half = base.shape[0]
    return pl.pallas_call(
        functools.partial(add_norm_kernel, layer=layer),
        name="add_norm",
        out_shape=norm_outs(half),
        in_specs=[pl.BlockSpec(memory_space=pltpu.VMEM)] * 4,
        out_specs=[pl.BlockSpec(memory_space=pltpu.VMEM)] * 4,
        compiler_params=params(),
        cost_estimate=cost(20 * half * D, 20 * half * D),
    )(base, part, recv, small)


def norm_bwd_kernel(*refs, row, summed):
    if summed:
        base, part, recv, n, rstd, small, gh, ghb, sums = refs
        gz = base[...] + part[...] + recv[...].astype(F32)
    else:
        base, live, n, rstd, small, gh, ghb, sums = refs
        gz = base[...].astype(F32) * live[...]
    normal = n[...]
    e = gz * small[ROW_GAIN + row : ROW_GAIN + row + 1, :]
    mean = jnp.mean(e, axis=-1, keepdims=True)
    slope = jnp.mean(e * normal, axis=-1, keepdims=True)
    grad = (e - mean - normal * slope) * rstd[...]
    low = grad.astype(BF16)
    gh[...] = grad
    ghb[...] = low
    sums[...] = jnp.zeros_like(sums)
    sums[0:1, :] = jnp.sum(gz * normal, axis=0, keepdims=True)
    sums[1:2, :] = jnp.sum(gz, axis=0, keepdims=True)
    sums[2:3, :] = jnp.sum(low.astype(F32), axis=0, keepdims=True)


def norm_bwd(sources, n, rstd, small, row):
    half = n.shape[0]
    operands = tuple(sources) + (n, rstd, small)
    return pl.pallas_call(
        functools.partial(norm_bwd_kernel, row=row, summed=len(sources) == 3),
        name="norm_bwd",
        out_shape=[sds((half, D), F32), sds((half, D), BF16), sds((8, D), F32)],
        in_specs=[pl.BlockSpec(memory_space=pltpu.VMEM)] * len(operands),
        out_specs=[pl.BlockSpec(memory_space=pltpu.VMEM)] * 3,
        compiler_params=params(),
        cost_estimate=cost(20 * half * D, 20 * half * D),
    )(*operands)


FF_BLOCK = 768
FF_STEPS = FF // CORES // FF_BLOCK


def ffn_fwd_kernel(yo, ys, w1, bias, w2, act, slope, po, ps, acc, *, layer):
    half = yo.shape[0]
    j = pl.program_id(0)
    for first, rows in ((0, yo), (half, ys)):
        span = slice(first, first + half)
        up = dot(rows[...], w1[...]) + bias[layer : layer + 1, :]
        cdf = 0.5 * (1.0 + lax.erf(up * (2.0**-0.5)))
        low = (up * cdf).astype(BF16)
        act[span, :] = low
        slope[span, :] = (cdf + up * (jnp.exp(-0.5 * up * up) * 0.3989422804014327)).astype(BF16)
        total = dot(low, w2[...])

        @pl.when(j == 0)
        def _():
            acc[span, :] = total

        @pl.when(j > 0)
        def _():
            acc[span, :] += total

    @pl.when(j == FF_STEPS - 1)
    def _():
        po[...] = acc[:half, :]
        ps[...] = acc[half:, :].astype(BF16)


DOWN_STEPS = D // FF_BLOCK


def ffn_specs(tokens, col):
    return (
        pl.BlockSpec((D, FF_BLOCK), lambda j: (0, j)),
        pl.BlockSpec((FF_BLOCK, D), lambda j: (j % DOWN_STEPS, col // D + j // DOWN_STEPS)),
        pl.BlockSpec((tokens, FF_BLOCK), lambda j: (0, j)),
    )


def ffn_fwd(yo, ys, w1, w2, col, bias, layer):
    half = yo.shape[0]
    tokens = 2 * half
    width = FF // CORES
    cols, down, rows = ffn_specs(tokens, col)
    return pl.pallas_call(
        functools.partial(ffn_fwd_kernel, layer=layer),
        name="ffn_fwd",
        out_shape=[sds((tokens, width), BF16)] * 2 + [sds((half, D), F32), sds((half, D), BF16)],
        grid=(FF_STEPS,),
        in_specs=[
            whole((half, D)),
            whole((half, D)),
            cols,
            pl.BlockSpec((LAYERS, FF_BLOCK), lambda j: (0, j)),
            down,
        ],
        out_specs=[rows] * 2 + [whole((half, D))] * 2,
        scratch_shapes=[pltpu.VMEM((tokens, D), F32)],
        compiler_params=params(),
        cost_estimate=cost(4 * tokens * D * width, 4 * D * width + 4 * tokens * width, tokens * width),
    )(yo, ys, w1, bias, w2)


def ffn_bwd_kernel(dfo, dfs, w1, w2, act, slope, yo, ys, dw1, dw2, sums, po, ps, acc, du, turned):
    half = yo.shape[0]
    j = pl.program_id(0)

    @pl.when(j == 0)
    def _():
        turned[:, :half] = yo[...].T
        turned[:, half:] = ys[...].T

    for first, rows in ((0, dfo), (half, dfs)):
        span = slice(first, first + half)
        low = (slope[span, :].astype(F32) * dot(rows[...], w2[...], NT)).astype(BF16)
        du[span, :] = low
        total = dot(low, w1[...], NT)

        @pl.when(j == 0)
        def _():
            acc[span, :] = total

        @pl.when(j > 0)
        def _():
            acc[span, :] += total

    sums[...] = jnp.zeros_like(sums)
    sums[0:1, :] = jnp.sum(du[...].astype(F32), axis=0, keepdims=True)
    dw1[...] = dot(turned[...], du[...]).astype(BF16)
    dw2[...] = (dot(act[:half, :], dfo[...], TN) + dot(act[half:, :], dfs[...], TN)).astype(BF16)

    @pl.when(j == FF_STEPS - 1)
    def _():
        po[...] = acc[:half, :]
        ps[...] = acc[half:, :].astype(BF16)


def ffn_bwd(dfo, dfs, w1, w2, col, act, slope, yo, ys):
    half = yo.shape[0]
    tokens = 2 * half
    width = FF // CORES
    cols, down, rows = ffn_specs(tokens, col)
    return pl.pallas_call(
        ffn_bwd_kernel,
        name="ffn_bwd",
        out_shape=[
            sds((2, D, D), BF16),
            sds((2, D, D), BF16),
            sds((8, width), F32),
            sds((half, D), F32),
            sds((half, D), BF16),
        ],
        grid=(FF_STEPS,),
        in_specs=[whole((half, D))] * 2 + [cols, down, rows, rows] + [whole((half, D))] * 2,
        out_specs=[
            pl.BlockSpec((None, D, FF_BLOCK), lambda j: (j // DOWN_STEPS, 0, j % DOWN_STEPS)),
            pl.BlockSpec((None, FF_BLOCK, D), lambda j: (j // DOWN_STEPS, j % DOWN_STEPS, 0)),
            pl.BlockSpec((8, FF_BLOCK), lambda j: (0, j)),
        ]
        + [whole((half, D))] * 2,
        scratch_shapes=[
            pltpu.VMEM((tokens, D), F32),
            pltpu.VMEM((tokens, FF_BLOCK), BF16),
            pltpu.VMEM((D, tokens), BF16),
        ],
        compiler_params=params(),
        cost_estimate=cost(8 * tokens * D * width, 8 * D * width + 4 * tokens * width),
    )(dfo, dfs, w1, w2, act, slope, yo, ys)


def shuffle_kernel(table, *refs, moves, count):
    for out, to, to_col, source, at, at_col, width in moves:
        to = table[to[0]] if isinstance(to, list) else to
        at = table[at[0]] if isinstance(at, list) else at
        refs[count + out][to, :, to_col : to_col + width] = refs[source][at, :, at_col : at_col + width]


def shuffle(table, sources, shapes, moves):
    nbytes = sum(4 * source.size for source in sources)
    return pl.pallas_call(
        functools.partial(shuffle_kernel, moves=moves, count=len(sources)),
        name="shuffle",
        out_shape=shapes,
        in_specs=[pl.BlockSpec(memory_space=pltpu.SMEM)]
        + [pl.BlockSpec(memory_space=pltpu.VMEM)] * len(sources),
        out_specs=[pl.BlockSpec(memory_space=pltpu.VMEM)] * len(shapes),
        compiler_params=params(),
        cost_estimate=cost(0, nbytes),
    )(table, *sources)


def pack_kernel(core, qkv, out, up, mine, send):
    chips = FF // (2 * CORES * FF_CHUNK)
    ups = up[0].astype(F32)
    parts = []
    for parity in range(CORES):
        starts = [
            ((chip * CORES + parity) * 2 + part) * FF_CHUNK for part in range(2) for chip in range(chips)
        ]
        parts.append(jnp.concatenate([ups[:, start : start + FF_CHUNK] for start in starts], axis=1))
    even = core[0] == 0
    for ref, cols, ff in (
        (mine, halves(core)[0], jnp.where(even, parts[0], parts[1])),
        (send, halves(core)[1], jnp.where(even, parts[1], parts[0])),
    ):
        for part in range(3):
            whole_part = qkv.at[0, :, part * D : (part + 1) * D]
            ref[:, part * HALF : (part + 1) * HALF] = whole_part[:, cols]
        ref[:, 3 * HALF : 4 * HALF] = out.at[0][:, cols]
        ref[:, 4 * HALF :] = ff.astype(BF16)


FF_CHUNK = 48
PACKED = 4 * HALF + FF // CORES


def layer_block(shape, layer):
    return pl.BlockSpec((1,) + shape, lambda *_: (layer, 0, 0))


def pack(core, attn_in, attn_out, ffn_in, layer):
    rows = attn_in.shape[1]
    return pl.pallas_call(
        pack_kernel,
        name="pack",
        out_shape=[sds((rows, PACKED), BF16)] * 2,
        grid=(1,),
        in_specs=[
            pl.BlockSpec(memory_space=pltpu.SMEM),
            layer_block((rows, 3 * D), layer),
            layer_block((rows, D), layer),
            layer_block((rows, FF), layer),
        ],
        out_specs=[whole((rows, PACKED))] * 2,
        compiler_params=params(),
        cost_estimate=cost(0, 8 * rows * PACKED),
    )(core, attn_in, attn_out, ffn_in)


def join_kernel(core, mine, recv, down, *outs):
    rows = mine.shape[0]
    even = core[0] == 0
    near, far = mine[...].astype(F32), recv[...].astype(F32)
    both = jnp.concatenate([jnp.where(even, near, far), jnp.where(even, far, near)], axis=0).astype(BF16)
    downs = [down[0, part * CORES * rows : (part + 1) * CORES * rows, :] for part in range(2)]
    attn, ffn = outs
    for unit in range(2):
        attn[unit] = both[:, unit * D : (unit + 1) * D]
        ffn[2 * unit] = both[:, (2 + unit) * D : (3 + unit) * D]
        ffn[2 * unit + 1] = downs[unit]


def join(core, mine, recv, ffn_out, layer, shapes):
    rows = mine.shape[0]
    down = ffn_out.shape[1]
    return pl.pallas_call(
        join_kernel,
        name="join",
        out_shape=[sds(shape, BF16) for shape in shapes],
        grid=(1,),
        in_specs=[
            pl.BlockSpec(memory_space=pltpu.SMEM),
            whole((rows, PACKED)),
            whole((rows, PACKED)),
            layer_block((down, D), layer),
        ],
        out_specs=[whole(shape) for shape in shapes],
        compiler_params=params(),
        cost_estimate=cost(0, 8 * rows * PACKED),
    )(core, mine, recv, ffn_out)


def split_kernel(core, *refs):
    mine, send = refs[-2:]
    rows = mine.shape[0]
    even = core[0] == 0
    for part, block in enumerate(refs[:-2]):
        top, bottom = block[:rows, :], block[rows:, :]
        mine[:, part * D : (part + 1) * D] = jnp.where(even, top, bottom)
        send[:, part * D : (part + 1) * D] = jnp.where(even, bottom, top)


def split(core, units):
    rows = units[0].shape[0] // CORES
    return pl.pallas_call(
        split_kernel,
        name="split",
        out_shape=[sds((rows, PACKED), F32)] * 2,
        in_specs=[pl.BlockSpec(memory_space=pltpu.SMEM)] + [pl.BlockSpec(memory_space=pltpu.VMEM)] * len(units),
        out_specs=[pl.BlockSpec(memory_space=pltpu.VMEM)] * 2,
        compiler_params=params(),
        cost_estimate=cost(0, 16 * rows * PACKED),
    )(core, *units)


def merge_kernel(core, *refs):
    qkv, out, up, down = refs[4 * LAYERS :]
    chips = FF // (2 * CORES * FF_CHUNK)
    even = core[0] == 0
    for layer in range(LAYERS):
        mine, recv, first_down, second_down = refs[4 * layer : 4 * layer + 4]
        near, far = mine[...], recv[...]
        first, second = jnp.where(even, near, far), jnp.where(even, far, near)
        for part in range(3):
            span = slice(part * HALF, (part + 1) * HALF)
            qkv[layer, :, part * D : part * D + HALF] = first[:, span]
            qkv[layer, :, part * D + HALF : (part + 1) * D] = second[:, span]
        out[layer, :, :HALF] = first[:, 3 * HALF : 4 * HALF]
        out[layer, :, HALF:] = second[:, 3 * HALF : 4 * HALF]
        chunks = []
        for chip in range(chips):
            for source in (first, second):
                for part in range(2):
                    start = 4 * HALF + part * D + chip * FF_CHUNK
                    chunks.append(source[:, start : start + FF_CHUNK])
        up[layer] = jnp.concatenate(chunks, axis=1)
        rows = first_down.shape[0]
        down[layer, :rows, :] = first_down[...]
        down[layer, rows:, :] = second_down[...]


def merge(core, parts):
    rows = parts[0].shape[0]
    down = 2 * parts[2].shape[0]
    return pl.pallas_call(
        merge_kernel,
        name="merge",
        out_shape=[
            sds((LAYERS, rows, 3 * D), F32),
            sds((LAYERS, rows, D), F32),
            sds((LAYERS, rows, FF), F32),
            sds((LAYERS, down, D), F32),
        ],
        in_specs=[pl.BlockSpec(memory_space=pltpu.SMEM)] + [pl.BlockSpec(memory_space=pltpu.VMEM)] * len(parts),
        out_specs=[pl.BlockSpec(memory_space=pltpu.VMEM)] * 4,
        compiler_params=params(),
        cost_estimate=cost(0, 32 * rows * PACKED),
    )(core, *parts)


class Places:
    def __init__(self, pages, bands):
        self.ny = bands // CORES
        self.nx = self.ny if pages % self.ny == 0 else 1
        self.nz = pages // self.nx
        self.chips = pages * self.ny
        page, band = lax.axis_index("page"), lax.axis_index("band")
        self.z, self.x = page // self.nx, page % self.nx
        self.y, self.core = band // CORES, band % CORES
        self.sizes = (self.nz, self.nx, self.ny, CORES)

    def move(self, value, axis, step, flip=False):
        pairs = []
        nz, nx, ny, nc = self.sizes
        for device in range(nz * nx * ny * nc):
            place = [device // (nx * ny * nc), device // (ny * nc) % nx, device // nc % ny, device % nc]
            place[axis] = place[axis] ^ step if flip else (place[axis] + step) % self.sizes[axis]
            pairs.append((device, ((place[0] * nx + place[1]) * ny + place[2]) * nc + place[3]))
        return lax.ppermute(value, ("page", "band"), pairs)

    def exchange(self, wants):
        keys = []
        for axis, step, _ in wants:
            key = (axis, step if axis == 0 else step % self.sizes[axis])
            keys.append(key)
        got = [None] * len(wants)
        for key in dict.fromkeys(keys):
            numbers = [i for i, other in enumerate(keys) if other == key]
            flat = [wants[i][2].reshape(-1, wants[i][2].shape[-1]) for i in numbers]
            moved = self.move(jnp.concatenate(flat) if len(flat) > 1 else flat[0], *key, flip=key[0] == 0)
            first = 0
            for i, part in zip(numbers, flat):
                got[i] = moved[first : first + part.shape[0]].reshape(wants[i][2].shape)
                first += part.shape[0]
        return got

    def swap(self, value):
        return self.move(value, 3, 1)

    def chip_of(self, kz, kx, ky):
        z, x, y = self.z ^ kz, (self.x - kx) % self.nx, (self.y - ky) % self.ny
        return (z * self.nx + x) * self.ny + y

    def flips(self):
        return [1 << bit for bit in reversed(range(self.nz.bit_length() - 1))]


def tie(values, *others):
    return lax.optimization_barrier((values, others))[0]


class Gather:
    def __init__(self, at, local, shapes, place):
        self.at, self.local = at, local
        self.half = local.shape[0] // 2
        self.shapes, self.place = shapes, place
        self.stages = [functools.partial(self.flip, step) for step in at.flips()]
        self.stages += [self.first, self.second]
        self.held = local[None]
        self.spots = [0]

    def flip(self, step, got):
        if got:
            self.held = jnp.concatenate([self.held] + list(got))
        self.spots = self.spots + [spot ^ step for spot in self.spots]
        return [(0, step, self.held)]

    def near(self, axis, part):
        return [(axis, k, part) for k in range(1, self.at.sizes[axis])]

    def first(self, got):
        held = jnp.concatenate([self.held] + list(got))
        self.sent = [held[:, : self.half], held[:, self.half :]]
        return self.near(1, self.sent[0]) + self.near(2, self.sent[1])

    def second(self, got):
        cut = self.at.nx - 1
        self.sent = [jnp.stack([part] + got) for part, got in zip(self.sent, (got[:cut], got[cut:]))]
        return self.near(2, self.sent[0]) + self.near(1, self.sent[1])

    def finish(self, got):
        at = self.at
        rows, cols = self.local.shape[1:]
        sources, moves, table = [], [], []
        cut = at.ny - 1
        for axes, part, other, start in (
            ((1, 2), self.sent[0], got[:cut], 0),
            ((2, 1), self.sent[1], got[cut:], self.half),
        ):
            for far, piece in enumerate([part] + list(other)):
                number = 0
                for near in range(at.sizes[axes[0]]):
                    kx, ky = (near, far) if axes[0] == 1 else (far, near)
                    for kz in self.spots:
                        chip = at.chip_of(kz, kx, ky)
                        for unit in range(start, start + self.half):
                            for out, step, offset, to_col, at_col, width in self.place[unit]:
                                moves.append(
                                    (out, [len(table)], to_col, len(sources), number, at_col, width)
                                )
                                table.append(chip * step + offset)
                            number += 1
                sources.append(piece.reshape((-1, rows, cols)))
        outs = shuffle(jnp.stack(table), sources, [sds(shape, BF16) for shape in self.shapes], moves)
        return [out.reshape(-1, out.shape[-1]) for out in outs]


class LateGather(Gather):
    def __init__(self, at, local, shapes, place, idle):
        self.at, self.local = at, local
        self.half = local.shape[0] // 2
        self.shapes, self.place = shapes, place
        self.stages = [self.first, self.second] + [self.rest] * idle
        self.stages += [functools.partial(self.flip, step) for step in at.flips()]
        self.spots = [0]
        self.got = None

    def first(self, got):
        self.sent = [self.local[None, : self.half], self.local[None, self.half :]]
        return self.near(1, self.sent[0]) + self.near(2, self.sent[1])

    def rest(self, got):
        if got:
            self.got = got
        return []

    def flip(self, step, got):
        if self.got is not None:
            got = self.got
        if len(self.spots) == 1:
            cut = self.at.ny - 1
            self.held = jnp.concatenate(
                [jnp.stack([part] + list(other)).reshape((-1,) + part.shape[-3:])
                 for part, other in zip(self.sent, (got[:cut], got[cut:]))],
                axis=1,
            )[None]
        else:
            self.held = jnp.concatenate([self.held] + list(got))
        self.got = None
        self.spots = self.spots + [spot ^ step for spot in self.spots]
        return [(0, step, self.held)]

    def finish(self, got):
        at = self.at
        rows, cols = self.local.shape[1:]
        sources, moves, table = [], [], []
        spots = len(self.spots) // 2
        for number, piece in enumerate([self.held] + list(got)):
            at_block = 0
            for spot in self.spots[number * spots : (number + 1) * spots]:
                for far in range(at.nx):
                    for near in range(at.ny):
                        for unit in range(2 * self.half):
                            kx, ky = (near, far) if unit < self.half else (far, near)
                            for out, step, offset, to_col, at_col, width in self.place[unit]:
                                moves.append((out, [len(table)], to_col, number, at_block, at_col, width))
                                table.append(at.chip_of(spot, kx, ky) * step + offset)
                            at_block += 1
            sources.append(piece.reshape((-1, rows, cols)))
        outs = shuffle(jnp.stack(table), sources, [sds(shape, BF16) for shape in self.shapes], moves)
        return [out.reshape(-1, out.shape[-1]) for out in outs]


class Reduce:
    def __init__(self, at, first, second):
        self.at, self.halves = at, (first, second)
        self.stages = [self.first, self.second]
        self.stages += [functools.partial(self.flip, number) for number in range(len(at.flips()))]

    def picked(self, groups, axis, index):
        at = self.at
        rows = []
        for group in groups:
            parts = []
            for part in group:
                blocks = part.reshape(at.nz, at.nx, at.ny, part.shape[0] // at.chips, part.shape[1])
                parts.append(pick(blocks, index, axis))
            rows.append(jnp.concatenate(parts, axis=-1) if len(parts) > 1 else parts[0])
        return jnp.concatenate(rows, axis=2) if len(rows) > 1 else rows[0]

    def first(self, got):
        at = self.at
        wants = [(2, -k, self.picked(self.halves[0], 2, (at.y - k) % at.ny)) for k in range(1, at.ny)]
        return wants + [
            (1, -k, self.picked(self.halves[1], 1, (at.x - k) % at.nx)) for k in range(1, at.nx)
        ]

    def second(self, got):
        at = self.at
        cut = at.ny - 1
        self.lows = []
        for mine, other in (
            (self.picked(self.halves[0], 2, at.y), got[:cut]),
            (self.picked(self.halves[1], 1, at.x), got[cut:]),
        ):
            self.lows.append(self.total(mine, other).astype(BF16))
        wants = [(1, -k, pick(self.lows[0], (at.x - k) % at.nx, 1)) for k in range(1, at.nx)]
        return wants + [(2, -k, pick(self.lows[1], (at.y - k) % at.ny, 1)) for k in range(1, at.ny)]

    def total(self, mine, other):
        mine = mine.astype(F32)
        for term in other:
            mine = mine + term.astype(F32)
        return mine

    def flip(self, number, got):
        at = self.at
        bit = 1 << number
        if number == 0:
            cut = at.nx - 1
            first = self.total(pick(self.lows[0], at.x, 1), got[:cut])
            second = self.total(pick(self.lows[1], at.y, 1), got[cut:])
            self.cut = first.shape[1]
            low = jnp.concatenate([first, second], axis=1).astype(BF16)
        else:
            low = self.total(self.low, got).astype(BF16)
        low = low.reshape((low.shape[0] // 2, 2) + low.shape[1:])
        side = at.z // bit % 2
        self.low = pick(low, side, 1)
        return [(0, bit, pick(low, 1 - side, 1))]

    def finish(self, got):
        total = self.total(self.low, got)[0]
        return total[: self.cut], total[self.cut :]


class Line:
    def __init__(self, at):
        self.at, self.chunks, self.age, self.got = at, [], [], []

    def add(self, chunk):
        self.chunks.append(chunk)
        self.age.append(0)
        self.got.append([])

    def step(self, *others, extra=None):
        wants, spans = [], []
        for number, chunk in enumerate(self.chunks):
            if self.age[number] < len(chunk.stages):
                new = chunk.stages[self.age[number]](self.got[number])
                spans.append((number, len(wants), len(wants) + len(new)))
                wants += new
                self.age[number] += 1
        values, others = lax.optimization_barrier(([want[2] for want in wants], others))
        wants = [want[:2] + (value,) for want, value in zip(wants, values)]
        self.spans, self.moved = spans, self.at.exchange(wants)
        return others

    def close(self, *others):
        self.moved, others = lax.optimization_barrier((self.moved, others))
        for number, start, stop in self.spans:
            self.got[number] = self.moved[start:stop]
        return others

    def busy(self):
        return not all(self.done(chunk) for chunk in self.chunks)

    def done(self, chunk):
        number = self.chunks.index(chunk)
        return self.age[number] == len(chunk.stages)

    def fresh(self, chunk):
        return self.done(chunk) and any(span[0] == self.chunks.index(chunk) for span in self.spans)

    def result(self, chunk):
        return chunk.finish(self.got[self.chunks.index(chunk)])


def blocks_kernel(scalars, *refs, counts, loads, jobs):
    sources, outs = refs[: counts[0]], refs[counts[0] : counts[0] + counts[1]]
    buffers = refs[counts[0] + counts[1] : -2]
    load_sems, out_sems = refs[-2:]

    def rows(place, height):
        start, slopes = place
        for number, slope in slopes:
            start = start + scalars[number] * slope
        return pl.ds(pl.multiple_of(start, 16) if slopes else start, height)

    copies = []
    for number, (source, place, height, buffer, row, col, width) in enumerate(loads):
        copies.append(
            pltpu.make_async_copy(
                sources[source].at[rows(place, height), :],
                buffers[buffer].at[row : row + height, col : col + width],
                load_sems.at[number],
            )
        )
    for copy in copies:
        copy.start()
    waited = set()

    def wait(numbers):
        for number in numbers:
            if number not in waited:
                waited.add(number)
                copies[number].wait()

    stores = []
    for out, (needs, sums) in enumerate(jobs):
        for to, height, terms in sums:
            total = None
            for buffer, place, numbers in terms:
                wait(numbers)
                value = buffers[buffer][rows(place, height), :].astype(buffers[out].dtype)
                total = value if total is None else total + value
            buffers[out][to : to + height, :] = total.astype(buffers[out].dtype)
        wait(needs)
        stores.append(pltpu.make_async_copy(buffers[out], outs[out], out_sems.at[out]))
        stores[-1].start()
    for store in stores:
        store.wait()


class Stream:
    def __init__(self, parts, first_y, rows, base=0):
        self.parts, self.first_y, self.rows, self.base = parts, first_y, rows, base
        self.age = 0
        self.keep = self.recv = self.total = self.joined = None


class Joined:
    def __init__(self, streams):
        self.streams, self.out, self.total = streams, None, None
        self.rows = sum(stream.rows for stream in streams)
        for stream in streams:
            stream.joined = self

    def start(self, stream):
        return sum(other.rows for other in self.streams[: self.streams.index(stream)])


class Pipe:
    def __init__(self, at):
        self.at, self.groups = at, []
        self.bits = at.nz.bit_length() - 1
        self.last = 2 + self.bits
        scalars = [at.x, at.y] + [at.z // (1 << bit) % 2 for bit in range(self.bits)]
        self.scalars = jnp.stack(scalars).astype(jnp.int32)

    def add(self, streams):
        self.groups.append(streams)

    def pieces(self, stream, rows):
        nz = self.at.nz
        first = 1 if stream.first_y else 0
        strides = (2, 1)

        def chip(z, coords):
            start, slopes = stream.base + 4 * z * rows, []
            for axis, (fixed, slope) in enumerate(coords):
                start += fixed * strides[axis] * rows
                if slope:
                    slopes.append((axis, slope * strides[axis] * rows))
            return start, slopes

        def spot(fixed, number, slope, scale, base=0):
            return (base + fixed * scale, [(number, slope * scale)])

        other, same = (1, -1), (0, 1)
        sent, kept = [], []
        if stream.age == 0:
            for z in range(nz):
                for far in range(2):
                    coords = [None, None]
                    coords[first], coords[1 - first] = other, (far, 0)
                    sent.append([(stream.parts, chip(z, coords))])
        elif stream.age == 1:
            ref, base = stream.recv
            for out, side in ((sent, other), (kept, same)):
                for z in range(nz):
                    coords = [None, None]
                    coords[first], coords[1 - first] = same, side
                    place = spot(2 * z + side[0], 1 - first, side[1], rows, base)
                    out.append([(stream.parts, chip(z, coords)), ([ref], place)])
        elif stream.age < self.last:
            bit = stream.age - 2
            ref, base = stream.recv
            for out, side in ((sent, other), (kept, same)):
                for high in range(nz >> (bit + 1)):
                    fixed = 2 * high + side[0]
                    keep = spot(fixed, 2 + bit, side[1], rows)
                    out.append([([stream.keep], keep), ([ref], spot(fixed, 2 + bit, side[1], rows, base))])
        else:
            ref, base = stream.recv
            kept.append([([stream.keep], (0, [])), ([ref], (base, []))])
        return sent, kept

    def step(self, *others, extra=None):
        heights, keeps, todo, self.sent = {}, [], [], []
        spots, self.joined = [], None
        for streams in self.groups:
            for stream in streams:
                if stream.age > self.last:
                    continue
                rows = stream.rows
                sent, kept = self.pieces(stream, rows)
                axis = (2, 1) if stream.first_y else (1, 2)
                key = axis[stream.age] if stream.age < 2 else -stream.age
                start = heights.get(key, 0)
                if sent:
                    heights[key] = start + len(sent) * rows
                    self.sent.append((stream, key, start))
                todo.append((stream, key, start, sent, kept, rows))
        if extra is not None:
            span = (heights.get(2, 0), extra.shape[0])
            heights[2] = sum(span)
        order = list(heights)
        shapes = [sds((heights[key], D), BF16) for key in order]
        jobs = [([], []) for _ in order]
        arrays, loads, buffers, held = [], [], [], {}

        def source(array):
            for i, known in enumerate(arrays):
                if known is array:
                    return i
            arrays.append(array)
            return len(arrays) - 1

        for stream, key, start, sent, kept, rows in todo:
            if kept:
                last = stream.age == self.last
                if last and stream.joined is not None:
                    if stream.joined.out is None:
                        stream.joined.out = len(shapes)
                        shapes.append(sds((stream.joined.rows, D), F32))
                        jobs.append(([], []))
                        self.joined = stream.joined
                    spots.append((stream.joined.out, stream.joined.start(stream)))
                    continue
                keeps.append((stream, len(shapes)))
                spots.append((len(shapes), 0))
                shapes.append(sds((len(kept) * rows, D), F32 if last else BF16))
                jobs.append(([], []))
        buffers = list(shapes)
        if extra is not None:
            jobs[order.index(2)][0].append(len(loads))
            loads.append((source(extra), (0, []), span[1], order.index(2), span[0], 0, D))
        spare = len(buffers)
        buffers.append(None)
        spare_rows = 0

        def term(parts, place, height):
            nonlocal spare_rows
            if len(parts) == 1 and not any(part is parts[0] for part in stream.parts):
                array = source(parts[0])
                if array not in held:
                    held[array] = (len(buffers), len(loads))
                    loads.append((array, (0, []), parts[0].shape[0], len(buffers), 0, 0, D))
                    buffers.append(sds(parts[0].shape, parts[0].dtype))
                return held[array][0], place, [held[array][1]]
            row, numbers = spare_rows, []
            spare_rows += height
            for number, part in enumerate(parts):
                width = D // len(parts)
                numbers.append(len(loads))
                loads.append((source(part), place, height, spare, row, number * width, width))
            return spare, (row, []), numbers

        for stream, key, start, sent, kept, rows in todo:
            for block, terms in enumerate(sent):
                out = order.index(key)
                to = start + block * rows
                if len(terms) == 1:
                    ((parts, place),) = terms
                    for number, part in enumerate(parts):
                        width = D // len(parts)
                        jobs[out][0].append(len(loads))
                        loads.append((source(part), place, rows, out, to, number * width, width))
                else:
                    jobs[out][1].append((to, rows, [term(parts, place, rows) for parts, place in terms]))
        spots = iter(spots)
        for stream, key, start, sent, kept, rows in todo:
            if kept:
                out, first = next(spots)
                for block, terms in enumerate(kept):
                    terms = [term(parts, place, rows) for parts, place in terms]
                    jobs[out][1].append((first + block * rows, rows, terms))
        buffers[spare] = sds((max(spare_rows, 16), D), BF16)
        outs = pl.pallas_call(
            functools.partial(
                blocks_kernel, counts=(len(arrays), len(shapes)), loads=loads, jobs=jobs
            ),
            name="blocks",
            out_shape=shapes,
            in_specs=[pl.BlockSpec(memory_space=pltpu.SMEM)]
            + [pl.BlockSpec(memory_space=pltpu.HBM)] * len(arrays),
            out_specs=[pl.BlockSpec(memory_space=pltpu.HBM)] * len(shapes),
            scratch_shapes=[pltpu.VMEM(buffer.shape, buffer.dtype) for buffer in buffers]
            + [pltpu.SemaphoreType.DMA((len(loads),)), pltpu.SemaphoreType.DMA((len(shapes),))],
            compiler_params=params(),
            cost_estimate=cost(0, sum(3 * array.size for array in arrays)),
        )(self.scalars, *arrays)
        if self.joined is not None:
            self.joined.total = outs[self.joined.out]
        for stream, out in keeps:
            stream.keep = outs[out]
            if stream.age == self.last:
                stream.total = outs[out]
        for stream, *_ in todo:
            stream.age += 1
        payloads, others = lax.optimization_barrier((outs[: len(order)], others))
        self.moved = {}
        self.span = None if extra is None else span
        for key, payload in zip(order, payloads):
            if key > 0:
                self.moved[key] = self.at.move(payload, key, 1)
            else:
                self.moved[key] = self.at.move(payload, 0, 1 << (-key - 2), flip=True)
        return others

    def close(self, *others):
        self.moved, others = lax.optimization_barrier((self.moved, others))
        for stream, key, start in self.sent:
            stream.recv = (self.moved[key], start)
        if self.span is not None:
            self.extra = [self.moved[2][self.span[0] : sum(self.span)]]
        return others

    def busy(self):
        return any(stream.age <= self.last for streams in self.groups for stream in streams)


def pick(stacked, index, axis=0):
    return lax.dynamic_index_in_dim(stacked, index, axis, keepdims=False)


def by_core(core, mine, theirs, axis):
    return jnp.where(core == 0, jnp.stack([mine, theirs], axis), jnp.stack([theirs, mine], axis))


def body(
    hidden,
    boxes,
    page_size,
    band_count,
    layout_tables,
    attn_in,
    attn_bias,
    attn_out,
    out_bias,
    norm_gain,
    norm_bias,
    ffn_in,
    ffn_in_bias,
    ffn_out,
    ffn_out_bias,
    out_grad,
    *,
    pages,
    bands,
):
    at = Places(pages, bands)
    core = at.core
    core_id = core.astype(jnp.int32).reshape(1)
    devices = pages * bands
    ny, chips = at.ny, at.chips
    cap = hidden.shape[2]
    rows_dev = attn_in.shape[1]
    table_rows = layout_tables.shape[1]
    ff_dev = ffn_out.shape[1]
    chip_rows = CORES * rows_dev
    tiled = rows_dev % 8 == 0 and ff_dev == 2 * FF_CHUNK and at.nx == ny == 2

    def local_weights(layer):
        if tiled:
            mine, send = pack(core_id, attn_in, attn_out, ffn_in, layer)
            shapes = ((2, chip_rows, D), (4, chip_rows, D))
            return join(core_id, mine, at.swap(send), ffn_out, layer, shapes)
        columns = jnp.concatenate(
            [attn_in[layer].reshape(rows_dev, 3, CORES, HALF), attn_out[layer].reshape(rows_dev, 1, CORES, HALF)],
            axis=1,
        ).transpose(2, 0, 1, 3)
        ups = ffn_in[layer].reshape(rows_dev, chips, CORES, 2, ff_dev // 2).transpose(2, 0, 3, 1, 4)
        packed = jnp.concatenate(
            [columns.reshape(CORES, rows_dev, 4 * HALF), ups.reshape(CORES, rows_dev, FF // CORES)], axis=2
        )
        both = by_core(core, pick(packed, core), at.swap(pick(packed, 1 - core)), 0)
        both = both.reshape(chip_rows, PACKED)
        down = ffn_out[layer].reshape(2, chip_rows, D)
        both = both.reshape(chip_rows, 4, D).swapaxes(0, 1)
        return both[:2], jnp.stack([both[2], down[0], both[3], down[1]])

    attn_place = ([(0, 1, 0, 0, 0, D)], [(0, 1, 0, D, 0, D), (1, 1, 0, 0, HALF, HALF)])
    attn_shapes = ((chips, chip_rows, 2 * D), (chips, chip_rows, HALF))
    ffn_place = [[(0, 1, 0, col * D, 0, D)] for col in (0, 2, 1, 3)]
    ffn_shapes = ((chips, chip_rows, 4 * D),)
    table_place = [[(table, 1, 0, 0, 0, D)] for table in range(4)]
    table_shapes = ((chips, table_rows, D),) * 4

    def to_chip(stacked):
        own = [pick(stacked, at.y)]
        for k in range(1, ny):
            own.append(at.move(pick(stacked, (at.y + k) % ny), 2, k))
        return own

    def send_back(rows):
        parts = rows.reshape((ny, cap) + rows.shape[1:])
        return [at.move(parts[k].astype(BF16), 2, -k) for k in range(1, ny)]

    def from_chip(rows, back):
        back = [rows[:cap]] + [part.astype(F32) for part in back]
        back = jnp.stack(back)
        return jnp.stack([pick(back, (page - at.y) % ny) for page in range(ny)])[:, None]

    def token_facts(hidden, out_grad, boxes, page_size, band_count):
        widths, heights = page_size[0][:, None], page_size[1][:, None]
        left = boxes[0, :, 0] * GRID // widths
        top = boxes[1, :, 0] * GRID // heights
        right = boxes[2, :, 0] * GRID // widths
        bottom = boxes[3, :, 0] * GRID // heights
        live = (lax.broadcasted_iota(jnp.int32, left.shape, 1) < band_count).astype(jnp.int32)
        facts = jnp.stack([left, top, right, bottom, bottom - top, right - left, live, live], axis=1)
        facts_own = jnp.concatenate(to_chip(facts), axis=-1)
        facts_all = jnp.concatenate([facts_own, at.swap(facts_own)], axis=-1)
        owner = facts_all // table_rows
        index = jnp.where(
            owner % CORES == core, owner // CORES * table_rows + facts_all % table_rows, -1
        )
        mask = jnp.where(facts_all[6:7] > 0, 0.0, DEAD).astype(F32)
        live_own = facts_own[6].astype(F32)[:, None]
        hidden_own = jnp.concatenate(to_chip(hidden[:, 0]), axis=0)
        grad_own = jnp.concatenate(to_chip(out_grad[:, 0]), axis=0)
        return index, mask, live_own, hidden_own, grad_own

    cut = SMALL_ROWS * rows_dev

    def small_params(attn_bias, out_bias, norm_gain, norm_bias, ffn_out_bias, ffn_in_bias):
        segment = jnp.concatenate(
            [
                attn_bias.reshape(-1),
                out_bias.reshape(-1),
                norm_gain.reshape(-1),
                norm_bias.reshape(-1),
                ffn_out_bias.reshape(-1),
                ffn_in_bias.reshape(-1),
            ]
        )
        smalls = lax.all_to_all(
            jnp.broadcast_to(segment, (devices, segment.shape[0])), ("page", "band"), 0, 0, tiled=True
        ).astype(F32)
        small = smalls[:, :cut].reshape(devices, SMALL_ROWS, rows_dev).swapaxes(0, 1).reshape(SMALL_ROWS, D)
        up_bias = pick(smalls[:, cut:].reshape(chips, CORES, LAYERS, 2, ff_dev // 2), core, 1)
        up_bias = up_bias.transpose(1, 2, 0, 3).reshape(LAYERS, FF // CORES)
        return small, up_bias

    saved = [[], []]
    weights = [[], []]

    def look_up(state):
        tables = line.result(chunks[0])
        looked_up = embed(index.T, tables)
        mine = hidden_own.astype(F32) + looked_up[:half]
        x = mine + at.swap(looked_up[half:].astype(BF16)).astype(F32)
        return x, x.astype(BF16)

    def attend(layer, state):
        x, x_low = state
        wa, wom = line.result(chunks[1 + 2 * layer])
        wot, x_other = at.swap(wom), at.swap(x_low)
        weights[layer] += [wa, wom, wot]
        q, k, v, mix_own, mix_other = attn_fwd(core_id, x_low, x_other, wa, small, mask, layer)
        y1, y1_low, n1, r1 = out_norm(core_id, mix_own, at.swap(mix_other), wom, wot, x, small, layer)
        saved[layer] += [x_low, x_other, q, k, v, mix_own, mix_other, n1, r1]
        return y1, y1_low

    def feed(layer, state):
        y1, y1_low = state
        (w1,) = line.result(chunks[2 + 2 * layer])
        w2, col = (w1, 2 * D) if layer == 0 else (downs[0], 0)
        y1_other = at.swap(y1_low)
        weights[layer] += [w1, w2, col]
        act, slope, part, part_other = ffn_fwd(y1_low, y1_other, w1, w2, col, up_bias, layer)
        x, x_low, n2, r2 = add_norm(y1, part, at.swap(part_other), small, layer)
        saved[layer] += [y1_low, y1_other, act, slope, n2, r2]
        return x, x_low

    half = ny * cap
    line = Line(at)
    chunks = [Gather(at, layout_tables, table_shapes, table_place)]
    parts = [look_up]
    line.add(chunks[0])
    down_chunk = LateGather(
        at,
        ffn_out[LAYERS - 1].reshape(2, chip_rows, D),
        ((chips, chip_rows, 2 * D),),
        ([(0, 1, 0, 0, 0, D)], [(0, 1, 0, D, 0, D)]),
        3,
    )
    line.add(down_chunk)
    line.step()
    locals0 = local_weights(0)
    token_args = (hidden, out_grad, boxes, page_size, band_count)
    small_args = (attn_bias, out_bias, norm_gain, norm_bias, ffn_out_bias, ffn_in_bias)
    locals0, token_args = line.close(locals0, token_args)
    state, downs = (), []
    running = None
    waiting = []
    for layer in range(LAYERS):
        waiting += [(layer, 0), (layer, 1)]
        parts += [functools.partial(attend, layer), functools.partial(feed, layer)]
    local = locals0
    while waiting or running is not None or not line.done(chunks[-1]):
        if waiting:
            layer, number = waiting.pop(0)
            if layer > 0 and number == 0:
                local = local_weights(layer)
            if layer > 0 and number == 1:
                shard = jnp.stack([local[1][0], local[1][2]])
                shapes, place = ((chips, chip_rows, 2 * D),), ([(0, 1, 0, 0, 0, D)], [(0, 1, 0, D, 0, D)])
            else:
                shard = local[number]
                shapes, place = (attn_shapes, ffn_shapes)[number], (attn_place, ffn_place)[number]
            chunks.append(Gather(at, shard, shapes, place))
            line.add(chunks[-1])
        if all(line.done(chunk) for chunk in chunks):
            state = running(state)
            break
        state = line.step(*state)
        if line.done(down_chunk) and not downs and not line.fresh(down_chunk):
            downs.append(line.result(down_chunk)[0])
        if running is not None:
            state = running(state)
        if len(chunks) == 2:
            tokens, small_args, late = line.close(
                token_facts(*token_args), small_args, (attn_in, attn_out, ffn_in)
            )
            index, mask, live_own, hidden_own, grad_own = tokens
            attn_in, attn_out, ffn_in = late
        elif len(chunks) == 3:
            (small_args,) = line.close(small_args)
        elif len(chunks) == 4:
            small, up_bias = line.close(*small_params(*small_args))
        elif downs:
            state, downs = line.close(state, downs)
        else:
            state = line.close(*state)
        ready = [number for number, chunk in enumerate(chunks) if line.fresh(chunk)]
        running = parts[ready[0]] if ready else None
    x = state[0]

    small_grads = [None] * LAYERS

    def backward_ffn(layer, sources):
        w1, w2, col = weights[layer][3:]
        y1_low, y1_other, act, slope, n2, r2 = saved[layer][9:]
        gh2, df, sums2 = norm_bwd(sources, n2, r2, small, 2 * layer + 1)
        dw1, dw2, up_sums, part, part_other = ffn_bwd(df, at.swap(df), w1, w2, col, act, slope, y1_low, y1_other)
        small_grads[layer] = [sums2, up_sums]
        return (gh2, part, at.swap(part_other)), dw1, dw2

    def backward_attn(layer, sources):
        wa, wom, wot = weights[layer][:3]
        x_low, x_other, q, k, v, mix_own, mix_other, n1, r1 = saved[layer][:9]
        gh1, da, sums1 = norm_bwd(sources, n1, r1, small, 2 * layer)
        dwq, dwk, dwv, dwo, attn_sums, part, part_other = attn_bwd(
            core_id, da, at.swap(da), wom, wot, q, k, v, mix_own, mix_other, x_low, x_other, wa, mask
        )
        small_grads[layer] = [sums1] + small_grads[layer] + [attn_sums]
        return (gh1, part, at.swap(part_other)), (dwq, dwk, dwv), (pick(dwo, core), at.swap(pick(dwo, 1 - core)))

    def attn_groups(dqkv, dwo):
        dwq, dwk, dwv = dqkv
        return [dwq, dwk], [dwv, by_core(core, *dwo, 0).reshape(D, HALF)]

    line = Pipe(at) if tiled else Line(at)

    def ffn_chunk(dw1, dw2):
        if tiled:
            flat = [dw.reshape(2 * D, D) for dw in (dw1, dw2)]
            streams = [Stream([unit], part == 0, chip_rows, part * D) for part in range(2) for unit in flat]
            line.add(streams)
            return streams
        chunk = Reduce(at, [[dw1[0]], [dw2[0]]], [[dw1[1]], [dw2[1]]])
        line.add(chunk)
        return chunk

    def attn_chunk(dqkv, dwo):
        first, second = attn_groups(dqkv, dwo)
        if tiled:
            streams = [Stream(first, True, chip_rows), Stream(second, False, chip_rows)]
            line.add(streams)
            return streams
        chunk = Reduce(at, [first], [second])
        line.add(chunk)
        return chunk

    def table_chunk(tables):
        if tiled:
            streams = [Stream([table], number < 2, table_rows) for number, table in enumerate(tables)]
            line.add(streams)
            return Joined(streams)
        chunk = Reduce(at, [[table] for table in tables[:2]], [[table] for table in tables[2:]])
        line.add(chunk)
        return chunk

    sources, dw1, dw2 = backward_ffn(1, (grad_own, live_own))
    ffn1 = ffn_chunk(dw1, dw2)
    output = x * live_own
    sources = line.step(*sources, extra=output[cap:].astype(BF16) if tiled else None)
    sources, dqkv, dwo = backward_attn(1, sources)
    sources = line.close(*sources)
    output = from_chip(output, line.extra if tiled else send_back(output))
    att1 = attn_chunk(dqkv, dwo)
    sources = line.step(*sources)
    sources, dw1, dw2 = backward_ffn(0, sources)
    sources = line.close(*sources)
    ffn0 = ffn_chunk(dw1, dw2)
    sources = line.step(*sources)
    sources, dqkv, dwo = backward_attn(0, sources)
    sources = line.close(*sources)
    att0 = attn_chunk(dqkv, dwo)
    sources = line.step(*sources)
    grad_x = sources[0] + sources[1] + sources[2].astype(F32)
    grad_low = grad_x.astype(BF16)
    table_parts = table_grads(index, grad_low, at.swap(grad_low), chips * table_rows)
    table_parts = line.close(*table_parts)
    tab = table_chunk(table_parts)
    line.step(extra=grad_x[cap:].astype(BF16) if tiled else None)
    line.close()
    input_grad = from_chip(grad_x, line.extra if tiled else send_back(grad_x))
    zeros = jnp.zeros((2, HALF), F32)
    vectors = []
    for layer in range(LAYERS):
        mine = small_grads[layer][3][:2]
        vectors.append(by_core(core, mine, zeros, 1).reshape(2, D))
    vectors.append(jnp.stack([small_grads[layer][0][2] for layer in range(LAYERS)]))
    for row in range(2):
        for layer in range(LAYERS):
            vectors.append(jnp.stack([small_grads[layer][norm][row] for norm in range(2)]))
    vectors.append(jnp.stack([small_grads[layer][1][2] for layer in range(LAYERS)]))
    vectors = lax.optimization_barrier(jnp.concatenate(vectors)).reshape(SMALL_ROWS, devices, rows_dev).swapaxes(0, 1)
    ups_grad = jnp.stack([small_grads[layer][2][0] for layer in range(LAYERS)])
    ups_grad = ups_grad.reshape(LAYERS, 2, chips, ff_dev // 2).transpose(2, 0, 1, 3)
    ups_grad = by_core(core, ups_grad, jnp.zeros_like(ups_grad), 1)
    segments = jnp.concatenate(
        [vectors.reshape(devices, cut), ups_grad.reshape(devices, LAYERS * ff_dev)], axis=1
    )
    segments = lax.all_to_all(segments, ("page", "band"), 0, 0, tiled=True)


    def small_outputs(segments):
        segment = jnp.sum(segments, axis=0)
        rows = segment[:cut].reshape(SMALL_ROWS, rows_dev)
        return (
            rows[ROW_ATTN:ROW_OUT].reshape(LAYERS, 2, rows_dev),
            rows[ROW_OUT:ROW_GAIN],
            rows[ROW_GAIN:ROW_SHIFT].reshape(LAYERS, 2, rows_dev),
            rows[ROW_SHIFT:ROW_DOWN].reshape(LAYERS, 2, rows_dev),
            segment[cut:].reshape(LAYERS, ff_dev),
            rows[ROW_DOWN:SMALL_ROWS],
        )

    grads = None
    while line.busy():
        line.step()
        if tiled and grads is None and att0[0].total is not None:
            results = [
                [stream.total for stream in attn[:2] + ffn] for attn, ffn in ((att0, ffn0), (att1, ffn1))
            ]
            parts = []
            for qk, vo, up_a, down_a, up_b, down_b in results:
                mine, send = split(core_id, (qk, vo, up_a, up_b))
                parts += [mine, at.swap(send), down_a, down_b]
            grads = merge(core_id, parts)
            smalls = small_outputs(tie(segments, grads[0]))
            grads, smalls = line.close(grads, smalls)
        else:
            line.close()
    if not tiled:
        smalls = small_outputs(segments)
    if tiled:
        grad_tables = tab.total.reshape(4, table_rows, D)
    else:
        sums = [line.result(chunk) for chunk in (att0, ffn0, att1, ffn1)]
        grad_tables = jnp.stack(line.result(tab)).reshape(4, table_rows, D)
        results = []
        for attn_sum, ffn_sum in ((sums[0], sums[1]), (sums[2], sums[3])):
            attn = jnp.stack(attn_sum)
            ffn = jnp.stack(ffn_sum).reshape(4, chip_rows, D)
            results.append((attn, ffn, ffn))

    if not tiled:
        grads = [[], [], [], []]
        for layer in range(LAYERS):
            attn_sum, up_sum, down_sum = results[layer]
            both = jnp.stack([attn_sum[0], attn_sum[1], up_sum[0], up_sum[2]])
            by_owner = both.reshape(4, CORES, rows_dev, D)
            mine, theirs = pick(by_owner, core, 1), at.swap(pick(by_owner, 1 - core, 1))
            both = by_core(core, mine, theirs, 0).transpose(2, 0, 1, 3)
            attn = both[:, :, :2].reshape(rows_dev, CORES, 4, HALF).swapaxes(1, 2)
            grads[0].append(attn[:, :3].reshape(rows_dev, 3 * D))
            grads[1].append(attn[:, 3].reshape(rows_dev, D))
            ups = both[:, :, 2:].reshape(rows_dev, CORES, 2, chips, ff_dev // 2).transpose(0, 3, 1, 2, 4)
            grads[2].append(ups.reshape(rows_dev, FF))
            grads[3].append(jnp.concatenate([down_sum[1], down_sum[3]]))
        grads = [jnp.stack(pair) for pair in grads]

    return (
        output,
        input_grad,
        grad_tables,
        grads[0],
        smalls[0],
        grads[1],
        smalls[1],
        smalls[2],
        smalls[3],
        grads[2],
        smalls[4],
        grads[3],
        smalls[5],
    )


def solution(mesh):
    both = ("page", "band")
    tokens = P("page", "band", None, None)
    middle = P(None, both, None)
    last = P(None, both)
    third = P(None, None, both)
    return jax.shard_map(
        functools.partial(body, pages=mesh.shape["page"], bands=mesh.shape["band"]),
        mesh=mesh,
        in_specs=(
            tokens,
            P(None, "page", "band", None),
            P(None, "page"),
            P("page", "band"),
            middle,
            middle,
            third,
            middle,
            last,
            third,
            third,
            middle,
            last,
            middle,
            last,
            tokens,
        ),
        out_specs=(
            tokens,
            tokens,
            middle,
            middle,
            third,
            middle,
            last,
            third,
            third,
            middle,
            last,
            middle,
            last,
        ),
        check_vma=False,
    )
```

```python
import functools

import jax
import jax.numpy as jnp
from jax import lax
from jax.experimental import pallas as pl
from jax.experimental.pallas import tpu as pltpu
from jax.sharding import PartitionSpec as P

D = 768
HEADS = 12
HEAD_DIM = 64
HALF = D // 2
PAIRS = HEADS // 4
FF = 3072
POS = 1024
GRID = 1000
LAYERS = 2
CORES = 2
LANES = 128
EPS = 1e-12
DEAD = -1000000000.0
SCALE = HEAD_DIM ** (-0.5)
VMEM = 52 * 1024 * 1024
F32 = jnp.float32
BF16 = jnp.bfloat16

ROW_ATTN, ROW_OUT, ROW_GAIN, ROW_SHIFT, ROW_DOWN = 0, 4, 6, 10, 14
SMALL_ROWS = 16


def dot(a, b, dims=((1,), (0,))):
    return lax.dot_general(a, b, (dims, ((), ())), preferred_element_type=F32)


def halves(core):
    first = core[0] * HALF
    return pl.ds(pl.multiple_of(first, LANES), HALF), pl.ds(pl.multiple_of(HALF - first, LANES), HALF)


NT = ((1,), (1,))
TN = ((0,), (0,))


def sds(shape, dtype):
    return jax.ShapeDtypeStruct(shape, dtype)


def whole(shape):
    return pl.BlockSpec(shape, lambda *_: (0,) * len(shape))


def cost(flops, nbytes, trans=0):
    return pl.CostEstimate(flops=flops, bytes_accessed=nbytes, transcendentals=trans)


def params():
    return pltpu.CompilerParams(vmem_limit_bytes=VMEM)


def embed_kernel(idx, t0, t1, t2, t3, out):
    rows = t0.shape[0]
    place = lax.broadcasted_iota(jnp.int32, (idx.shape[0], rows), 1)

    def hot(*cols):
        total = None
        for col in cols:
            one = jnp.where(place == idx[:, col : col + 1], 1.0, 0.0)
            total = one if total is None else total + one
        return total.astype(BF16)

    out[...] = (
        dot(hot(0, 2), t0[...])
        + dot(hot(1, 3), t1[...])
        + dot(hot(4), t2[...])
        + dot(hot(5), t3[...])
    )


def embed(idx, tables):
    tokens = idx.shape[0]
    block = 128
    rows = tables[0].shape[0]
    return pl.pallas_call(
        embed_kernel,
        name="embed",
        out_shape=sds((tokens, D), F32),
        grid=(tokens // block,),
        in_specs=[pl.BlockSpec((block, 8), lambda i: (i, 0))] + [whole((rows, D))] * 4,
        out_specs=pl.BlockSpec((block, D), lambda i: (i, 0)),
        compiler_params=params(),
        cost_estimate=cost(8 * tokens * rows * D, 8 * rows * D + 4 * tokens * D),
    )(idx, *tables)


def table_kernel(idx, own, sib, o0, o1, o2, o3):
    half = own.shape[0]
    block = o0.shape[0]
    first = pl.program_id(0) * block
    place = lax.broadcasted_iota(jnp.int32, (block, 2 * half), 0) + first

    def hot(*rows):
        total = None
        for row in rows:
            one = jnp.where(place == idx[row : row + 1, :], 1.0, 0.0)
            total = one if total is None else total + one
        return total.astype(BF16)

    for out, rows in ((o0, (0, 2)), (o1, (1, 3)), (o2, (4,)), (o3, (5,))):
        mark = hot(*rows)
        out[...] = (dot(mark[:, :half], own[...]) + dot(mark[:, half:], sib[...])).astype(BF16)


def table_grads(idx, own, sib, rows):
    half = own.shape[0]
    block = 256
    return pl.pallas_call(
        table_kernel,
        name="table_grads",
        out_shape=[sds((rows, D), BF16)] * 4,
        grid=(rows // block,),
        in_specs=[whole((8, 2 * half)), whole((half, D)), whole((half, D))],
        out_specs=[pl.BlockSpec((block, D), lambda i: (i, 0))] * 4,
        compiler_params=params(),
        cost_estimate=cost(16 * half * rows * D, 8 * rows * D),
    )(idx, own, sib)


def attn_fwd_kernel(core, xo, xs, wq, wk, wv, small, mask, q, k, v, mo, ms, *, layer):
    half = xo.shape[0]
    joined = jnp.concatenate([wq[...], wk[...], wv[...]], axis=1)
    row = ROW_ATTN + 2 * layer
    for first, rows in ((0, xo), (half, xs)):
        span = slice(first, first + half)
        qkv = dot(rows[...], joined)
        q[span, :] = (qkv[:, :LANES] + small[row : row + 1, :]).astype(BF16)
        k[span, :] = qkv[:, LANES : 2 * LANES].astype(BF16)
        v[span, :] = (qkv[:, 2 * LANES :] + small[row + 1 : row + 2, :]).astype(BF16)
    keys, values = k[...], v[...]
    low_lanes = lax.broadcasted_iota(jnp.int32, (1, LANES), 1) < HEAD_DIM
    for first, out in ((0, mo), (half, ms)):
        queries = q[first : first + half, :].astype(F32) * SCALE
        parts = []
        for head in range(2):
            lanes = low_lanes if head == 0 else jnp.logical_not(low_lanes)
            one = jnp.where(lanes, queries, 0.0).astype(BF16)
            scores = dot(one, keys, NT) + mask[...]
            expo = jnp.exp(scores - jnp.max(scores, axis=-1, keepdims=True))
            total = jnp.sum(expo, axis=-1, keepdims=True)
            parts.append(dot(expo.astype(BF16), values) / total)
        out[...] = jnp.where(low_lanes, parts[0], parts[1]).astype(BF16)


def weight_block(part):
    return pl.BlockSpec((D, LANES), lambda p, core: (0, part * PAIRS + p))


def attn_fwd(core, xo, xs, wa, small, mask, layer):
    half = xo.shape[0]
    tokens = 2 * half
    col = lambda p, core: (0, p)
    rows = pl.BlockSpec((tokens, LANES), col)
    return pl.pallas_call(
        functools.partial(attn_fwd_kernel, layer=layer),
        name="attn_fwd",
        out_shape=[sds((tokens, HALF), BF16)] * 3 + [sds((half, HALF), BF16)] * 2,
        grid_spec=pltpu.PrefetchScalarGridSpec(
            num_scalar_prefetch=1,
            grid=(PAIRS,),
            in_specs=[
                whole((half, D)),
                whole((half, D)),
                weight_block(0),
                weight_block(1),
                weight_block(2),
                pl.BlockSpec((SMALL_ROWS, LANES), lambda p, core: (0, core[0] * PAIRS + p)),
                whole((1, tokens)),
            ],
            out_specs=[rows] * 3 + [pl.BlockSpec((half, LANES), col)] * 2,
        ),
        compiler_params=params(),
        cost_estimate=cost(
            2 * tokens * D * 3 * HALF + 4 * PAIRS * 2 * tokens * tokens * LANES,
            2 * (tokens * D + 3 * D * HALF + 4 * tokens * HALF),
            PAIRS * 2 * tokens * tokens,
        ),
    )(core, xo, xs, wa, wa, wa, small, mask)


def attn_bwd_kernel(
    core, dao, das, wom, wot, q, k, v, mo, ms, xo, xs, wq, wk, wv, mask,
    dwq, dwk, dwv, dwo, dwo_sent, sums, dxo, dxs, acc, all_s, turned,
):
    half = xo.shape[0]
    step = pl.program_id(0)
    mine_cols, their_cols = halves(core)
    dq_s, dk_s, dv_s = [all_s.at[:, part * LANES : (part + 1) * LANES] for part in range(3)]

    @pl.when(step == 0)
    def _():
        turned[:, :half] = xo[...].T
        turned[:, half:] = xs[...].T

    keys, values = k[...], v[...]
    low_lanes = lax.broadcasted_iota(jnp.int32, (1, LANES), 1) < HEAD_DIM
    grad_keys = [None, None]
    grad_values = [None, None]
    for part, da in ((0, dao), (1, das)):
        first = part * half
        span = slice(first, first + half)
        grad_mix = dot(da[:, mine_cols], wom[...], NT) + dot(da[:, their_cols], wot[...], NT)
        queries = q[span, :].astype(F32) * SCALE
        grad_queries = []
        for head in range(2):
            lanes = low_lanes if head == 0 else jnp.logical_not(low_lanes)
            one = jnp.where(lanes, queries, 0.0).astype(BF16)
            scores = dot(one, keys, NT) + mask[...]
            expo = jnp.exp(scores - jnp.max(scores, axis=-1, keepdims=True))
            probs = expo * (1.0 / jnp.sum(expo, axis=-1, keepdims=True))
            grad_one = jnp.where(lanes, grad_mix, 0.0).astype(BF16)
            grad_probs = dot(grad_one, values, NT)
            weighted = probs * grad_probs
            delta = jnp.sum(weighted, axis=-1, keepdims=True)
            grad_scores = (weighted - probs * delta).astype(BF16)
            grad_queries.append(dot(grad_scores, keys))
            key_part = dot(grad_scores, one, TN)
            value_part = dot(probs.astype(BF16), grad_one, TN)
            if part == 0:
                grad_keys[head], grad_values[head] = key_part, value_part
            else:
                grad_keys[head] = grad_keys[head] + key_part
                grad_values[head] = grad_values[head] + value_part
        dq_s[span, :] = (jnp.where(low_lanes, grad_queries[0], grad_queries[1]) * SCALE).astype(BF16)
    dk_s[...] = (grad_keys[0] + grad_keys[1]).astype(BF16)
    dv_s[...] = (grad_values[0] + grad_values[1]).astype(BF16)
    sums[...] = jnp.zeros_like(sums)
    sums[0:1, :] = jnp.sum(dq_s[...].astype(F32), axis=0, keepdims=True)
    sums[1:2, :] = jnp.sum(dv_s[...].astype(F32), axis=0, keepdims=True)
    weight_grads = dot(turned[...], all_s[...]).astype(BF16)
    for part, out in enumerate((dwq, dwk, dwv)):
        out[...] = weight_grads[:, part * LANES : (part + 1) * LANES]
    out_rows = dot(mo[...], dao[...], TN) + dot(ms[...], das[...], TN)
    even = core[0] == 0
    dwo[...] = jnp.where(even, out_rows[:, :HALF], out_rows[:, HALF:]).astype(BF16)
    dwo_sent[...] = jnp.where(even, out_rows[:, HALF:], out_rows[:, :HALF]).astype(BF16)
    total = dot(all_s[...], jnp.concatenate([wq[...], wk[...], wv[...]], axis=1), NT)

    @pl.when(step == 0)
    def _():
        acc[...] = total

    @pl.when(step > 0)
    def _():
        acc[...] += total

    @pl.when(step == PAIRS - 1)
    def _():
        dxo[...] = acc[:half, :]
        dxs[...] = acc[half:, :].astype(BF16)


def attn_bwd(core, dao, das, wom, wot, q, k, v, mo, ms, xo, xs, wa, mask):
    half = xo.shape[0]
    tokens = 2 * half
    col = lambda p, core: (0, p)
    weight = pl.BlockSpec((D, LANES), col)
    rows = pl.BlockSpec((tokens, LANES), col)
    part = pl.BlockSpec((half, LANES), col)
    out_rows = pl.BlockSpec((LANES, HALF), lambda p, core: (core[0] * PAIRS + p, 0))
    return pl.pallas_call(
        attn_bwd_kernel,
        name="attn_bwd",
        out_shape=[sds((D, HALF), BF16)] * 3
        + [
            sds((HALF, HALF), BF16),
            sds((HALF, HALF), BF16),
            sds((8, HALF), F32),
            sds((half, D), F32),
            sds((half, D), BF16),
        ],
        grid_spec=pltpu.PrefetchScalarGridSpec(
            num_scalar_prefetch=1,
            grid=(PAIRS,),
            in_specs=[
                whole((half, D)),
                whole((half, D)),
                out_rows,
                out_rows,
                rows,
                rows,
                rows,
                part,
                part,
                whole((half, D)),
                whole((half, D)),
                weight_block(0),
                weight_block(1),
                weight_block(2),
                whole((1, tokens)),
            ],
            out_specs=[weight] * 3
            + [
                pl.BlockSpec((LANES, HALF), lambda p, core: (p, 0)),
                pl.BlockSpec((LANES, HALF), lambda p, core: (p, 0)),
                pl.BlockSpec((8, LANES), col),
                whole((half, D)),
                whole((half, D)),
            ],
            scratch_shapes=[
                pltpu.VMEM((tokens, D), F32),
                pltpu.VMEM((tokens, 3 * LANES), BF16),
                pltpu.VMEM((D, tokens), BF16),
            ],
        ),
        compiler_params=params(),
        cost_estimate=cost(
            8 * tokens * D * 3 * HALF // 2 + 10 * PAIRS * 2 * tokens * tokens * LANES,
            2 * (4 * tokens * D + 8 * D * HALF + 4 * tokens * HALF),
            PAIRS * 2 * tokens * tokens,
        ),
    )(core, dao, das, wom, wot, q, k, v, mo, ms, xo, xs, wa, wa, wa, mask)


def norm_rows(h, gain, shift, y, yb, n, rstd):
    mean = jnp.mean(h, axis=-1, keepdims=True)
    centred = h - mean
    scale = lax.rsqrt(jnp.mean(centred * centred, axis=-1, keepdims=True) + EPS)
    normal = centred * scale
    out = normal * gain + shift
    y[...] = out
    yb[...] = out.astype(BF16)
    n[...] = normal
    rstd[...] = scale


def norm_outs(half):
    return [sds((half, D), F32), sds((half, D), BF16), sds((half, D), F32), sds((half, 1), F32)]


def out_norm_kernel(core, mine, theirs, wom, wot, base, small, y, yb, n, rstd, *, layer):
    mine_rows, their_rows = halves(core)
    near = dot(mine[...], wom[mine_rows, :]) + dot(theirs[...], wom[their_rows, :])
    far = dot(mine[...], wot[mine_rows, :]) + dot(theirs[...], wot[their_rows, :])
    first = core[0] == 0
    mixed = jnp.concatenate([jnp.where(first, near, far), jnp.where(first, far, near)], axis=1)
    h = base[...] + mixed + small[ROW_OUT + layer : ROW_OUT + layer + 1, :]
    row = 2 * layer
    norm_rows(
        h, small[ROW_GAIN + row : ROW_GAIN + row + 1, :], small[ROW_SHIFT + row : ROW_SHIFT + row + 1, :],
        y, yb, n, rstd,
    )


def out_norm(core, mine, theirs, wom, wot, base, small, layer):
    half = base.shape[0]
    return pl.pallas_call(
        functools.partial(out_norm_kernel, layer=layer),
        name="out_norm",
        out_shape=norm_outs(half),
        in_specs=[pl.BlockSpec(memory_space=pltpu.SMEM)] + [pl.BlockSpec(memory_space=pltpu.VMEM)] * 6,
        out_specs=[pl.BlockSpec(memory_space=pltpu.VMEM)] * 4,
        compiler_params=params(),
        cost_estimate=cost(2 * half * D * D, 2 * D * D + 16 * half * D),
    )(core, mine, theirs, wom, wot, base, small)


def add_norm_kernel(base, part, recv, small, y, yb, n, rstd, *, layer):
    h = base[...] + part[...] + recv[...].astype(F32) + small[ROW_DOWN + layer : ROW_DOWN + layer + 1, :]
    row = 2 * layer + 1
    norm_rows(
        h, small[ROW_GAIN + row : ROW_GAIN + row + 1, :], small[ROW_SHIFT + row : ROW_SHIFT + row + 1, :],
        y, yb, n, rstd,
    )


def add_norm(base, part, recv, small, layer):
    half = base.shape[0]
    return pl.pallas_call(
        functools.partial(add_norm_kernel, layer=layer),
        name="add_norm",
        out_shape=norm_outs(half),
        in_specs=[pl.BlockSpec(memory_space=pltpu.VMEM)] * 4,
        out_specs=[pl.BlockSpec(memory_space=pltpu.VMEM)] * 4,
        compiler_params=params(),
        cost_estimate=cost(20 * half * D, 20 * half * D),
    )(base, part, recv, small)


def norm_bwd_kernel(*refs, row, summed):
    if summed:
        base, part, recv, n, rstd, small, gh, ghb, sums = refs
        gz = base[...] + part[...] + recv[...].astype(F32)
    else:
        base, live, n, rstd, small, gh, ghb, sums = refs
        gz = base[...].astype(F32) * live[...]
    normal = n[...]
    e = gz * small[ROW_GAIN + row : ROW_GAIN + row + 1, :]
    mean = jnp.mean(e, axis=-1, keepdims=True)
    slope = jnp.mean(e * normal, axis=-1, keepdims=True)
    grad = (e - mean - normal * slope) * rstd[...]
    low = grad.astype(BF16)
    gh[...] = grad
    ghb[...] = low
    sums[...] = jnp.zeros_like(sums)
    sums[0:1, :] = jnp.sum(gz * normal, axis=0, keepdims=True)
    sums[1:2, :] = jnp.sum(gz, axis=0, keepdims=True)
    sums[2:3, :] = jnp.sum(low.astype(F32), axis=0, keepdims=True)


def norm_bwd(sources, n, rstd, small, row):
    half = n.shape[0]
    operands = tuple(sources) + (n, rstd, small)
    return pl.pallas_call(
        functools.partial(norm_bwd_kernel, row=row, summed=len(sources) == 3),
        name="norm_bwd",
        out_shape=[sds((half, D), F32), sds((half, D), BF16), sds((8, D), F32)],
        in_specs=[pl.BlockSpec(memory_space=pltpu.VMEM)] * len(operands),
        out_specs=[pl.BlockSpec(memory_space=pltpu.VMEM)] * 3,
        compiler_params=params(),
        cost_estimate=cost(20 * half * D, 20 * half * D),
    )(*operands)


FF_BLOCK = 768
FF_STEPS = FF // CORES // FF_BLOCK


def ffn_fwd_kernel(yo, ys, w1, bias, w2, act, slope, po, ps, acc, *, layer):
    half = yo.shape[0]
    j = pl.program_id(0)
    for first, rows in ((0, yo), (half, ys)):
        span = slice(first, first + half)
        up = dot(rows[...], w1[...]) + bias[layer : layer + 1, :]
        cdf = 0.5 * (1.0 + lax.erf(up * (2.0**-0.5)))
        low = (up * cdf).astype(BF16)
        act[span, :] = low
        slope[span, :] = (cdf + up * (jnp.exp(-0.5 * up * up) * 0.3989422804014327)).astype(BF16)
        total = dot(low, w2[...])

        @pl.when(j == 0)
        def _():
            acc[span, :] = total

        @pl.when(j > 0)
        def _():
            acc[span, :] += total

    @pl.when(j == FF_STEPS - 1)
    def _():
        po[...] = acc[:half, :]
        ps[...] = acc[half:, :].astype(BF16)


DOWN_STEPS = D // FF_BLOCK


def ffn_specs(tokens, col):
    return (
        pl.BlockSpec((D, FF_BLOCK), lambda j: (0, j)),
        pl.BlockSpec((FF_BLOCK, D), lambda j: (j % DOWN_STEPS, col // D + j // DOWN_STEPS)),
        pl.BlockSpec((tokens, FF_BLOCK), lambda j: (0, j)),
    )


def ffn_fwd(yo, ys, w1, w2, col, bias, layer):
    half = yo.shape[0]
    tokens = 2 * half
    width = FF // CORES
    cols, down, rows = ffn_specs(tokens, col)
    return pl.pallas_call(
        functools.partial(ffn_fwd_kernel, layer=layer),
        name="ffn_fwd",
        out_shape=[sds((tokens, width), BF16)] * 2 + [sds((half, D), F32), sds((half, D), BF16)],
        grid=(FF_STEPS,),
        in_specs=[
            whole((half, D)),
            whole((half, D)),
            cols,
            pl.BlockSpec((LAYERS, FF_BLOCK), lambda j: (0, j)),
            down,
        ],
        out_specs=[rows] * 2 + [whole((half, D))] * 2,
        scratch_shapes=[pltpu.VMEM((tokens, D), F32)],
        compiler_params=params(),
        cost_estimate=cost(4 * tokens * D * width, 4 * D * width + 4 * tokens * width, tokens * width),
    )(yo, ys, w1, bias, w2)


def ffn_bwd_kernel(dfo, dfs, w1, w2, act, slope, yo, ys, dw1, dw2, sums, po, ps, acc, du, turned):
    half = yo.shape[0]
    j = pl.program_id(0)

    @pl.when(j == 0)
    def _():
        turned[:, :half] = yo[...].T
        turned[:, half:] = ys[...].T

    for first, rows in ((0, dfo), (half, dfs)):
        span = slice(first, first + half)
        low = (slope[span, :].astype(F32) * dot(rows[...], w2[...], NT)).astype(BF16)
        du[span, :] = low
        total = dot(low, w1[...], NT)

        @pl.when(j == 0)
        def _():
            acc[span, :] = total

        @pl.when(j > 0)
        def _():
            acc[span, :] += total

    sums[...] = jnp.zeros_like(sums)
    sums[0:1, :] = jnp.sum(du[...].astype(F32), axis=0, keepdims=True)
    dw1[...] = dot(turned[...], du[...]).astype(BF16)
    dw2[...] = (dot(act[:half, :], dfo[...], TN) + dot(act[half:, :], dfs[...], TN)).astype(BF16)

    @pl.when(j == FF_STEPS - 1)
    def _():
        po[...] = acc[:half, :]
        ps[...] = acc[half:, :].astype(BF16)


def ffn_bwd(dfo, dfs, w1, w2, col, act, slope, yo, ys):
    half = yo.shape[0]
    tokens = 2 * half
    width = FF // CORES
    cols, down, rows = ffn_specs(tokens, col)
    return pl.pallas_call(
        ffn_bwd_kernel,
        name="ffn_bwd",
        out_shape=[
            sds((2, D, D), BF16),
            sds((2, D, D), BF16),
            sds((8, width), F32),
            sds((half, D), F32),
            sds((half, D), BF16),
        ],
        grid=(FF_STEPS,),
        in_specs=[whole((half, D))] * 2 + [cols, down, rows, rows] + [whole((half, D))] * 2,
        out_specs=[
            pl.BlockSpec((None, D, FF_BLOCK), lambda j: (j // DOWN_STEPS, 0, j % DOWN_STEPS)),
            pl.BlockSpec((None, FF_BLOCK, D), lambda j: (j // DOWN_STEPS, j % DOWN_STEPS, 0)),
            pl.BlockSpec((8, FF_BLOCK), lambda j: (0, j)),
        ]
        + [whole((half, D))] * 2,
        scratch_shapes=[
            pltpu.VMEM((tokens, D), F32),
            pltpu.VMEM((tokens, FF_BLOCK), BF16),
            pltpu.VMEM((D, tokens), BF16),
        ],
        compiler_params=params(),
        cost_estimate=cost(8 * tokens * D * width, 8 * D * width + 4 * tokens * width),
    )(dfo, dfs, w1, w2, act, slope, yo, ys)


def shuffle_kernel(table, *refs, moves, count):
    for out, to, to_col, source, at, at_col, width in moves:
        to = table[to[0]] if isinstance(to, list) else to
        at = table[at[0]] if isinstance(at, list) else at
        refs[count + out][to, :, to_col : to_col + width] = refs[source][at, :, at_col : at_col + width]


def shuffle(table, sources, shapes, moves):
    nbytes = sum(4 * source.size for source in sources)
    return pl.pallas_call(
        functools.partial(shuffle_kernel, moves=moves, count=len(sources)),
        name="shuffle",
        out_shape=shapes,
        in_specs=[pl.BlockSpec(memory_space=pltpu.SMEM)]
        + [pl.BlockSpec(memory_space=pltpu.VMEM)] * len(sources),
        out_specs=[pl.BlockSpec(memory_space=pltpu.VMEM)] * len(shapes),
        compiler_params=params(),
        cost_estimate=cost(0, nbytes),
    )(table, *sources)


def pack_kernel(core, qkv, out, up, mine, send):
    chips = FF // (2 * CORES * FF_CHUNK)
    ups = up[0].astype(F32)
    parts = []
    for parity in range(CORES):
        starts = [
            ((chip * CORES + parity) * 2 + part) * FF_CHUNK for part in range(2) for chip in range(chips)
        ]
        parts.append(jnp.concatenate([ups[:, start : start + FF_CHUNK] for start in starts], axis=1))
    even = core[0] == 0
    for ref, cols, ff in (
        (mine, halves(core)[0], jnp.where(even, parts[0], parts[1])),
        (send, halves(core)[1], jnp.where(even, parts[1], parts[0])),
    ):
        for part in range(3):
            whole_part = qkv.at[0, :, part * D : (part + 1) * D]
            ref[:, part * HALF : (part + 1) * HALF] = whole_part[:, cols]
        ref[:, 3 * HALF : 4 * HALF] = out.at[0][:, cols]
        ref[:, 4 * HALF :] = ff.astype(BF16)


FF_CHUNK = 48
PACKED = 4 * HALF + FF // CORES


def layer_block(shape, layer):
    return pl.BlockSpec((1,) + shape, lambda *_: (layer, 0, 0))


def pack(core, attn_in, attn_out, ffn_in, layer):
    rows = attn_in.shape[1]
    return pl.pallas_call(
        pack_kernel,
        name="pack",
        out_shape=[sds((rows, PACKED), BF16)] * 2,
        grid=(1,),
        in_specs=[
            pl.BlockSpec(memory_space=pltpu.SMEM),
            layer_block((rows, 3 * D), layer),
            layer_block((rows, D), layer),
            layer_block((rows, FF), layer),
        ],
        out_specs=[whole((rows, PACKED))] * 2,
        compiler_params=params(),
        cost_estimate=cost(0, 8 * rows * PACKED),
    )(core, attn_in, attn_out, ffn_in)


def join_kernel(core, mine, recv, down, *outs):
    rows = mine.shape[0]
    even = core[0] == 0
    near, far = mine[...].astype(F32), recv[...].astype(F32)
    both = jnp.concatenate([jnp.where(even, near, far), jnp.where(even, far, near)], axis=0).astype(BF16)
    downs = [down[0, part * CORES * rows : (part + 1) * CORES * rows, :] for part in range(2)]
    attn, ffn = outs
    for unit in range(2):
        attn[unit] = both[:, unit * D : (unit + 1) * D]
        ffn[2 * unit] = both[:, (2 + unit) * D : (3 + unit) * D]
        ffn[2 * unit + 1] = downs[unit]


def join(core, mine, recv, ffn_out, layer, shapes):
    rows = mine.shape[0]
    down = ffn_out.shape[1]
    return pl.pallas_call(
        join_kernel,
        name="join",
        out_shape=[sds(shape, BF16) for shape in shapes],
        grid=(1,),
        in_specs=[
            pl.BlockSpec(memory_space=pltpu.SMEM),
            whole((rows, PACKED)),
            whole((rows, PACKED)),
            layer_block((down, D), layer),
        ],
        out_specs=[whole(shape) for shape in shapes],
        compiler_params=params(),
        cost_estimate=cost(0, 8 * rows * PACKED),
    )(core, mine, recv, ffn_out)


def split_kernel(core, *refs):
    mine, send = refs[-2:]
    rows = mine.shape[0]
    even = core[0] == 0
    for part, block in enumerate(refs[:-2]):
        top, bottom = block[:rows, :], block[rows:, :]
        mine[:, part * D : (part + 1) * D] = jnp.where(even, top, bottom)
        send[:, part * D : (part + 1) * D] = jnp.where(even, bottom, top)


def split(core, units):
    rows = units[0].shape[0] // CORES
    return pl.pallas_call(
        split_kernel,
        name="split",
        out_shape=[sds((rows, PACKED), F32)] * 2,
        in_specs=[pl.BlockSpec(memory_space=pltpu.SMEM)] + [pl.BlockSpec(memory_space=pltpu.VMEM)] * len(units),
        out_specs=[pl.BlockSpec(memory_space=pltpu.VMEM)] * 2,
        compiler_params=params(),
        cost_estimate=cost(0, 16 * rows * PACKED),
    )(core, *units)


def merge_kernel(core, *refs):
    qkv, out, up, down = refs[4 * LAYERS :]
    chips = FF // (2 * CORES * FF_CHUNK)
    even = core[0] == 0
    for layer in range(LAYERS):
        mine, recv, first_down, second_down = refs[4 * layer : 4 * layer + 4]
        near, far = mine[...], recv[...]
        first, second = jnp.where(even, near, far), jnp.where(even, far, near)
        for part in range(3):
            span = slice(part * HALF, (part + 1) * HALF)
            qkv[layer, :, part * D : part * D + HALF] = first[:, span]
            qkv[layer, :, part * D + HALF : (part + 1) * D] = second[:, span]
        out[layer, :, :HALF] = first[:, 3 * HALF : 4 * HALF]
        out[layer, :, HALF:] = second[:, 3 * HALF : 4 * HALF]
        chunks = []
        for chip in range(chips):
            for source in (first, second):
                for part in range(2):
                    start = 4 * HALF + part * D + chip * FF_CHUNK
                    chunks.append(source[:, start : start + FF_CHUNK])
        up[layer] = jnp.concatenate(chunks, axis=1)
        rows = first_down.shape[0]
        down[layer, :rows, :] = first_down[...]
        down[layer, rows:, :] = second_down[...]


def merge(core, parts):
    rows = parts[0].shape[0]
    down = 2 * parts[2].shape[0]
    return pl.pallas_call(
        merge_kernel,
        name="merge",
        out_shape=[
            sds((LAYERS, rows, 3 * D), F32),
            sds((LAYERS, rows, D), F32),
            sds((LAYERS, rows, FF), F32),
            sds((LAYERS, down, D), F32),
        ],
        in_specs=[pl.BlockSpec(memory_space=pltpu.SMEM)] + [pl.BlockSpec(memory_space=pltpu.VMEM)] * len(parts),
        out_specs=[pl.BlockSpec(memory_space=pltpu.VMEM)] * 4,
        compiler_params=params(),
        cost_estimate=cost(0, 32 * rows * PACKED),
    )(core, *parts)


class Places:
    def __init__(self, pages, bands):
        self.ny = bands // CORES
        self.nx = self.ny if pages % self.ny == 0 else 1
        self.nz = pages // self.nx
        self.chips = pages * self.ny
        page, band = lax.axis_index("page"), lax.axis_index("band")
        self.z, self.x = page // self.nx, page % self.nx
        self.y, self.core = band // CORES, band % CORES
        self.sizes = (self.nz, self.nx, self.ny, CORES)

    def move(self, value, axis, step, flip=False):
        pairs = []
        nz, nx, ny, nc = self.sizes
        for device in range(nz * nx * ny * nc):
            place = [device // (nx * ny * nc), device // (ny * nc) % nx, device // nc % ny, device % nc]
            place[axis] = place[axis] ^ step if flip else (place[axis] + step) % self.sizes[axis]
            pairs.append((device, ((place[0] * nx + place[1]) * ny + place[2]) * nc + place[3]))
        return lax.ppermute(value, ("page", "band"), pairs)

    def exchange(self, wants):
        keys = []
        for axis, step, _ in wants:
            key = (axis, step if axis == 0 else step % self.sizes[axis])
            keys.append(key)
        got = [None] * len(wants)
        for key in dict.fromkeys(keys):
            numbers = [i for i, other in enumerate(keys) if other == key]
            flat = [wants[i][2].reshape(-1, wants[i][2].shape[-1]) for i in numbers]
            moved = self.move(jnp.concatenate(flat) if len(flat) > 1 else flat[0], *key, flip=key[0] == 0)
            first = 0
            for i, part in zip(numbers, flat):
                got[i] = moved[first : first + part.shape[0]].reshape(wants[i][2].shape)
                first += part.shape[0]
        return got

    def swap(self, value):
        return self.move(value, 3, 1)

    def chip_of(self, kz, kx, ky):
        z, x, y = self.z ^ kz, (self.x - kx) % self.nx, (self.y - ky) % self.ny
        return (z * self.nx + x) * self.ny + y

    def flips(self):
        return [1 << bit for bit in reversed(range(self.nz.bit_length() - 1))]


def tie(values, *others):
    return lax.optimization_barrier((values, others))[0]


class Gather:
    def __init__(self, at, local, shapes, place):
        self.at, self.local = at, local
        self.half = local.shape[0] // 2
        self.shapes, self.place = shapes, place
        self.stages = [functools.partial(self.flip, step) for step in at.flips()]
        self.stages += [self.first, self.second]
        self.held = local[None]
        self.spots = [0]

    def flip(self, step, got):
        if got:
            self.held = jnp.concatenate([self.held] + list(got))
        self.spots = self.spots + [spot ^ step for spot in self.spots]
        return [(0, step, self.held)]

    def near(self, axis, part):
        return [(axis, k, part) for k in range(1, self.at.sizes[axis])]

    def first(self, got):
        held = jnp.concatenate([self.held] + list(got))
        self.sent = [held[:, : self.half], held[:, self.half :]]
        return self.near(1, self.sent[0]) + self.near(2, self.sent[1])

    def second(self, got):
        cut = self.at.nx - 1
        self.sent = [jnp.stack([part] + got) for part, got in zip(self.sent, (got[:cut], got[cut:]))]
        return self.near(2, self.sent[0]) + self.near(1, self.sent[1])

    def finish(self, got):
        at = self.at
        rows, cols = self.local.shape[1:]
        sources, moves, table = [], [], []
        cut = at.ny - 1
        for axes, part, other, start in (
            ((1, 2), self.sent[0], got[:cut], 0),
            ((2, 1), self.sent[1], got[cut:], self.half),
        ):
            for far, piece in enumerate([part] + list(other)):
                number = 0
                for near in range(at.sizes[axes[0]]):
                    kx, ky = (near, far) if axes[0] == 1 else (far, near)
                    for kz in self.spots:
                        chip = at.chip_of(kz, kx, ky)
                        for unit in range(start, start + self.half):
                            for out, step, offset, to_col, at_col, width in self.place[unit]:
                                moves.append(
                                    (out, [len(table)], to_col, len(sources), number, at_col, width)
                                )
                                table.append(chip * step + offset)
                            number += 1
                sources.append(piece.reshape((-1, rows, cols)))
        outs = shuffle(jnp.stack(table), sources, [sds(shape, BF16) for shape in self.shapes], moves)
        return [out.reshape(-1, out.shape[-1]) for out in outs]


class LateGather(Gather):
    def __init__(self, at, local, shapes, place, idle):
        self.at, self.local = at, local
        self.half = local.shape[0] // 2
        self.shapes, self.place = shapes, place
        self.stages = [self.first, self.second] + [self.rest] * idle
        self.stages += [functools.partial(self.flip, step) for step in at.flips()]
        self.spots = [0]
        self.got = None

    def first(self, got):
        self.sent = [self.local[None, : self.half], self.local[None, self.half :]]
        return self.near(1, self.sent[0]) + self.near(2, self.sent[1])

    def rest(self, got):
        if got:
            self.got = got
        return []

    def flip(self, step, got):
        if self.got is not None:
            got = self.got
        if len(self.spots) == 1:
            cut = self.at.ny - 1
            self.held = jnp.concatenate(
                [jnp.stack([part] + list(other)).reshape((-1,) + part.shape[-3:])
                 for part, other in zip(self.sent, (got[:cut], got[cut:]))],
                axis=1,
            )[None]
        else:
            self.held = jnp.concatenate([self.held] + list(got))
        self.got = None
        self.spots = self.spots + [spot ^ step for spot in self.spots]
        return [(0, step, self.held)]

    def finish(self, got):
        at = self.at
        rows, cols = self.local.shape[1:]
        sources, moves, table = [], [], []
        spots = len(self.spots) // 2
        for number, piece in enumerate([self.held] + list(got)):
            at_block = 0
            for spot in self.spots[number * spots : (number + 1) * spots]:
                for far in range(at.nx):
                    for near in range(at.ny):
                        for unit in range(2 * self.half):
                            kx, ky = (near, far) if unit < self.half else (far, near)
                            for out, step, offset, to_col, at_col, width in self.place[unit]:
                                moves.append((out, [len(table)], to_col, number, at_block, at_col, width))
                                table.append(at.chip_of(spot, kx, ky) * step + offset)
                            at_block += 1
            sources.append(piece.reshape((-1, rows, cols)))
        outs = shuffle(jnp.stack(table), sources, [sds(shape, BF16) for shape in self.shapes], moves)
        return [out.reshape(-1, out.shape[-1]) for out in outs]


class Reduce:
    def __init__(self, at, first, second):
        self.at, self.halves = at, (first, second)
        self.stages = [self.first, self.second]
        self.stages += [functools.partial(self.flip, number) for number in range(len(at.flips()))]

    def picked(self, groups, axis, index):
        at = self.at
        rows = []
        for group in groups:
            parts = []
            for part in group:
                blocks = part.reshape(at.nz, at.nx, at.ny, part.shape[0] // at.chips, part.shape[1])
                parts.append(pick(blocks, index, axis))
            rows.append(jnp.concatenate(parts, axis=-1) if len(parts) > 1 else parts[0])
        return jnp.concatenate(rows, axis=2) if len(rows) > 1 else rows[0]

    def first(self, got):
        at = self.at
        wants = [(2, -k, self.picked(self.halves[0], 2, (at.y - k) % at.ny)) for k in range(1, at.ny)]
        return wants + [
            (1, -k, self.picked(self.halves[1], 1, (at.x - k) % at.nx)) for k in range(1, at.nx)
        ]

    def second(self, got):
        at = self.at
        cut = at.ny - 1
        self.lows = []
        for mine, other in (
            (self.picked(self.halves[0], 2, at.y), got[:cut]),
            (self.picked(self.halves[1], 1, at.x), got[cut:]),
        ):
            self.lows.append(self.total(mine, other).astype(BF16))
        wants = [(1, -k, pick(self.lows[0], (at.x - k) % at.nx, 1)) for k in range(1, at.nx)]
        return wants + [(2, -k, pick(self.lows[1], (at.y - k) % at.ny, 1)) for k in range(1, at.ny)]

    def total(self, mine, other):
        mine = mine.astype(F32)
        for term in other:
            mine = mine + term.astype(F32)
        return mine

    def flip(self, number, got):
        at = self.at
        bit = 1 << number
        if number == 0:
            cut = at.nx - 1
            first = self.total(pick(self.lows[0], at.x, 1), got[:cut])
            second = self.total(pick(self.lows[1], at.y, 1), got[cut:])
            self.cut = first.shape[1]
            low = jnp.concatenate([first, second], axis=1).astype(BF16)
        else:
            low = self.total(self.low, got).astype(BF16)
        low = low.reshape((low.shape[0] // 2, 2) + low.shape[1:])
        side = at.z // bit % 2
        self.low = pick(low, side, 1)
        return [(0, bit, pick(low, 1 - side, 1))]

    def finish(self, got):
        total = self.total(self.low, got)[0]
        return total[: self.cut], total[self.cut :]


class Line:
    def __init__(self, at):
        self.at, self.chunks, self.age, self.got = at, [], [], []

    def add(self, chunk):
        self.chunks.append(chunk)
        self.age.append(0)
        self.got.append([])

    def step(self, *others, extra=None):
        wants, spans = [], []
        for number, chunk in enumerate(self.chunks):
            if self.age[number] < len(chunk.stages):
                new = chunk.stages[self.age[number]](self.got[number])
                spans.append((number, len(wants), len(wants) + len(new)))
                wants += new
                self.age[number] += 1
        values, others = lax.optimization_barrier(([want[2] for want in wants], others))
        wants = [want[:2] + (value,) for want, value in zip(wants, values)]
        self.spans, self.moved = spans, self.at.exchange(wants)
        return others

    def close(self, *others):
        self.moved, others = lax.optimization_barrier((self.moved, others))
        for number, start, stop in self.spans:
            self.got[number] = self.moved[start:stop]
        return others

    def busy(self):
        return not all(self.done(chunk) for chunk in self.chunks)

    def done(self, chunk):
        number = self.chunks.index(chunk)
        return self.age[number] == len(chunk.stages)

    def fresh(self, chunk):
        return self.done(chunk) and any(span[0] == self.chunks.index(chunk) for span in self.spans)

    def result(self, chunk):
        return chunk.finish(self.got[self.chunks.index(chunk)])


def blocks_kernel(scalars, *refs, counts, loads, jobs):
    sources, outs = refs[: counts[0]], refs[counts[0] : counts[0] + counts[1]]
    buffers = refs[counts[0] + counts[1] : -2]
    load_sems, out_sems = refs[-2:]

    def rows(place, height):
        start, slopes = place
        for number, slope in slopes:
            start = start + scalars[number] * slope
        return pl.ds(pl.multiple_of(start, 16) if slopes else start, height)

    copies = []
    for number, (source, place, height, buffer, row, col, width) in enumerate(loads):
        copies.append(
            pltpu.make_async_copy(
                sources[source].at[rows(place, height), :],
                buffers[buffer].at[row : row + height, col : col + width],
                load_sems.at[number],
            )
        )
    for copy in copies:
        copy.start()
    waited = set()

    def wait(numbers):
        for number in numbers:
            if number not in waited:
                waited.add(number)
                copies[number].wait()

    stores = []
    for out, (needs, sums) in enumerate(jobs):
        for to, height, terms in sums:
            total = None
            for buffer, place, numbers in terms:
                wait(numbers)
                value = buffers[buffer][rows(place, height), :].astype(buffers[out].dtype)
                total = value if total is None else total + value
            buffers[out][to : to + height, :] = total.astype(buffers[out].dtype)
        wait(needs)
        stores.append(pltpu.make_async_copy(buffers[out], outs[out], out_sems.at[out]))
        stores[-1].start()
    for store in stores:
        store.wait()


class Stream:
    def __init__(self, parts, first_y, rows, base=0, direct=False):
        self.parts, self.first_y, self.rows, self.base = parts, first_y, rows, base
        self.age, self.direct, self.last = 0, direct, False
        self.keep = self.recv = self.total = self.joined = None


class Joined:
    def __init__(self, streams):
        self.streams, self.out, self.total = streams, None, None
        self.rows = sum(stream.rows for stream in streams)
        for stream in streams:
            stream.joined = self

    def start(self, stream):
        return sum(other.rows for other in self.streams[: self.streams.index(stream)])


class Pipe:
    def __init__(self, at):
        self.at, self.groups = at, []
        self.bits = at.nz.bit_length() - 1
        scalars = [at.x, at.y] + [at.z // (1 << bit) % 2 for bit in range(self.bits)]
        self.scalars = jnp.stack(scalars).astype(jnp.int32)

    def add(self, streams):
        self.groups.append(streams)

    def pieces(self, stream, rows):
        nz = self.at.nz
        first = 1 if stream.first_y else 0
        strides = (2, 1)

        def chip(z, coords):
            start, slopes = stream.base + 4 * z * rows, []
            for axis, (fixed, slope) in enumerate(coords):
                start += fixed * strides[axis] * rows
                if slope:
                    slopes.append((axis, slope * strides[axis] * rows))
            return start, slopes

        def spot(fixed, number, slope, scale, base=0):
            return (base + fixed * scale, [(number, slope * scale)])

        other, same = (1, -1), (0, 1)
        sent, kept = [], []
        if stream.age == 0:
            for z in range(nz):
                for far in range(2):
                    coords = [None, None]
                    coords[first], coords[1 - first] = other, (far, 0)
                    sent.append([(stream.parts, chip(z, coords))])
        elif stream.age == 1:
            ((ref, base),) = stream.recv
            for out, side in ((sent, other), (kept, same)):
                for z in range(nz):
                    coords = [None, None]
                    coords[first], coords[1 - first] = same, side
                    place = spot(2 * z + side[0], 1 - first, side[1], rows, base)
                    out.append([(stream.parts, chip(z, coords)), ([ref], place)])
        elif stream.direct and stream.age == 2:
            ((ref, base),) = stream.recv
            for flip in range(nz):
                start, slopes = 0, []
                for bit in range(self.bits):
                    fixed, slope = other if flip >> bit & 1 else same
                    start += (fixed << bit) * rows
                    slopes.append((2 + bit, (slope << bit) * rows))
                out = sent if flip else kept
                out.append([([stream.keep], (start, slopes)), ([ref], (base + start, slopes))])
        elif not self.final(stream):
            bit = stream.age - 2
            ((ref, base),) = stream.recv
            for out, side in ((sent, other), (kept, same)):
                for high in range(nz >> (bit + 1)):
                    fixed = 2 * high + side[0]
                    keep = spot(fixed, 2 + bit, side[1], rows)
                    out.append([([stream.keep], keep), ([ref], spot(fixed, 2 + bit, side[1], rows, base))])
        else:
            kept.append([([stream.keep], (0, []))] + [([ref], (base, [])) for ref, base in stream.recv])
        return sent, kept

    def final(self, stream):
        return stream.age == (3 if stream.direct else 2 + self.bits)

    def step(self, *others, extra=None):
        heights, keeps, todo, self.sent = {}, [], [], []
        spots, self.joined = [], None
        for streams in self.groups:
            for stream in streams:
                if stream.last:
                    continue
                rows = stream.rows
                sent, kept = self.pieces(stream, rows)
                axis = (2, 1) if stream.first_y else (1, 2)
                blocks, spans = [], []
                if stream.age < 2:
                    spans = [(axis[stream.age], len(sent))]
                elif sent:
                    spans = [(-flip, 1) for flip in range(1, len(sent) + 1)]
                    if not stream.direct:
                        spans = [(-(1 << (stream.age - 2)), len(sent))]
                for key, many in spans:
                    start = heights.get(key, 0)
                    heights[key] = start + many * rows
                    self.sent.append((stream, key, start))
                    blocks += [(key, start + block * rows) for block in range(many)]
                todo.append((stream, blocks, sent, kept, rows))
        if extra is not None:
            span = (heights.get(2, 0), extra.shape[0])
            heights[2] = sum(span)
        order = list(heights)
        shapes = [sds((heights[key], D), BF16) for key in order]
        jobs = [([], []) for _ in order]
        arrays, loads, buffers, held = [], [], [], {}

        def source(array):
            for i, known in enumerate(arrays):
                if known is array:
                    return i
            arrays.append(array)
            return len(arrays) - 1

        for stream, blocks, sent, kept, rows in todo:
            if kept:
                last = self.final(stream)
                if last and stream.joined is not None:
                    if stream.joined.out is None:
                        stream.joined.out = len(shapes)
                        shapes.append(sds((stream.joined.rows, D), F32))
                        jobs.append(([], []))
                        self.joined = stream.joined
                    spots.append((stream.joined.out, stream.joined.start(stream)))
                    continue
                keeps.append((stream, len(shapes)))
                spots.append((len(shapes), 0))
                shapes.append(sds((len(kept) * rows, D), F32 if last else BF16))
                jobs.append(([], []))
        buffers = list(shapes)
        if extra is not None:
            jobs[order.index(2)][0].append(len(loads))
            loads.append((source(extra), (0, []), span[1], order.index(2), span[0], 0, D))
        spare = len(buffers)
        buffers.append(None)
        spare_rows = 0

        def term(parts, place, height):
            nonlocal spare_rows
            if len(parts) == 1 and not any(part is parts[0] for part in stream.parts):
                array = source(parts[0])
                if array not in held:
                    held[array] = (len(buffers), len(loads))
                    loads.append((array, (0, []), parts[0].shape[0], len(buffers), 0, 0, D))
                    buffers.append(sds(parts[0].shape, parts[0].dtype))
                return held[array][0], place, [held[array][1]]
            row, numbers = spare_rows, []
            spare_rows += height
            for number, part in enumerate(parts):
                width = D // len(parts)
                numbers.append(len(loads))
                loads.append((source(part), place, height, spare, row, number * width, width))
            return spare, (row, []), numbers

        for stream, blocks, sent, kept, rows in todo:
            for (key, to), terms in zip(blocks, sent):
                out = order.index(key)
                if len(terms) == 1:
                    ((parts, place),) = terms
                    for number, part in enumerate(parts):
                        width = D // len(parts)
                        jobs[out][0].append(len(loads))
                        loads.append((source(part), place, rows, out, to, number * width, width))
                else:
                    jobs[out][1].append((to, rows, [term(parts, place, rows) for parts, place in terms]))
        spots = iter(spots)
        for stream, blocks, sent, kept, rows in todo:
            if kept:
                out, first = next(spots)
                for block, terms in enumerate(kept):
                    terms = [term(parts, place, rows) for parts, place in terms]
                    jobs[out][1].append((first + block * rows, rows, terms))
        buffers[spare] = sds((max(spare_rows, 16), D), BF16)
        outs = pl.pallas_call(
            functools.partial(
                blocks_kernel, counts=(len(arrays), len(shapes)), loads=loads, jobs=jobs
            ),
            name="blocks",
            out_shape=shapes,
            in_specs=[pl.BlockSpec(memory_space=pltpu.SMEM)]
            + [pl.BlockSpec(memory_space=pltpu.HBM)] * len(arrays),
            out_specs=[pl.BlockSpec(memory_space=pltpu.HBM)] * len(shapes),
            scratch_shapes=[pltpu.VMEM(buffer.shape, buffer.dtype) for buffer in buffers]
            + [pltpu.SemaphoreType.DMA((len(loads),)), pltpu.SemaphoreType.DMA((len(shapes),))],
            compiler_params=params(),
            cost_estimate=cost(0, sum(3 * array.size for array in arrays)),
        )(self.scalars, *arrays)
        if self.joined is not None:
            self.joined.total = outs[self.joined.out]
        for stream, out in keeps:
            stream.keep = outs[out]
            if self.final(stream):
                stream.total = outs[out]
        for stream, *_ in todo:
            stream.last = self.final(stream)
            stream.age += 1
        payloads, others = lax.optimization_barrier((outs[: len(order)], others))
        self.moved = {}
        self.span = None if extra is None else span
        for key, payload in zip(order, payloads):
            if key > 0:
                self.moved[key] = self.at.move(payload, key, 1)
            else:
                self.moved[key] = self.at.move(payload, 0, -key, flip=True)
        return others

    def close(self, *others):
        self.moved, others = lax.optimization_barrier((self.moved, others))
        for stream, key, start in self.sent:
            stream.recv = []
        for stream, key, start in self.sent:
            stream.recv.append((self.moved[key], start))
        if self.span is not None:
            self.extra = [self.moved[2][self.span[0] : sum(self.span)]]
        return others

    def busy(self):
        return not all(stream.last for streams in self.groups for stream in streams)


def pick(stacked, index, axis=0):
    return lax.dynamic_index_in_dim(stacked, index, axis, keepdims=False)


def by_core(core, mine, theirs, axis):
    return jnp.where(core == 0, jnp.stack([mine, theirs], axis), jnp.stack([theirs, mine], axis))


def body(
    hidden,
    boxes,
    page_size,
    band_count,
    layout_tables,
    attn_in,
    attn_bias,
    attn_out,
    out_bias,
    norm_gain,
    norm_bias,
    ffn_in,
    ffn_in_bias,
    ffn_out,
    ffn_out_bias,
    out_grad,
    *,
    pages,
    bands,
):
    at = Places(pages, bands)
    core = at.core
    core_id = core.astype(jnp.int32).reshape(1)
    devices = pages * bands
    ny, chips = at.ny, at.chips
    cap = hidden.shape[2]
    rows_dev = attn_in.shape[1]
    table_rows = layout_tables.shape[1]
    ff_dev = ffn_out.shape[1]
    chip_rows = CORES * rows_dev
    tiled = rows_dev % 8 == 0 and ff_dev == 2 * FF_CHUNK and at.nx == ny == 2

    def local_weights(layer):
        if tiled:
            mine, send = pack(core_id, attn_in, attn_out, ffn_in, layer)
            shapes = ((2, chip_rows, D), (4, chip_rows, D))
            return join(core_id, mine, at.swap(send), ffn_out, layer, shapes)
        columns = jnp.concatenate(
            [attn_in[layer].reshape(rows_dev, 3, CORES, HALF), attn_out[layer].reshape(rows_dev, 1, CORES, HALF)],
            axis=1,
        ).transpose(2, 0, 1, 3)
        ups = ffn_in[layer].reshape(rows_dev, chips, CORES, 2, ff_dev // 2).transpose(2, 0, 3, 1, 4)
        packed = jnp.concatenate(
            [columns.reshape(CORES, rows_dev, 4 * HALF), ups.reshape(CORES, rows_dev, FF // CORES)], axis=2
        )
        both = by_core(core, pick(packed, core), at.swap(pick(packed, 1 - core)), 0)
        both = both.reshape(chip_rows, PACKED)
        down = ffn_out[layer].reshape(2, chip_rows, D)
        both = both.reshape(chip_rows, 4, D).swapaxes(0, 1)
        return both[:2], jnp.stack([both[2], down[0], both[3], down[1]])

    attn_place = ([(0, 1, 0, 0, 0, D)], [(0, 1, 0, D, 0, D), (1, 1, 0, 0, HALF, HALF)])
    attn_shapes = ((chips, chip_rows, 2 * D), (chips, chip_rows, HALF))
    ffn_place = [[(0, 1, 0, col * D, 0, D)] for col in (0, 2, 1, 3)]
    ffn_shapes = ((chips, chip_rows, 4 * D),)
    table_place = [[(table, 1, 0, 0, 0, D)] for table in range(4)]
    table_shapes = ((chips, table_rows, D),) * 4

    def to_chip(stacked):
        own = [pick(stacked, at.y)]
        for k in range(1, ny):
            own.append(at.move(pick(stacked, (at.y + k) % ny), 2, k))
        return own

    def send_back(rows):
        parts = rows.reshape((ny, cap) + rows.shape[1:])
        return [at.move(parts[k].astype(BF16), 2, -k) for k in range(1, ny)]

    def from_chip(rows, back):
        back = [rows[:cap]] + [part.astype(F32) for part in back]
        back = jnp.stack(back)
        return jnp.stack([pick(back, (page - at.y) % ny) for page in range(ny)])[:, None]

    def token_facts(hidden, out_grad, boxes, page_size, band_count):
        widths, heights = page_size[0][:, None], page_size[1][:, None]
        left = boxes[0, :, 0] * GRID // widths
        top = boxes[1, :, 0] * GRID // heights
        right = boxes[2, :, 0] * GRID // widths
        bottom = boxes[3, :, 0] * GRID // heights
        live = (lax.broadcasted_iota(jnp.int32, left.shape, 1) < band_count).astype(jnp.int32)
        facts = jnp.stack([left, top, right, bottom, bottom - top, right - left, live, live], axis=1)
        facts_own = jnp.concatenate(to_chip(facts), axis=-1)
        facts_all = jnp.concatenate([facts_own, at.swap(facts_own)], axis=-1)
        owner = facts_all // table_rows
        index = jnp.where(
            owner % CORES == core, owner // CORES * table_rows + facts_all % table_rows, -1
        )
        mask = jnp.where(facts_all[6:7] > 0, 0.0, DEAD).astype(F32)
        live_own = facts_own[6].astype(F32)[:, None]
        hidden_own = jnp.concatenate(to_chip(hidden[:, 0]), axis=0)
        grad_own = jnp.concatenate(to_chip(out_grad[:, 0]), axis=0)
        return index, mask, live_own, hidden_own, grad_own

    cut = SMALL_ROWS * rows_dev

    def small_params(attn_bias, out_bias, norm_gain, norm_bias, ffn_out_bias, ffn_in_bias):
        segment = jnp.concatenate(
            [
                attn_bias.reshape(-1),
                out_bias.reshape(-1),
                norm_gain.reshape(-1),
                norm_bias.reshape(-1),
                ffn_out_bias.reshape(-1),
                ffn_in_bias.reshape(-1),
            ]
        )
        smalls = lax.all_to_all(
            jnp.broadcast_to(segment, (devices, segment.shape[0])), ("page", "band"), 0, 0, tiled=True
        ).astype(F32)
        small = smalls[:, :cut].reshape(devices, SMALL_ROWS, rows_dev).swapaxes(0, 1).reshape(SMALL_ROWS, D)
        up_bias = pick(smalls[:, cut:].reshape(chips, CORES, LAYERS, 2, ff_dev // 2), core, 1)
        up_bias = up_bias.transpose(1, 2, 0, 3).reshape(LAYERS, FF // CORES)
        return small, up_bias

    saved = [[], []]
    weights = [[], []]

    def look_up(state):
        tables = line.result(chunks[0])
        looked_up = embed(index.T, tables)
        mine = hidden_own.astype(F32) + looked_up[:half]
        x = mine + at.swap(looked_up[half:].astype(BF16)).astype(F32)
        return x, x.astype(BF16)

    def attend(layer, state):
        x, x_low = state
        wa, wom = line.result(chunks[1 + 2 * layer])
        wot, x_other = at.swap(wom), at.swap(x_low)
        weights[layer] += [wa, wom, wot]
        q, k, v, mix_own, mix_other = attn_fwd(core_id, x_low, x_other, wa, small, mask, layer)
        y1, y1_low, n1, r1 = out_norm(core_id, mix_own, at.swap(mix_other), wom, wot, x, small, layer)
        saved[layer] += [x_low, x_other, q, k, v, mix_own, mix_other, n1, r1]
        return y1, y1_low

    def feed(layer, state):
        y1, y1_low = state
        (w1,) = line.result(chunks[2 + 2 * layer])
        w2, col = (w1, 2 * D) if layer == 0 else (downs[0], 0)
        y1_other = at.swap(y1_low)
        weights[layer] += [w1, w2, col]
        act, slope, part, part_other = ffn_fwd(y1_low, y1_other, w1, w2, col, up_bias, layer)
        x, x_low, n2, r2 = add_norm(y1, part, at.swap(part_other), small, layer)
        saved[layer] += [y1_low, y1_other, act, slope, n2, r2]
        return x, x_low

    half = ny * cap
    line = Line(at)
    chunks = [Gather(at, layout_tables, table_shapes, table_place)]
    parts = [look_up]
    line.add(chunks[0])
    down_chunk = LateGather(
        at,
        ffn_out[LAYERS - 1].reshape(2, chip_rows, D),
        ((chips, chip_rows, 2 * D),),
        ([(0, 1, 0, 0, 0, D)], [(0, 1, 0, D, 0, D)]),
        3,
    )
    line.add(down_chunk)
    line.step()
    locals0 = local_weights(0)
    token_args = (hidden, out_grad, boxes, page_size, band_count)
    small_args = (attn_bias, out_bias, norm_gain, norm_bias, ffn_out_bias, ffn_in_bias)
    locals0, token_args = line.close(locals0, token_args)
    state, downs = (), []
    running = None
    waiting = []
    for layer in range(LAYERS):
        waiting += [(layer, 0), (layer, 1)]
        parts += [functools.partial(attend, layer), functools.partial(feed, layer)]
    local = locals0
    while waiting or running is not None or not line.done(chunks[-1]):
        if waiting:
            layer, number = waiting.pop(0)
            if layer > 0 and number == 0:
                local = local_weights(layer)
            if layer > 0 and number == 1:
                shard = jnp.stack([local[1][0], local[1][2]])
                shapes, place = ((chips, chip_rows, 2 * D),), ([(0, 1, 0, 0, 0, D)], [(0, 1, 0, D, 0, D)])
            else:
                shard = local[number]
                shapes, place = (attn_shapes, ffn_shapes)[number], (attn_place, ffn_place)[number]
            chunks.append(Gather(at, shard, shapes, place))
            line.add(chunks[-1])
        if all(line.done(chunk) for chunk in chunks):
            state = running(state)
            break
        state = line.step(*state)
        if line.done(down_chunk) and not downs and not line.fresh(down_chunk):
            downs.append(line.result(down_chunk)[0])
        if running is not None:
            state = running(state)
        if len(chunks) == 2:
            tokens, small_args, late = line.close(
                token_facts(*token_args), small_args, (attn_in, attn_out, ffn_in)
            )
            index, mask, live_own, hidden_own, grad_own = tokens
            attn_in, attn_out, ffn_in = late
        elif len(chunks) == 3:
            (small_args,) = line.close(small_args)
        elif len(chunks) == 4:
            small, up_bias = line.close(*small_params(*small_args))
        elif downs:
            state, downs = line.close(state, downs)
        else:
            state = line.close(*state)
        ready = [number for number, chunk in enumerate(chunks) if line.fresh(chunk)]
        running = parts[ready[0]] if ready else None
    x = state[0]

    small_grads = [None] * LAYERS

    def backward_ffn(layer, sources):
        w1, w2, col = weights[layer][3:]
        y1_low, y1_other, act, slope, n2, r2 = saved[layer][9:]
        gh2, df, sums2 = norm_bwd(sources, n2, r2, small, 2 * layer + 1)
        dw1, dw2, up_sums, part, part_other = ffn_bwd(df, at.swap(df), w1, w2, col, act, slope, y1_low, y1_other)
        small_grads[layer] = [sums2, up_sums]
        return (gh2, part, at.swap(part_other)), dw1, dw2

    def backward_attn(layer, sources):
        wa, wom, wot = weights[layer][:3]
        x_low, x_other, q, k, v, mix_own, mix_other, n1, r1 = saved[layer][:9]
        gh1, da, sums1 = norm_bwd(sources, n1, r1, small, 2 * layer)
        dwq, dwk, dwv, dwo, dwo_sent, attn_sums, part, part_other = attn_bwd(
            core_id, da, at.swap(da), wom, wot, q, k, v, mix_own, mix_other, x_low, x_other, wa, mask
        )
        small_grads[layer] = [sums1] + small_grads[layer] + [attn_sums]
        return (gh1, part, at.swap(part_other)), (dwq, dwk, dwv), (dwo, at.swap(dwo_sent))

    def attn_groups(dqkv, dwo):
        dwq, dwk, dwv = dqkv
        return [dwq, dwk], [dwv, by_core(core, *dwo, 0).reshape(D, HALF)]

    line = Pipe(at) if tiled else Line(at)

    def ffn_chunk(dw1, dw2):
        if tiled:
            flat = [dw.reshape(2 * D, D) for dw in (dw1, dw2)]
            streams = [Stream([unit], part == 0, chip_rows, part * D) for part in range(2) for unit in flat]
            line.add(streams)
            return streams
        chunk = Reduce(at, [[dw1[0]], [dw2[0]]], [[dw1[1]], [dw2[1]]])
        line.add(chunk)
        return chunk

    def attn_chunk(dqkv, dwo, direct):
        first, second = attn_groups(dqkv, dwo)
        if tiled:
            streams = [
                Stream(part, part is first, chip_rows, direct=direct) for part in (first, second)
            ]
            line.add(streams)
            return streams
        chunk = Reduce(at, [first], [second])
        line.add(chunk)
        return chunk

    def table_chunk(tables):
        if tiled:
            streams = [Stream([table], number < 2, table_rows) for number, table in enumerate(tables)]
            line.add(streams)
            return Joined(streams)
        chunk = Reduce(at, [[table] for table in tables[:2]], [[table] for table in tables[2:]])
        line.add(chunk)
        return chunk

    sources, dw1, dw2 = backward_ffn(1, (grad_own, live_own))
    ffn1 = ffn_chunk(dw1, dw2)
    output = x * live_own
    sources = line.step(*sources, extra=output[cap:].astype(BF16) if tiled else None)
    sources, dqkv, dwo = backward_attn(1, sources)
    sources = line.close(*sources)
    output = from_chip(output, line.extra if tiled else send_back(output))
    att1 = attn_chunk(dqkv, dwo, False)
    sources = line.step(*sources)
    sources, dw1, dw2 = backward_ffn(0, sources)
    sources = line.close(*sources)
    ffn0 = ffn_chunk(dw1, dw2)
    sources = line.step(*sources)
    sources, dqkv, dwo = backward_attn(0, sources)
    sources = line.close(*sources)
    att0 = attn_chunk(dqkv, dwo, False)
    sources = line.step(*sources)
    grad_x = sources[0] + sources[1] + sources[2].astype(F32)
    grad_low = grad_x.astype(BF16)
    table_parts = table_grads(index, grad_low, at.swap(grad_low), chips * table_rows)
    table_parts = line.close(*table_parts)
    tab = table_chunk(table_parts)
    line.step(extra=grad_x[cap:].astype(BF16) if tiled else None)
    line.close()
    input_grad = from_chip(grad_x, line.extra if tiled else send_back(grad_x))
    zeros = jnp.zeros((2, HALF), F32)
    vectors = []
    for layer in range(LAYERS):
        mine = small_grads[layer][3][:2]
        vectors.append(by_core(core, mine, zeros, 1).reshape(2, D))
    vectors.append(jnp.stack([small_grads[layer][0][2] for layer in range(LAYERS)]))
    for row in range(2):
        for layer in range(LAYERS):
            vectors.append(jnp.stack([small_grads[layer][norm][row] for norm in range(2)]))
    vectors.append(jnp.stack([small_grads[layer][1][2] for layer in range(LAYERS)]))
    vectors = lax.optimization_barrier(jnp.concatenate(vectors)).reshape(SMALL_ROWS, devices, rows_dev).swapaxes(0, 1)
    ups_grad = jnp.stack([small_grads[layer][2][0] for layer in range(LAYERS)])
    ups_grad = ups_grad.reshape(LAYERS, 2, chips, ff_dev // 2).transpose(2, 0, 1, 3)
    ups_grad = by_core(core, ups_grad, jnp.zeros_like(ups_grad), 1)
    segments = jnp.concatenate(
        [vectors.reshape(devices, cut), ups_grad.reshape(devices, LAYERS * ff_dev)], axis=1
    )
    segments = lax.all_to_all(segments, ("page", "band"), 0, 0, tiled=True)


    def small_outputs(segments):
        segment = jnp.sum(segments, axis=0)
        rows = segment[:cut].reshape(SMALL_ROWS, rows_dev)
        return (
            rows[ROW_ATTN:ROW_OUT].reshape(LAYERS, 2, rows_dev),
            rows[ROW_OUT:ROW_GAIN],
            rows[ROW_GAIN:ROW_SHIFT].reshape(LAYERS, 2, rows_dev),
            rows[ROW_SHIFT:ROW_DOWN].reshape(LAYERS, 2, rows_dev),
            segment[cut:].reshape(LAYERS, ff_dev),
            rows[ROW_DOWN:SMALL_ROWS],
        )

    grads = None
    while line.busy():
        line.step()
        if tiled and grads is None and att0[0].total is not None:
            results = [
                [stream.total for stream in attn[:2] + ffn] for attn, ffn in ((att0, ffn0), (att1, ffn1))
            ]
            parts = []
            for qk, vo, up_a, down_a, up_b, down_b in results:
                mine, send = split(core_id, (qk, vo, up_a, up_b))
                parts += [mine, at.swap(send), down_a, down_b]
            grads = merge(core_id, parts)
            smalls = small_outputs(tie(segments, grads[0]))
            grads, smalls = line.close(grads, smalls)
        else:
            line.close()
    if not tiled:
        smalls = small_outputs(segments)
    if tiled:
        grad_tables = tab.total.reshape(4, table_rows, D)
    else:
        sums = [line.result(chunk) for chunk in (att0, ffn0, att1, ffn1)]
        grad_tables = jnp.stack(line.result(tab)).reshape(4, table_rows, D)
        results = []
        for attn_sum, ffn_sum in ((sums[0], sums[1]), (sums[2], sums[3])):
            attn = jnp.stack(attn_sum)
            ffn = jnp.stack(ffn_sum).reshape(4, chip_rows, D)
            results.append((attn, ffn, ffn))

    if not tiled:
        grads = [[], [], [], []]
        for layer in range(LAYERS):
            attn_sum, up_sum, down_sum = results[layer]
            both = jnp.stack([attn_sum[0], attn_sum[1], up_sum[0], up_sum[2]])
            by_owner = both.reshape(4, CORES, rows_dev, D)
            mine, theirs = pick(by_owner, core, 1), at.swap(pick(by_owner, 1 - core, 1))
            both = by_core(core, mine, theirs, 0).transpose(2, 0, 1, 3)
            attn = both[:, :, :2].reshape(rows_dev, CORES, 4, HALF).swapaxes(1, 2)
            grads[0].append(attn[:, :3].reshape(rows_dev, 3 * D))
            grads[1].append(attn[:, 3].reshape(rows_dev, D))
            ups = both[:, :, 2:].reshape(rows_dev, CORES, 2, chips, ff_dev // 2).transpose(0, 3, 1, 2, 4)
            grads[2].append(ups.reshape(rows_dev, FF))
            grads[3].append(jnp.concatenate([down_sum[1], down_sum[3]]))
        grads = [jnp.stack(pair) for pair in grads]

    return (
        output,
        input_grad,
        grad_tables,
        grads[0],
        smalls[0],
        grads[1],
        smalls[1],
        smalls[2],
        smalls[3],
        grads[2],
        smalls[4],
        grads[3],
        smalls[5],
    )


def solution(mesh):
    both = ("page", "band")
    tokens = P("page", "band", None, None)
    middle = P(None, both, None)
    last = P(None, both)
    third = P(None, None, both)
    return jax.shard_map(
        functools.partial(body, pages=mesh.shape["page"], bands=mesh.shape["band"]),
        mesh=mesh,
        in_specs=(
            tokens,
            P(None, "page", "band", None),
            P(None, "page"),
            P("page", "band"),
            middle,
            middle,
            third,
            middle,
            last,
            third,
            third,
            middle,
            last,
            middle,
            last,
            tokens,
        ),
        out_specs=(
            tokens,
            tokens,
            middle,
            middle,
            third,
            middle,
            last,
            third,
            third,
            middle,
            last,
            middle,
            last,
        ),
        check_vma=False,
    )
```

```python
import functools
import math

import jax
import jax.numpy as jnp
from jax import lax
from jax.experimental import pallas as pl
from jax.experimental.pallas import tpu as pltpu
from jax.sharding import PartitionSpec as P

D = 768
HEADS = 12
HEAD_DIM = 64
HALF = D // 2
PAIRS = HEADS // 4
FF = 3072
POS = 1024
GRID = 1000
LAYERS = 2
CORES = 2
LANES = 128
EPS = 1e-12
DEAD = -1000000000.0
SCALE = HEAD_DIM ** (-0.5)
VMEM = 52 * 1024 * 1024
F32 = jnp.float32
BF16 = jnp.bfloat16

ROW_ATTN, ROW_OUT, ROW_GAIN, ROW_SHIFT, ROW_DOWN = 0, 4, 6, 10, 14
SMALL_ROWS = 16


def dot(a, b, dims=((1,), (0,))):
    return lax.dot_general(a, b, (dims, ((), ())), preferred_element_type=F32)


def halves(core):
    first = core[0] * HALF
    return pl.ds(pl.multiple_of(first, LANES), HALF), pl.ds(pl.multiple_of(HALF - first, LANES), HALF)


NT = ((1,), (1,))
TN = ((0,), (0,))


def sds(shape, dtype):
    return jax.ShapeDtypeStruct(shape, dtype)


def whole(shape):
    return pl.BlockSpec(shape, lambda *_: (0,) * len(shape))


def cost(flops, nbytes, trans=0):
    return pl.CostEstimate(flops=flops, bytes_accessed=nbytes, transcendentals=trans)


def params():
    return pltpu.CompilerParams(vmem_limit_bytes=VMEM)


def embed_kernel(idx, t0, t1, t2, t3, out):
    rows = t0.shape[0]
    place = lax.broadcasted_iota(jnp.int32, (idx.shape[0], rows), 1)

    def hot(*cols):
        total = None
        for col in cols:
            one = jnp.where(place == idx[:, col : col + 1], 1.0, 0.0)
            total = one if total is None else total + one
        return total.astype(BF16)

    out[...] = (
        dot(hot(0, 2), t0[...])
        + dot(hot(1, 3), t1[...])
        + dot(hot(4), t2[...])
        + dot(hot(5), t3[...])
    )


def embed(idx, tables):
    tokens = idx.shape[0]
    block = 128
    rows = tables[0].shape[0]
    return pl.pallas_call(
        embed_kernel,
        name="embed",
        out_shape=sds((tokens, D), F32),
        grid=(tokens // block,),
        in_specs=[pl.BlockSpec((block, 8), lambda i: (i, 0))] + [whole((rows, D))] * 4,
        out_specs=pl.BlockSpec((block, D), lambda i: (i, 0)),
        compiler_params=params(),
        cost_estimate=cost(8 * tokens * rows * D, 8 * rows * D + 4 * tokens * D),
    )(idx, *tables)


def table_kernel(idx, own, sib, o0, o1, o2, o3):
    half = own.shape[0]
    block = o0.shape[0]
    first = pl.program_id(0) * block
    place = lax.broadcasted_iota(jnp.int32, (block, 2 * half), 0) + first

    def hot(*rows):
        total = None
        for row in rows:
            one = jnp.where(place == idx[row : row + 1, :], 1.0, 0.0)
            total = one if total is None else total + one
        return total.astype(BF16)

    for out, rows in ((o0, (0, 2)), (o1, (1, 3)), (o2, (4,)), (o3, (5,))):
        mark = hot(*rows)
        out[...] = (dot(mark[:, :half], own[...]) + dot(mark[:, half:], sib[...])).astype(BF16)


def table_grads(idx, own, sib, rows):
    half = own.shape[0]
    block = 256
    return pl.pallas_call(
        table_kernel,
        name="table_grads",
        out_shape=[sds((rows, D), BF16)] * 4,
        grid=(rows // block,),
        in_specs=[whole((8, 2 * half)), whole((half, D)), whole((half, D))],
        out_specs=[pl.BlockSpec((block, D), lambda i: (i, 0))] * 4,
        compiler_params=params(),
        cost_estimate=cost(16 * half * rows * D, 8 * rows * D),
    )(idx, own, sib)


def attn_fwd_kernel(core, xo, xs, wq, wk, wv, small, mask, q, k, v, mo, ms, *, layer):
    half = xo.shape[0]
    joined = jnp.concatenate([wq[...], wk[...], wv[...]], axis=1)
    row = ROW_ATTN + 2 * layer
    for first, rows in ((0, xo), (half, xs)):
        span = slice(first, first + half)
        qkv = dot(rows[...], joined)
        q[span, :] = (qkv[:, :LANES] + small[row : row + 1, :]).astype(BF16)
        k[span, :] = qkv[:, LANES : 2 * LANES].astype(BF16)
        v[span, :] = (qkv[:, 2 * LANES :] + small[row + 1 : row + 2, :]).astype(BF16)
    keys, values = k[...], v[...]
    low_lanes = lax.broadcasted_iota(jnp.int32, (1, LANES), 1) < HEAD_DIM
    for first, out in ((0, mo), (half, ms)):
        queries = q[first : first + half, :].astype(F32) * SCALE
        parts = []
        for head in range(2):
            lanes = low_lanes if head == 0 else jnp.logical_not(low_lanes)
            one = jnp.where(lanes, queries, 0.0).astype(BF16)
            scores = dot(one, keys, NT) + mask[...]
            expo = jnp.exp(scores - jnp.max(scores, axis=-1, keepdims=True))
            total = jnp.sum(expo, axis=-1, keepdims=True)
            parts.append(dot(expo.astype(BF16), values) / total)
        out[...] = jnp.where(low_lanes, parts[0], parts[1]).astype(BF16)


def weight_block(part):
    return pl.BlockSpec((D, LANES), lambda p, core: (0, part * PAIRS + p))


def attn_fwd(core, xo, xs, wa, small, mask, layer):
    half = xo.shape[0]
    tokens = 2 * half
    col = lambda p, core: (0, p)
    rows = pl.BlockSpec((tokens, LANES), col)
    return pl.pallas_call(
        functools.partial(attn_fwd_kernel, layer=layer),
        name="attn_fwd",
        out_shape=[sds((tokens, HALF), BF16)] * 3 + [sds((half, HALF), BF16)] * 2,
        grid_spec=pltpu.PrefetchScalarGridSpec(
            num_scalar_prefetch=1,
            grid=(PAIRS,),
            in_specs=[
                whole((half, D)),
                whole((half, D)),
                weight_block(0),
                weight_block(1),
                weight_block(2),
                pl.BlockSpec((SMALL_ROWS, LANES), lambda p, core: (0, core[0] * PAIRS + p)),
                whole((1, tokens)),
            ],
            out_specs=[rows] * 3 + [pl.BlockSpec((half, LANES), col)] * 2,
        ),
        compiler_params=params(),
        cost_estimate=cost(
            2 * tokens * D * 3 * HALF + 4 * PAIRS * 2 * tokens * tokens * LANES,
            2 * (tokens * D + 3 * D * HALF + 4 * tokens * HALF),
            PAIRS * 2 * tokens * tokens,
        ),
    )(core, xo, xs, wa, wa, wa, small, mask)


def attn_bwd_kernel(
    core, dao, das, wom, wot, q, k, v, mo, ms, xo, xs, wq, wk, wv, mask,
    dwq, dwk, dwv, dwo, dwo_sent, sums, dxo, dxs, acc, all_s, turned,
):
    half = xo.shape[0]
    step = pl.program_id(0)
    mine_cols, their_cols = halves(core)
    dq_s, dk_s, dv_s = [all_s.at[:, part * LANES : (part + 1) * LANES] for part in range(3)]

    @pl.when(step == 0)
    def _():
        turned[:, :half] = xo[...].T
        turned[:, half:] = xs[...].T

    keys, values = k[...], v[...]
    low_lanes = lax.broadcasted_iota(jnp.int32, (1, LANES), 1) < HEAD_DIM
    grad_keys = [None, None]
    grad_values = [None, None]
    for part, da in ((0, dao), (1, das)):
        first = part * half
        span = slice(first, first + half)
        grad_mix = dot(da[:, mine_cols], wom[...], NT) + dot(da[:, their_cols], wot[...], NT)
        queries = q[span, :].astype(F32) * SCALE
        grad_queries = []
        for head in range(2):
            lanes = low_lanes if head == 0 else jnp.logical_not(low_lanes)
            one = jnp.where(lanes, queries, 0.0).astype(BF16)
            scores = dot(one, keys, NT) + mask[...]
            expo = jnp.exp(scores - jnp.max(scores, axis=-1, keepdims=True))
            probs = expo * (1.0 / jnp.sum(expo, axis=-1, keepdims=True))
            grad_one = jnp.where(lanes, grad_mix, 0.0).astype(BF16)
            grad_probs = dot(grad_one, values, NT)
            weighted = probs * grad_probs
            delta = jnp.sum(weighted, axis=-1, keepdims=True)
            grad_scores = (weighted - probs * delta).astype(BF16)
            grad_queries.append(dot(grad_scores, keys))
            key_part = dot(grad_scores, one, TN)
            value_part = dot(probs.astype(BF16), grad_one, TN)
            if part == 0:
                grad_keys[head], grad_values[head] = key_part, value_part
            else:
                grad_keys[head] = grad_keys[head] + key_part
                grad_values[head] = grad_values[head] + value_part
        dq_s[span, :] = (jnp.where(low_lanes, grad_queries[0], grad_queries[1]) * SCALE).astype(BF16)
    dk_s[...] = (grad_keys[0] + grad_keys[1]).astype(BF16)
    dv_s[...] = (grad_values[0] + grad_values[1]).astype(BF16)
    sums[...] = jnp.zeros_like(sums)
    sums[0:1, :] = jnp.sum(dq_s[...].astype(F32), axis=0, keepdims=True)
    sums[1:2, :] = jnp.sum(dv_s[...].astype(F32), axis=0, keepdims=True)
    weight_grads = dot(turned[...], all_s[...]).astype(BF16)
    for part, out in enumerate((dwq, dwk, dwv)):
        out[...] = weight_grads[:, part * LANES : (part + 1) * LANES]
    out_rows = dot(mo[...], dao[...], TN) + dot(ms[...], das[...], TN)
    even = core[0] == 0
    dwo[...] = jnp.where(even, out_rows[:, :HALF], out_rows[:, HALF:]).astype(BF16)
    dwo_sent[...] = jnp.where(even, out_rows[:, HALF:], out_rows[:, :HALF]).astype(BF16)
    total = dot(all_s[...], jnp.concatenate([wq[...], wk[...], wv[...]], axis=1), NT)

    @pl.when(step == 0)
    def _():
        acc[...] = total

    @pl.when(step > 0)
    def _():
        acc[...] += total

    @pl.when(step == PAIRS - 1)
    def _():
        dxo[...] = acc[:half, :]
        dxs[...] = acc[half:, :].astype(BF16)


def attn_bwd(core, dao, das, wom, wot, q, k, v, mo, ms, xo, xs, wa, mask):
    half = xo.shape[0]
    tokens = 2 * half
    col = lambda p, core: (0, p)
    weight = pl.BlockSpec((D, LANES), col)
    rows = pl.BlockSpec((tokens, LANES), col)
    part = pl.BlockSpec((half, LANES), col)
    out_rows = pl.BlockSpec((LANES, HALF), lambda p, core: (core[0] * PAIRS + p, 0))
    return pl.pallas_call(
        attn_bwd_kernel,
        name="attn_bwd",
        out_shape=[sds((D, HALF), BF16)] * 3
        + [
            sds((HALF, HALF), BF16),
            sds((HALF, HALF), BF16),
            sds((8, HALF), F32),
            sds((half, D), F32),
            sds((half, D), BF16),
        ],
        grid_spec=pltpu.PrefetchScalarGridSpec(
            num_scalar_prefetch=1,
            grid=(PAIRS,),
            in_specs=[
                whole((half, D)),
                whole((half, D)),
                out_rows,
                out_rows,
                rows,
                rows,
                rows,
                part,
                part,
                whole((half, D)),
                whole((half, D)),
                weight_block(0),
                weight_block(1),
                weight_block(2),
                whole((1, tokens)),
            ],
            out_specs=[weight] * 3
            + [
                pl.BlockSpec((LANES, HALF), lambda p, core: (p, 0)),
                pl.BlockSpec((LANES, HALF), lambda p, core: (p, 0)),
                pl.BlockSpec((8, LANES), col),
                whole((half, D)),
                whole((half, D)),
            ],
            scratch_shapes=[
                pltpu.VMEM((tokens, D), F32),
                pltpu.VMEM((tokens, 3 * LANES), BF16),
                pltpu.VMEM((D, tokens), BF16),
            ],
        ),
        compiler_params=params(),
        cost_estimate=cost(
            8 * tokens * D * 3 * HALF // 2 + 10 * PAIRS * 2 * tokens * tokens * LANES,
            2 * (4 * tokens * D + 8 * D * HALF + 4 * tokens * HALF),
            PAIRS * 2 * tokens * tokens,
        ),
    )(core, dao, das, wom, wot, q, k, v, mo, ms, xo, xs, wa, wa, wa, mask)


def norm_rows(h, gain, shift, y, yb, n, rstd):
    mean = jnp.mean(h, axis=-1, keepdims=True)
    centred = h - mean
    scale = lax.rsqrt(jnp.mean(centred * centred, axis=-1, keepdims=True) + EPS)
    normal = centred * scale
    out = normal * gain + shift
    y[...] = out
    yb[...] = out.astype(BF16)
    n[...] = normal
    rstd[...] = scale


def norm_outs(half):
    return [sds((half, D), F32), sds((half, D), BF16), sds((half, D), F32), sds((half, 1), F32)]


def out_norm_kernel(core, mine, theirs, wom, wot, base, small, y, yb, n, rstd, *, layer):
    mine_rows, their_rows = halves(core)
    near = dot(mine[...], wom[mine_rows, :]) + dot(theirs[...], wom[their_rows, :])
    far = dot(mine[...], wot[mine_rows, :]) + dot(theirs[...], wot[their_rows, :])
    first = core[0] == 0
    mixed = jnp.concatenate([jnp.where(first, near, far), jnp.where(first, far, near)], axis=1)
    h = base[...] + mixed + small[ROW_OUT + layer : ROW_OUT + layer + 1, :]
    row = 2 * layer
    norm_rows(
        h, small[ROW_GAIN + row : ROW_GAIN + row + 1, :], small[ROW_SHIFT + row : ROW_SHIFT + row + 1, :],
        y, yb, n, rstd,
    )


def out_norm(core, mine, theirs, wom, wot, base, small, layer):
    half = base.shape[0]
    return pl.pallas_call(
        functools.partial(out_norm_kernel, layer=layer),
        name="out_norm",
        out_shape=norm_outs(half),
        in_specs=[pl.BlockSpec(memory_space=pltpu.SMEM)] + [pl.BlockSpec(memory_space=pltpu.VMEM)] * 6,
        out_specs=[pl.BlockSpec(memory_space=pltpu.VMEM)] * 4,
        compiler_params=params(),
        cost_estimate=cost(2 * half * D * D, 2 * D * D + 16 * half * D),
    )(core, mine, theirs, wom, wot, base, small)


def add_norm_kernel(base, part, recv, small, y, yb, n, rstd, *, layer):
    h = base[...] + part[...] + recv[...].astype(F32) + small[ROW_DOWN + layer : ROW_DOWN + layer + 1, :]
    row = 2 * layer + 1
    norm_rows(
        h, small[ROW_GAIN + row : ROW_GAIN + row + 1, :], small[ROW_SHIFT + row : ROW_SHIFT + row + 1, :],
        y, yb, n, rstd,
    )


def add_norm(base, part, recv, small, layer):
    half = base.shape[0]
    return pl.pallas_call(
        functools.partial(add_norm_kernel, layer=layer),
        name="add_norm",
        out_shape=norm_outs(half),
        in_specs=[pl.BlockSpec(memory_space=pltpu.VMEM)] * 4,
        out_specs=[pl.BlockSpec(memory_space=pltpu.VMEM)] * 4,
        compiler_params=params(),
        cost_estimate=cost(20 * half * D, 20 * half * D),
    )(base, part, recv, small)


def norm_bwd_kernel(*refs, row, summed):
    if summed:
        base, part, recv, n, rstd, small, gh, ghb, sums = refs
        gz = base[...] + part[...] + recv[...].astype(F32)
    else:
        base, live, n, rstd, small, gh, ghb, sums = refs
        gz = base[...].astype(F32) * live[...]
    normal = n[...]
    e = gz * small[ROW_GAIN + row : ROW_GAIN + row + 1, :]
    mean = jnp.mean(e, axis=-1, keepdims=True)
    slope = jnp.mean(e * normal, axis=-1, keepdims=True)
    grad = (e - mean - normal * slope) * rstd[...]
    low = grad.astype(BF16)
    gh[...] = grad
    ghb[...] = low
    sums[...] = jnp.zeros_like(sums)
    sums[0:1, :] = jnp.sum(gz * normal, axis=0, keepdims=True)
    sums[1:2, :] = jnp.sum(gz, axis=0, keepdims=True)
    sums[2:3, :] = jnp.sum(low.astype(F32), axis=0, keepdims=True)


def norm_bwd(sources, n, rstd, small, row):
    half = n.shape[0]
    operands = tuple(sources) + (n, rstd, small)
    return pl.pallas_call(
        functools.partial(norm_bwd_kernel, row=row, summed=len(sources) == 3),
        name="norm_bwd",
        out_shape=[sds((half, D), F32), sds((half, D), BF16), sds((8, D), F32)],
        in_specs=[pl.BlockSpec(memory_space=pltpu.VMEM)] * len(operands),
        out_specs=[pl.BlockSpec(memory_space=pltpu.VMEM)] * 3,
        compiler_params=params(),
        cost_estimate=cost(20 * half * D, 20 * half * D),
    )(*operands)


FF_BLOCK = 768
FF_STEPS = FF // CORES // FF_BLOCK


def ffn_fwd_kernel(yo, ys, w1, bias, w2, act, slope, po, ps, acc, *, layer):
    half = yo.shape[0]
    j = pl.program_id(0)
    for first, rows in ((0, yo), (half, ys)):
        span = slice(first, first + half)
        up = dot(rows[...], w1[...]) + bias[layer : layer + 1, :]
        cdf = 0.5 * (1.0 + lax.erf(up * (2.0**-0.5)))
        low = (up * cdf).astype(BF16)
        act[span, :] = low
        slope[span, :] = (cdf + up * (jnp.exp(-0.5 * up * up) * 0.3989422804014327)).astype(BF16)
        total = dot(low, w2[...])

        @pl.when(j == 0)
        def _():
            acc[span, :] = total

        @pl.when(j > 0)
        def _():
            acc[span, :] += total

    @pl.when(j == FF_STEPS - 1)
    def _():
        po[...] = acc[:half, :]
        ps[...] = acc[half:, :].astype(BF16)


DOWN_STEPS = D // FF_BLOCK


def ffn_specs(tokens, col):
    return (
        pl.BlockSpec((D, FF_BLOCK), lambda j: (0, j)),
        pl.BlockSpec((FF_BLOCK, D), lambda j: (j % DOWN_STEPS, col // D + j // DOWN_STEPS)),
        pl.BlockSpec((tokens, FF_BLOCK), lambda j: (0, j)),
    )


def ffn_fwd(yo, ys, w1, w2, col, bias, layer):
    half = yo.shape[0]
    tokens = 2 * half
    width = FF // CORES
    cols, down, rows = ffn_specs(tokens, col)
    return pl.pallas_call(
        functools.partial(ffn_fwd_kernel, layer=layer),
        name="ffn_fwd",
        out_shape=[sds((tokens, width), BF16)] * 2 + [sds((half, D), F32), sds((half, D), BF16)],
        grid=(FF_STEPS,),
        in_specs=[
            whole((half, D)),
            whole((half, D)),
            cols,
            pl.BlockSpec((LAYERS, FF_BLOCK), lambda j: (0, j)),
            down,
        ],
        out_specs=[rows] * 2 + [whole((half, D))] * 2,
        scratch_shapes=[pltpu.VMEM((tokens, D), F32)],
        compiler_params=params(),
        cost_estimate=cost(4 * tokens * D * width, 4 * D * width + 4 * tokens * width, tokens * width),
    )(yo, ys, w1, bias, w2)


def ffn_bwd_kernel(dfo, dfs, w1, w2, act, slope, yo, ys, dw1, dw2, sums, po, ps, acc, du, turned):
    half = yo.shape[0]
    j = pl.program_id(0)

    @pl.when(j == 0)
    def _():
        turned[:, :half] = yo[...].T
        turned[:, half:] = ys[...].T

    for first, rows in ((0, dfo), (half, dfs)):
        span = slice(first, first + half)
        low = (slope[span, :].astype(F32) * dot(rows[...], w2[...], NT)).astype(BF16)
        du[span, :] = low
        total = dot(low, w1[...], NT)

        @pl.when(j == 0)
        def _():
            acc[span, :] = total

        @pl.when(j > 0)
        def _():
            acc[span, :] += total

    sums[...] = jnp.zeros_like(sums)
    sums[0:1, :] = jnp.sum(du[...].astype(F32), axis=0, keepdims=True)
    dw1[...] = dot(turned[...], du[...]).astype(BF16)
    dw2[...] = (dot(act[:half, :], dfo[...], TN) + dot(act[half:, :], dfs[...], TN)).astype(BF16)

    @pl.when(j == FF_STEPS - 1)
    def _():
        po[...] = acc[:half, :]
        ps[...] = acc[half:, :].astype(BF16)


def ffn_bwd(dfo, dfs, w1, w2, col, act, slope, yo, ys):
    half = yo.shape[0]
    tokens = 2 * half
    width = FF // CORES
    cols, down, rows = ffn_specs(tokens, col)
    return pl.pallas_call(
        ffn_bwd_kernel,
        name="ffn_bwd",
        out_shape=[
            sds((2, D, D), BF16),
            sds((2, D, D), BF16),
            sds((8, width), F32),
            sds((half, D), F32),
            sds((half, D), BF16),
        ],
        grid=(FF_STEPS,),
        in_specs=[whole((half, D))] * 2 + [cols, down, rows, rows] + [whole((half, D))] * 2,
        out_specs=[
            pl.BlockSpec((None, D, FF_BLOCK), lambda j: (j // DOWN_STEPS, 0, j % DOWN_STEPS)),
            pl.BlockSpec((None, FF_BLOCK, D), lambda j: (j // DOWN_STEPS, j % DOWN_STEPS, 0)),
            pl.BlockSpec((8, FF_BLOCK), lambda j: (0, j)),
        ]
        + [whole((half, D))] * 2,
        scratch_shapes=[
            pltpu.VMEM((tokens, D), F32),
            pltpu.VMEM((tokens, FF_BLOCK), BF16),
            pltpu.VMEM((D, tokens), BF16),
        ],
        compiler_params=params(),
        cost_estimate=cost(8 * tokens * D * width, 8 * D * width + 4 * tokens * width),
    )(dfo, dfs, w1, w2, act, slope, yo, ys)


def shuffle_kernel(table, *refs, moves, count):
    for out, to, to_col, source, at, at_col, width in moves:
        to = table[to[0]] if isinstance(to, list) else to
        at = table[at[0]] if isinstance(at, list) else at
        ref, cols = refs[source], slice(at_col, at_col + width)
        rows = refs[count + out].shape[1]
        block = ref[at : at + rows, cols] if len(ref.shape) == 2 else ref[at, :, cols]
        refs[count + out][to, :, to_col : to_col + width] = block


def shuffle(table, sources, shapes, moves):
    nbytes = sum(4 * source.size for source in sources)
    return pl.pallas_call(
        functools.partial(shuffle_kernel, moves=moves, count=len(sources)),
        name="shuffle",
        out_shape=shapes,
        in_specs=[pl.BlockSpec(memory_space=pltpu.SMEM)]
        + [pl.BlockSpec(memory_space=pltpu.VMEM)] * len(sources),
        out_specs=[pl.BlockSpec(memory_space=pltpu.VMEM)] * len(shapes),
        compiler_params=params(),
        cost_estimate=cost(0, nbytes),
    )(table, *sources)


def pack_kernel(core, qkv, out, up, mine, send):
    chips = FF // (2 * CORES * FF_CHUNK)
    ups = up[0].astype(F32)
    parts = []
    for parity in range(CORES):
        starts = [
            ((chip * CORES + parity) * 2 + part) * FF_CHUNK for part in range(2) for chip in range(chips)
        ]
        parts.append(jnp.concatenate([ups[:, start : start + FF_CHUNK] for start in starts], axis=1))
    even = core[0] == 0
    for ref, cols, ff in (
        (mine, halves(core)[0], jnp.where(even, parts[0], parts[1])),
        (send, halves(core)[1], jnp.where(even, parts[1], parts[0])),
    ):
        for part in range(3):
            whole_part = qkv.at[0, :, part * D : (part + 1) * D]
            ref[:, part * HALF : (part + 1) * HALF] = whole_part[:, cols]
        ref[:, 3 * HALF : 4 * HALF] = out.at[0][:, cols]
        ref[:, 4 * HALF :] = ff.astype(BF16)


FF_CHUNK = 48
PACKED = 4 * HALF + FF // CORES


def layer_block(shape, layer):
    return pl.BlockSpec((1,) + shape, lambda *_: (layer, 0, 0))


def pack(core, attn_in, attn_out, ffn_in, layer):
    rows = attn_in.shape[1]
    return pl.pallas_call(
        pack_kernel,
        name="pack",
        out_shape=[sds((rows, PACKED), BF16)] * 2,
        grid=(1,),
        in_specs=[
            pl.BlockSpec(memory_space=pltpu.SMEM),
            layer_block((rows, 3 * D), layer),
            layer_block((rows, D), layer),
            layer_block((rows, FF), layer),
        ],
        out_specs=[whole((rows, PACKED))] * 2,
        compiler_params=params(),
        cost_estimate=cost(0, 8 * rows * PACKED),
    )(core, attn_in, attn_out, ffn_in)


def join_kernel(core, mine, recv, down, *outs):
    rows = mine.shape[0]
    even = core[0] == 0
    near, far = mine[...].astype(F32), recv[...].astype(F32)
    both = jnp.concatenate([jnp.where(even, near, far), jnp.where(even, far, near)], axis=0).astype(BF16)
    downs = [down[0, part * CORES * rows : (part + 1) * CORES * rows, :] for part in range(2)]
    attn, ffn = outs
    for unit in range(2):
        attn[unit] = both[:, unit * D : (unit + 1) * D]
        ffn[2 * unit] = both[:, (2 + unit) * D : (3 + unit) * D]
        ffn[2 * unit + 1] = downs[unit]


def join(core, mine, recv, ffn_out, layer, shapes):
    rows = mine.shape[0]
    down = ffn_out.shape[1]
    return pl.pallas_call(
        join_kernel,
        name="join",
        out_shape=[sds(shape, BF16) for shape in shapes],
        grid=(1,),
        in_specs=[
            pl.BlockSpec(memory_space=pltpu.SMEM),
            whole((rows, PACKED)),
            whole((rows, PACKED)),
            layer_block((down, D), layer),
        ],
        out_specs=[whole(shape) for shape in shapes],
        compiler_params=params(),
        cost_estimate=cost(0, 8 * rows * PACKED),
    )(core, mine, recv, ffn_out)


def split_kernel(core, *refs):
    mine, send = refs[-2:]
    rows = mine.shape[0]
    even = core[0] == 0
    for part, block in enumerate(refs[:-2]):
        top, bottom = block[:rows, :], block[rows:, :]
        mine[:, part * D : (part + 1) * D] = jnp.where(even, top, bottom)
        send[:, part * D : (part + 1) * D] = jnp.where(even, bottom, top)


def split(core, units):
    rows = units[0].shape[0] // CORES
    return pl.pallas_call(
        split_kernel,
        name="split",
        out_shape=[sds((rows, PACKED), F32)] * 2,
        in_specs=[pl.BlockSpec(memory_space=pltpu.SMEM)] + [pl.BlockSpec(memory_space=pltpu.VMEM)] * len(units),
        out_specs=[pl.BlockSpec(memory_space=pltpu.VMEM)] * 2,
        compiler_params=params(),
        cost_estimate=cost(0, 16 * rows * PACKED),
    )(core, *units)


def merge_kernel(core, *refs):
    qkv, out, up, down = refs[4 * LAYERS :]
    chips = FF // (2 * CORES * FF_CHUNK)
    even = core[0] == 0
    for layer in range(LAYERS):
        mine, recv, first_down, second_down = refs[4 * layer : 4 * layer + 4]
        near, far = mine[...], recv[...]
        first, second = jnp.where(even, near, far), jnp.where(even, far, near)
        for part in range(3):
            span = slice(part * HALF, (part + 1) * HALF)
            qkv[layer, :, part * D : part * D + HALF] = first[:, span]
            qkv[layer, :, part * D + HALF : (part + 1) * D] = second[:, span]
        out[layer, :, :HALF] = first[:, 3 * HALF : 4 * HALF]
        out[layer, :, HALF:] = second[:, 3 * HALF : 4 * HALF]
        chunks = []
        for chip in range(chips):
            for source in (first, second):
                for part in range(2):
                    start = 4 * HALF + part * D + chip * FF_CHUNK
                    chunks.append(source[:, start : start + FF_CHUNK])
        up[layer] = jnp.concatenate(chunks, axis=1)
        rows = first_down.shape[0]
        down[layer, :rows, :] = first_down[...]
        down[layer, rows:, :] = second_down[...]


def merge(core, parts):
    rows = parts[0].shape[0]
    down = 2 * parts[2].shape[0]
    return pl.pallas_call(
        merge_kernel,
        name="merge",
        out_shape=[
            sds((LAYERS, rows, 3 * D), F32),
            sds((LAYERS, rows, D), F32),
            sds((LAYERS, rows, FF), F32),
            sds((LAYERS, down, D), F32),
        ],
        in_specs=[pl.BlockSpec(memory_space=pltpu.SMEM)] + [pl.BlockSpec(memory_space=pltpu.VMEM)] * len(parts),
        out_specs=[pl.BlockSpec(memory_space=pltpu.VMEM)] * 4,
        compiler_params=params(),
        cost_estimate=cost(0, 32 * rows * PACKED),
    )(core, *parts)


class Places:
    def __init__(self, pages, bands):
        self.ny = bands // CORES
        self.nx = self.ny if pages % self.ny == 0 else 1
        self.nz = pages // self.nx
        self.chips = pages * self.ny
        page, band = lax.axis_index("page"), lax.axis_index("band")
        self.z, self.x = page // self.nx, page % self.nx
        self.y, self.core = band // CORES, band % CORES
        self.sizes = (self.nz, self.nx, self.ny, CORES)

    def move(self, value, axis, step, flip=False):
        pairs = []
        nz, nx, ny, nc = self.sizes
        for device in range(nz * nx * ny * nc):
            place = [device // (nx * ny * nc), device // (ny * nc) % nx, device // nc % ny, device % nc]
            place[axis] = place[axis] ^ step if flip else (place[axis] + step) % self.sizes[axis]
            pairs.append((device, ((place[0] * nx + place[1]) * ny + place[2]) * nc + place[3]))
        return lax.ppermute(value, ("page", "band"), pairs)

    def payloads(self, wants):
        keys = []
        for axis, step, _ in wants:
            keys.append((axis, step if axis == 0 else step % self.sizes[axis]))
        merged, places = {}, [None] * len(wants)
        for key in dict.fromkeys(keys):
            numbers = [i for i, other in enumerate(keys) if other == key]
            flat = [wants[i][2].reshape(-1, wants[i][2].shape[-1]) for i in numbers]
            merged[key] = jnp.concatenate(flat) if len(flat) > 1 else flat[0]
            first = 0
            for i, part in zip(numbers, flat):
                places[i] = (key, first, wants[i][2].shape)
                first += part.shape[0]
        return merged, places

    def swap(self, value):
        return self.move(value, 3, 1)

    def chip_of(self, kz, kx, ky):
        z, x, y = self.z ^ kz, (self.x - kx) % self.nx, (self.y - ky) % self.ny
        return (z * self.nx + x) * self.ny + y

    def flips(self):
        return [1 << bit for bit in reversed(range(self.nz.bit_length() - 1))]


def tie(values, *others):
    return lax.optimization_barrier((values, others))[0]


class Gather:
    def __init__(self, at, local, shapes, place):
        self.at, self.local = at, local
        self.half = local.shape[0] // 2
        self.shapes, self.place = shapes, place
        self.stages = [functools.partial(self.flip, step) for step in at.flips()]
        self.stages += [self.first, self.second]
        self.held = local[None]
        self.spots = [0]

    def flip(self, step, got):
        if got:
            self.held = jnp.concatenate([self.held] + list(got))
        self.spots = self.spots + [spot ^ step for spot in self.spots]
        return [(0, step, self.held)]

    def near(self, axis, part):
        return [(axis, k, part) for k in range(1, self.at.sizes[axis])]

    def first(self, got):
        held = jnp.concatenate([self.held] + list(got))
        self.sent = [held[:, : self.half], held[:, self.half :]]
        return self.near(1, self.sent[0]) + self.near(2, self.sent[1])

    def second(self, got):
        cut = self.at.nx - 1
        self.sent = [jnp.stack([part] + got) for part, got in zip(self.sent, (got[:cut], got[cut:]))]
        return self.near(2, self.sent[0]) + self.near(1, self.sent[1])

    def finish(self, got, mine):
        at = self.at
        rows = self.local.shape[1]
        sources, moves, table = [], [], []
        cut = at.ny - 1
        for axes, pieces, start in (
            ((1, 2), mine[:1] + got[:cut], 0),
            ((2, 1), mine[cut : cut + 1] + got[cut:], self.half),
        ):
            for far, piece in enumerate(pieces):
                source, spot, stride = piece.source(sources, rows)
                for near in range(at.sizes[axes[0]]):
                    kx, ky = (near, far) if axes[0] == 1 else (far, near)
                    for kz in self.spots:
                        chip = at.chip_of(kz, kx, ky)
                        for unit in range(start, start + self.half):
                            for out, step, offset, to_col, at_col, width in self.place[unit]:
                                moves.append((out, [len(table)], to_col, source, spot, at_col, width))
                                table.append(chip * step + offset)
                            spot += stride
        outs = shuffle(jnp.stack(table), sources, [sds(shape, BF16) for shape in self.shapes], moves)
        return [out.reshape(-1, out.shape[-1]) for out in outs]


class LateGather(Gather):
    def __init__(self, at, local, shapes, place, idle):
        self.at, self.local = at, local
        self.half = local.shape[0] // 2
        self.shapes, self.place = shapes, place
        self.stages = [self.first, self.second] + [self.rest] * idle
        self.stages += [functools.partial(self.flip, step) for step in at.flips()]
        self.spots = [0]
        self.got = None

    def first(self, got):
        self.sent = [self.local[None, : self.half], self.local[None, self.half :]]
        return self.near(1, self.sent[0]) + self.near(2, self.sent[1])

    def rest(self, got):
        if got:
            self.got = got
        return []

    def flip(self, step, got):
        if self.got is not None:
            got = self.got
        if len(self.spots) == 1:
            cut = self.at.ny - 1
            self.held = jnp.concatenate(
                [jnp.stack([part] + list(other)).reshape((-1,) + part.shape[-3:])
                 for part, other in zip(self.sent, (got[:cut], got[cut:]))],
                axis=1,
            )[None]
        else:
            self.held = jnp.concatenate([self.held] + list(got))
        self.got = None
        self.spots = self.spots + [spot ^ step for spot in self.spots]
        return [(0, step, self.held)]

    def finish(self, got, mine):
        at = self.at
        rows = self.local.shape[1]
        sources, moves, table = [], [], []
        spots = len(self.spots) // 2
        for number, piece in enumerate((mine[0], got[0])):
            source, block, stride = piece.source(sources, rows)
            for spot in self.spots[number * spots : (number + 1) * spots]:
                for far in range(at.nx):
                    for near in range(at.ny):
                        for unit in range(2 * self.half):
                            kx, ky = (near, far) if unit < self.half else (far, near)
                            for out, step, offset, to_col, at_col, width in self.place[unit]:
                                moves.append((out, [len(table)], to_col, source, block, at_col, width))
                                table.append(at.chip_of(spot, kx, ky) * step + offset)
                            block += stride
        outs = shuffle(jnp.stack(table), sources, [sds(shape, BF16) for shape in self.shapes], moves)
        return [out.reshape(-1, out.shape[-1]) for out in outs]


class Reduce:
    def __init__(self, at, first, second):
        self.at, self.halves = at, (first, second)
        self.stages = [self.first, self.second]
        self.stages += [functools.partial(self.flip, number) for number in range(len(at.flips()))]

    def picked(self, groups, axis, index):
        at = self.at
        rows = []
        for group in groups:
            parts = []
            for part in group:
                blocks = part.reshape(at.nz, at.nx, at.ny, part.shape[0] // at.chips, part.shape[1])
                parts.append(pick(blocks, index, axis))
            rows.append(jnp.concatenate(parts, axis=-1) if len(parts) > 1 else parts[0])
        return jnp.concatenate(rows, axis=2) if len(rows) > 1 else rows[0]

    def first(self, got):
        at = self.at
        wants = [(2, -k, self.picked(self.halves[0], 2, (at.y - k) % at.ny)) for k in range(1, at.ny)]
        return wants + [
            (1, -k, self.picked(self.halves[1], 1, (at.x - k) % at.nx)) for k in range(1, at.nx)
        ]

    def second(self, got):
        at = self.at
        cut = at.ny - 1
        self.lows = []
        for mine, other in (
            (self.picked(self.halves[0], 2, at.y), got[:cut]),
            (self.picked(self.halves[1], 1, at.x), got[cut:]),
        ):
            self.lows.append(self.total(mine, other).astype(BF16))
        wants = [(1, -k, pick(self.lows[0], (at.x - k) % at.nx, 1)) for k in range(1, at.nx)]
        return wants + [(2, -k, pick(self.lows[1], (at.y - k) % at.ny, 1)) for k in range(1, at.ny)]

    def total(self, mine, other):
        mine = mine.astype(F32)
        for term in other:
            mine = mine + term.astype(F32)
        return mine

    def flip(self, number, got):
        at = self.at
        bit = 1 << number
        if number == 0:
            cut = at.nx - 1
            first = self.total(pick(self.lows[0], at.x, 1), got[:cut])
            second = self.total(pick(self.lows[1], at.y, 1), got[cut:])
            self.cut = first.shape[1]
            low = jnp.concatenate([first, second], axis=1).astype(BF16)
        else:
            low = self.total(self.low, got).astype(BF16)
        low = low.reshape((low.shape[0] // 2, 2) + low.shape[1:])
        side = at.z // bit % 2
        self.low = pick(low, side, 1)
        return [(0, bit, pick(low, 1 - side, 1))]

    def finish(self, got):
        total = self.total(self.low, got)[0]
        return total[: self.cut], total[self.cut :]


class Piece:
    def __init__(self, array, first, shape):
        self.array, self.first, self.shape = array, first, shape

    def value(self):
        rows = math.prod(self.shape[:-1])
        return self.array[self.first : self.first + rows].reshape(self.shape)

    def source(self, sources, rows):
        if rows % 16:
            sources.append(self.value().reshape(-1, rows, self.shape[-1]))
            return len(sources) - 1, 0, 1
        for number, array in enumerate(sources):
            if array is self.array:
                return number, self.first, rows
        sources.append(self.array)
        return len(sources) - 1, self.first, rows


class Line:
    def __init__(self, at):
        self.at, self.chunks, self.age, self.got, self.mine = at, [], [], [], []

    def add(self, chunk):
        self.chunks.append(chunk)
        self.age.append(0)
        self.got.append([])
        self.mine.append([])

    def step(self, *others, extra=None):
        wants, spans = [], []
        for number, chunk in enumerate(self.chunks):
            if self.age[number] < len(chunk.stages):
                new = chunk.stages[self.age[number]]([piece.value() for piece in self.got[number]])
                spans.append((number, len(wants), len(wants) + len(new)))
                wants += new
                self.age[number] += 1
        merged, self.places = self.at.payloads(wants)
        values, others = lax.optimization_barrier((list(merged.values()), others))
        merged = dict(zip(merged, values))
        self.moved = {key: self.at.move(value, *key, flip=key[0] == 0) for key, value in merged.items()}
        self.spans = spans
        for number, start, stop in spans:
            self.mine[number] = [Piece(merged[key], *place) for key, *place in self.places[start:stop]]
        return others

    def close(self, *others):
        self.moved, others = lax.optimization_barrier((self.moved, others))
        for number, start, stop in self.spans:
            self.got[number] = [Piece(self.moved[key], *place) for key, *place in self.places[start:stop]]
        return others

    def busy(self):
        return not all(self.done(chunk) for chunk in self.chunks)

    def done(self, chunk):
        number = self.chunks.index(chunk)
        return self.age[number] == len(chunk.stages)

    def fresh(self, chunk):
        return self.done(chunk) and any(span[0] == self.chunks.index(chunk) for span in self.spans)

    def result(self, chunk):
        number = self.chunks.index(chunk)
        if isinstance(chunk, Gather):
            return chunk.finish(self.got[number], self.mine[number])
        return chunk.finish([piece.value() for piece in self.got[number]])


def blocks_kernel(scalars, *refs, counts, loads, jobs):
    sources, outs = refs[: counts[0]], refs[counts[0] : counts[0] + counts[1]]
    buffers = refs[counts[0] + counts[1] : -2]
    load_sems, out_sems = refs[-2:]

    def rows(place, height):
        start, slopes = place
        for number, slope in slopes:
            start = start + scalars[number] * slope
        return pl.ds(pl.multiple_of(start, 16) if slopes else start, height)

    copies = []
    for number, (source, place, height, buffer, row, col, width) in enumerate(loads):
        copies.append(
            pltpu.make_async_copy(
                sources[source].at[rows(place, height), :],
                buffers[buffer].at[row : row + height, col : col + width],
                load_sems.at[number],
            )
        )
    for copy in copies:
        copy.start()
    waited = set()

    def wait(numbers):
        for number in numbers:
            if number not in waited:
                waited.add(number)
                copies[number].wait()

    stores = []
    for out, (needs, sums) in enumerate(jobs):
        for to, height, terms in sums:
            total = None
            for buffer, place, numbers in terms:
                wait(numbers)
                value = buffers[buffer][rows(place, height), :].astype(buffers[out].dtype)
                total = value if total is None else total + value
            buffers[out][to : to + height, :] = total.astype(buffers[out].dtype)
        wait(needs)
        stores.append(pltpu.make_async_copy(buffers[out], outs[out], out_sems.at[out]))
        stores[-1].start()
    for store in stores:
        store.wait()


class Stream:
    def __init__(self, parts, first_y, rows, base=0, direct=False):
        self.parts, self.first_y, self.rows, self.base = parts, first_y, rows, base
        self.age, self.direct, self.last = 0, direct, False
        self.keep = self.recv = self.total = self.joined = None


class Joined:
    def __init__(self, streams):
        self.streams, self.out, self.total = streams, None, None
        self.rows = sum(stream.rows for stream in streams)
        for stream in streams:
            stream.joined = self

    def start(self, stream):
        return sum(other.rows for other in self.streams[: self.streams.index(stream)])


class Pipe:
    def __init__(self, at):
        self.at, self.groups = at, []
        self.bits = at.nz.bit_length() - 1
        scalars = [at.x, at.y] + [at.z // (1 << bit) % 2 for bit in range(self.bits)]
        self.scalars = jnp.stack(scalars).astype(jnp.int32)

    def add(self, streams):
        self.groups.append(streams)

    def pieces(self, stream, rows):
        nz = self.at.nz
        first = 1 if stream.first_y else 0
        strides = (2, 1)

        def chip(z, coords):
            start, slopes = stream.base + 4 * z * rows, []
            for axis, (fixed, slope) in enumerate(coords):
                start += fixed * strides[axis] * rows
                if slope:
                    slopes.append((axis, slope * strides[axis] * rows))
            return start, slopes

        def spot(fixed, number, slope, scale, base=0):
            return (base + fixed * scale, [(number, slope * scale)])

        other, same = (1, -1), (0, 1)
        sent, kept = [], []
        if stream.age == 0:
            for z in range(nz):
                for far in range(2):
                    coords = [None, None]
                    coords[first], coords[1 - first] = other, (far, 0)
                    sent.append([(stream.parts, chip(z, coords))])
        elif stream.age == 1:
            ((ref, base),) = stream.recv
            for out, side in ((sent, other), (kept, same)):
                for z in range(nz):
                    coords = [None, None]
                    coords[first], coords[1 - first] = same, side
                    place = spot(2 * z + side[0], 1 - first, side[1], rows, base)
                    out.append([(stream.parts, chip(z, coords)), ([ref], place)])
        elif stream.direct and stream.age == 2:
            ((ref, base),) = stream.recv
            for flip in range(nz):
                start, slopes = 0, []
                for bit in range(self.bits):
                    fixed, slope = other if flip >> bit & 1 else same
                    start += (fixed << bit) * rows
                    slopes.append((2 + bit, (slope << bit) * rows))
                out = sent if flip else kept
                out.append([([stream.keep], (start, slopes)), ([ref], (base + start, slopes))])
        elif not self.final(stream):
            bit = stream.age - 2
            ((ref, base),) = stream.recv
            for out, side in ((sent, other), (kept, same)):
                for high in range(nz >> (bit + 1)):
                    fixed = 2 * high + side[0]
                    keep = spot(fixed, 2 + bit, side[1], rows)
                    out.append([([stream.keep], keep), ([ref], spot(fixed, 2 + bit, side[1], rows, base))])
        else:
            kept.append([([stream.keep], (0, []))] + [([ref], (base, [])) for ref, base in stream.recv])
        return sent, kept

    def final(self, stream):
        return stream.age == (3 if stream.direct else 2 + self.bits)

    def step(self, *others, extra=None):
        heights, keeps, todo, self.sent = {}, [], [], []
        spots, self.joined = [], None
        for streams in self.groups:
            for stream in streams:
                if stream.last:
                    continue
                rows = stream.rows
                sent, kept = self.pieces(stream, rows)
                axis = (2, 1) if stream.first_y else (1, 2)
                blocks, spans = [], []
                if stream.age < 2:
                    spans = [(axis[stream.age], len(sent))]
                elif sent:
                    spans = [(-flip, 1) for flip in range(1, len(sent) + 1)]
                    if not stream.direct:
                        spans = [(-(1 << (stream.age - 2)), len(sent))]
                for key, many in spans:
                    start = heights.get(key, 0)
                    heights[key] = start + many * rows
                    self.sent.append((stream, key, start))
                    blocks += [(key, start + block * rows) for block in range(many)]
                todo.append((stream, blocks, sent, kept, rows))
        if extra is not None:
            span = (heights.get(2, 0), extra.shape[0])
            heights[2] = sum(span)
        order = list(heights)
        shapes = [sds((heights[key], D), BF16) for key in order]
        jobs = [([], []) for _ in order]
        arrays, loads, buffers, held = [], [], [], {}

        def source(array):
            for i, known in enumerate(arrays):
                if known is array:
                    return i
            arrays.append(array)
            return len(arrays) - 1

        for stream, blocks, sent, kept, rows in todo:
            if kept:
                last = self.final(stream)
                if last and stream.joined is not None:
                    if stream.joined.out is None:
                        stream.joined.out = len(shapes)
                        shapes.append(sds((stream.joined.rows, D), F32))
                        jobs.append(([], []))
                        self.joined = stream.joined
                    spots.append((stream.joined.out, stream.joined.start(stream)))
                    continue
                keeps.append((stream, len(shapes)))
                spots.append((len(shapes), 0))
                shapes.append(sds((len(kept) * rows, D), F32 if last else BF16))
                jobs.append(([], []))
        buffers = list(shapes)
        if extra is not None:
            jobs[order.index(2)][0].append(len(loads))
            loads.append((source(extra), (0, []), span[1], order.index(2), span[0], 0, D))
        spare = len(buffers)
        buffers.append(None)
        spare_rows = 0

        def term(parts, place, height):
            nonlocal spare_rows
            if len(parts) == 1 and not any(part is parts[0] for part in stream.parts):
                array = source(parts[0])
                if array not in held:
                    held[array] = (len(buffers), len(loads))
                    loads.append((array, (0, []), parts[0].shape[0], len(buffers), 0, 0, D))
                    buffers.append(sds(parts[0].shape, parts[0].dtype))
                return held[array][0], place, [held[array][1]]
            row, numbers = spare_rows, []
            spare_rows += height
            for number, part in enumerate(parts):
                width = D // len(parts)
                numbers.append(len(loads))
                loads.append((source(part), place, height, spare, row, number * width, width))
            return spare, (row, []), numbers

        for stream, blocks, sent, kept, rows in todo:
            for (key, to), terms in zip(blocks, sent):
                out = order.index(key)
                if len(terms) == 1:
                    ((parts, place),) = terms
                    for number, part in enumerate(parts):
                        width = D // len(parts)
                        jobs[out][0].append(len(loads))
                        loads.append((source(part), place, rows, out, to, number * width, width))
                else:
                    jobs[out][1].append((to, rows, [term(parts, place, rows) for parts, place in terms]))
        spots = iter(spots)
        for stream, blocks, sent, kept, rows in todo:
            if kept:
                out, first = next(spots)
                for block, terms in enumerate(kept):
                    terms = [term(parts, place, rows) for parts, place in terms]
                    jobs[out][1].append((first + block * rows, rows, terms))
        buffers[spare] = sds((max(spare_rows, 16), D), BF16)
        outs = pl.pallas_call(
            functools.partial(
                blocks_kernel, counts=(len(arrays), len(shapes)), loads=loads, jobs=jobs
            ),
            name="blocks",
            out_shape=shapes,
            in_specs=[pl.BlockSpec(memory_space=pltpu.SMEM)]
            + [pl.BlockSpec(memory_space=pltpu.HBM)] * len(arrays),
            out_specs=[pl.BlockSpec(memory_space=pltpu.HBM)] * len(shapes),
            scratch_shapes=[pltpu.VMEM(buffer.shape, buffer.dtype) for buffer in buffers]
            + [pltpu.SemaphoreType.DMA((len(loads),)), pltpu.SemaphoreType.DMA((len(shapes),))],
            compiler_params=params(),
            cost_estimate=cost(0, sum(3 * array.size for array in arrays)),
        )(self.scalars, *arrays)
        if self.joined is not None:
            self.joined.total = outs[self.joined.out]
        for stream, out in keeps:
            stream.keep = outs[out]
            if self.final(stream):
                stream.total = outs[out]
        for stream, *_ in todo:
            stream.last = self.final(stream)
            stream.age += 1
        payloads, others = lax.optimization_barrier((outs[: len(order)], others))
        self.moved = {}
        self.span = None if extra is None else span
        for key, payload in zip(order, payloads):
            if key > 0:
                self.moved[key] = self.at.move(payload, key, 1)
            else:
                self.moved[key] = self.at.move(payload, 0, -key, flip=True)
        return others

    def close(self, *others):
        self.moved, others = lax.optimization_barrier((self.moved, others))
        for stream, key, start in self.sent:
            stream.recv = []
        for stream, key, start in self.sent:
            stream.recv.append((self.moved[key], start))
        if self.span is not None:
            self.extra = [self.moved[2][self.span[0] : sum(self.span)]]
        return others

    def busy(self):
        return not all(stream.last for streams in self.groups for stream in streams)


def pick(stacked, index, axis=0):
    return lax.dynamic_index_in_dim(stacked, index, axis, keepdims=False)


def by_core(core, mine, theirs, axis):
    return jnp.where(core == 0, jnp.stack([mine, theirs], axis), jnp.stack([theirs, mine], axis))


def body(
    hidden,
    boxes,
    page_size,
    band_count,
    layout_tables,
    attn_in,
    attn_bias,
    attn_out,
    out_bias,
    norm_gain,
    norm_bias,
    ffn_in,
    ffn_in_bias,
    ffn_out,
    ffn_out_bias,
    out_grad,
    *,
    pages,
    bands,
):
    at = Places(pages, bands)
    core = at.core
    core_id = core.astype(jnp.int32).reshape(1)
    devices = pages * bands
    ny, chips = at.ny, at.chips
    cap = hidden.shape[2]
    rows_dev = attn_in.shape[1]
    table_rows = layout_tables.shape[1]
    ff_dev = ffn_out.shape[1]
    chip_rows = CORES * rows_dev
    tiled = rows_dev % 8 == 0 and ff_dev == 2 * FF_CHUNK and at.nx == ny == 2

    def local_weights(layer):
        if tiled:
            mine, send = pack(core_id, attn_in, attn_out, ffn_in, layer)
            shapes = ((2, chip_rows, D), (4, chip_rows, D))
            return join(core_id, mine, at.swap(send), ffn_out, layer, shapes)
        columns = jnp.concatenate(
            [attn_in[layer].reshape(rows_dev, 3, CORES, HALF), attn_out[layer].reshape(rows_dev, 1, CORES, HALF)],
            axis=1,
        ).transpose(2, 0, 1, 3)
        ups = ffn_in[layer].reshape(rows_dev, chips, CORES, 2, ff_dev // 2).transpose(2, 0, 3, 1, 4)
        packed = jnp.concatenate(
            [columns.reshape(CORES, rows_dev, 4 * HALF), ups.reshape(CORES, rows_dev, FF // CORES)], axis=2
        )
        both = by_core(core, pick(packed, core), at.swap(pick(packed, 1 - core)), 0)
        both = both.reshape(chip_rows, PACKED)
        down = ffn_out[layer].reshape(2, chip_rows, D)
        both = both.reshape(chip_rows, 4, D).swapaxes(0, 1)
        return both[:2], jnp.stack([both[2], down[0], both[3], down[1]])

    attn_place = ([(0, 1, 0, 0, 0, D)], [(0, 1, 0, D, 0, D), (1, 1, 0, 0, HALF, HALF)])
    attn_shapes = ((chips, chip_rows, 2 * D), (chips, chip_rows, HALF))
    ffn_place = [[(0, 1, 0, col * D, 0, D)] for col in (0, 2, 1, 3)]
    ffn_shapes = ((chips, chip_rows, 4 * D),)
    table_place = [[(table, 1, 0, 0, 0, D)] for table in range(4)]
    table_shapes = ((chips, table_rows, D),) * 4

    def to_chip(stacked):
        own = [pick(stacked, at.y)]
        for k in range(1, ny):
            own.append(at.move(pick(stacked, (at.y + k) % ny), 2, k))
        return own

    def send_back(rows):
        parts = rows.reshape((ny, cap) + rows.shape[1:])
        return [at.move(parts[k].astype(BF16), 2, -k) for k in range(1, ny)]

    def from_chip(rows, back):
        back = [rows[:cap]] + [part.astype(F32) for part in back]
        back = jnp.stack(back)
        return jnp.stack([pick(back, (page - at.y) % ny) for page in range(ny)])[:, None]

    def token_facts(hidden, out_grad, boxes, page_size, band_count):
        widths, heights = page_size[0][:, None], page_size[1][:, None]
        left = boxes[0, :, 0] * GRID // widths
        top = boxes[1, :, 0] * GRID // heights
        right = boxes[2, :, 0] * GRID // widths
        bottom = boxes[3, :, 0] * GRID // heights
        live = (lax.broadcasted_iota(jnp.int32, left.shape, 1) < band_count).astype(jnp.int32)
        facts = jnp.stack([left, top, right, bottom, bottom - top, right - left, live, live], axis=1)
        facts_own = jnp.concatenate(to_chip(facts), axis=-1)
        facts_all = jnp.concatenate([facts_own, at.swap(facts_own)], axis=-1)
        owner = facts_all // table_rows
        index = jnp.where(
            owner % CORES == core, owner // CORES * table_rows + facts_all % table_rows, -1
        )
        mask = jnp.where(facts_all[6:7] > 0, 0.0, DEAD).astype(F32)
        live_own = facts_own[6].astype(F32)[:, None]
        hidden_own = jnp.concatenate(to_chip(hidden[:, 0]), axis=0)
        grad_own = jnp.concatenate(to_chip(out_grad[:, 0]), axis=0)
        return index, mask, live_own, hidden_own, grad_own

    cut = SMALL_ROWS * rows_dev

    def small_params(attn_bias, out_bias, norm_gain, norm_bias, ffn_out_bias, ffn_in_bias):
        segment = jnp.concatenate(
            [
                attn_bias.reshape(-1),
                out_bias.reshape(-1),
                norm_gain.reshape(-1),
                norm_bias.reshape(-1),
                ffn_out_bias.reshape(-1),
                ffn_in_bias.reshape(-1),
            ]
        )
        smalls = lax.all_to_all(
            jnp.broadcast_to(segment, (devices, segment.shape[0])), ("page", "band"), 0, 0, tiled=True
        ).astype(F32)
        small = smalls[:, :cut].reshape(devices, SMALL_ROWS, rows_dev).swapaxes(0, 1).reshape(SMALL_ROWS, D)
        up_bias = pick(smalls[:, cut:].reshape(chips, CORES, LAYERS, 2, ff_dev // 2), core, 1)
        up_bias = up_bias.transpose(1, 2, 0, 3).reshape(LAYERS, FF // CORES)
        return small, up_bias

    saved = [[], []]
    weights = [[], []]

    def look_up(state):
        tables = line.result(chunks[0])
        looked_up = embed(index.T, tables)
        mine = hidden_own.astype(F32) + looked_up[:half]
        x = mine + at.swap(looked_up[half:].astype(BF16)).astype(F32)
        return x, x.astype(BF16)

    def attend(layer, state):
        x, x_low = state
        wa, wom = line.result(chunks[1 + 2 * layer])
        wot, x_other = at.swap(wom), at.swap(x_low)
        weights[layer] += [wa, wom, wot]
        q, k, v, mix_own, mix_other = attn_fwd(core_id, x_low, x_other, wa, small, mask, layer)
        y1, y1_low, n1, r1 = out_norm(core_id, mix_own, at.swap(mix_other), wom, wot, x, small, layer)
        saved[layer] += [x_low, x_other, q, k, v, mix_own, mix_other, n1, r1]
        return y1, y1_low

    def feed(layer, state):
        y1, y1_low = state
        (w1,) = line.result(chunks[2 + 2 * layer])
        w2, col = (w1, 2 * D) if layer == 0 else (downs[0], 0)
        y1_other = at.swap(y1_low)
        weights[layer] += [w1, w2, col]
        act, slope, part, part_other = ffn_fwd(y1_low, y1_other, w1, w2, col, up_bias, layer)
        x, x_low, n2, r2 = add_norm(y1, part, at.swap(part_other), small, layer)
        saved[layer] += [y1_low, y1_other, act, slope, n2, r2]
        return x, x_low

    half = ny * cap
    line = Line(at)
    chunks = [Gather(at, layout_tables, table_shapes, table_place)]
    parts = [look_up]
    line.add(chunks[0])
    down_chunk = LateGather(
        at,
        ffn_out[LAYERS - 1].reshape(2, chip_rows, D),
        ((chips, chip_rows, 2 * D),),
        ([(0, 1, 0, 0, 0, D)], [(0, 1, 0, D, 0, D)]),
        3,
    )
    line.add(down_chunk)
    line.step()
    locals0 = local_weights(0)
    token_args = (hidden, out_grad, boxes, page_size, band_count)
    small_args = (attn_bias, out_bias, norm_gain, norm_bias, ffn_out_bias, ffn_in_bias)
    locals0, token_args = line.close(locals0, token_args)
    state, downs = (), []
    running = None
    waiting = []
    for layer in range(LAYERS):
        waiting += [(layer, 0), (layer, 1)]
        parts += [functools.partial(attend, layer), functools.partial(feed, layer)]
    local = locals0
    while waiting or running is not None or not line.done(chunks[-1]):
        if waiting:
            layer, number = waiting.pop(0)
            if layer > 0 and number == 0:
                local = local_weights(layer)
            if layer > 0 and number == 1:
                shard = jnp.stack([local[1][0], local[1][2]])
                shapes, place = ((chips, chip_rows, 2 * D),), ([(0, 1, 0, 0, 0, D)], [(0, 1, 0, D, 0, D)])
            else:
                shard = local[number]
                shapes, place = (attn_shapes, ffn_shapes)[number], (attn_place, ffn_place)[number]
            chunks.append(Gather(at, shard, shapes, place))
            line.add(chunks[-1])
        if all(line.done(chunk) for chunk in chunks):
            state = running(state)
            break
        state = line.step(*state)
        if line.done(down_chunk) and not downs and not line.fresh(down_chunk):
            downs.append(line.result(down_chunk)[0])
        if running is not None:
            state = running(state)
        if len(chunks) == 2:
            tokens, small_args, late = line.close(
                token_facts(*token_args), small_args, (attn_in, attn_out, ffn_in)
            )
            index, mask, live_own, hidden_own, grad_own = tokens
            attn_in, attn_out, ffn_in = late
        elif len(chunks) == 3:
            (small_args,) = line.close(small_args)
        elif len(chunks) == 4:
            small, up_bias = line.close(*small_params(*small_args))
        elif downs:
            state, downs = line.close(state, downs)
        else:
            state = line.close(*state)
        ready = [number for number, chunk in enumerate(chunks) if line.fresh(chunk)]
        running = parts[ready[0]] if ready else None
    x = state[0]

    small_grads = [None] * LAYERS

    def backward_ffn(layer, sources):
        w1, w2, col = weights[layer][3:]
        y1_low, y1_other, act, slope, n2, r2 = saved[layer][9:]
        gh2, df, sums2 = norm_bwd(sources, n2, r2, small, 2 * layer + 1)
        dw1, dw2, up_sums, part, part_other = ffn_bwd(df, at.swap(df), w1, w2, col, act, slope, y1_low, y1_other)
        small_grads[layer] = [sums2, up_sums]
        return (gh2, part, at.swap(part_other)), dw1, dw2

    def backward_attn(layer, sources):
        wa, wom, wot = weights[layer][:3]
        x_low, x_other, q, k, v, mix_own, mix_other, n1, r1 = saved[layer][:9]
        gh1, da, sums1 = norm_bwd(sources, n1, r1, small, 2 * layer)
        dwq, dwk, dwv, dwo, dwo_sent, attn_sums, part, part_other = attn_bwd(
            core_id, da, at.swap(da), wom, wot, q, k, v, mix_own, mix_other, x_low, x_other, wa, mask
        )
        small_grads[layer] = [sums1] + small_grads[layer] + [attn_sums]
        return (gh1, part, at.swap(part_other)), (dwq, dwk, dwv), (dwo, at.swap(dwo_sent))

    def attn_groups(dqkv, dwo):
        dwq, dwk, dwv = dqkv
        return [dwq, dwk], [dwv, by_core(core, *dwo, 0).reshape(D, HALF)]

    line = Pipe(at) if tiled else Line(at)

    def ffn_chunk(dw1, dw2):
        if tiled:
            flat = [dw.reshape(2 * D, D) for dw in (dw1, dw2)]
            streams = [Stream([unit], part == 0, chip_rows, part * D) for part in range(2) for unit in flat]
            line.add(streams)
            return streams
        chunk = Reduce(at, [[dw1[0]], [dw2[0]]], [[dw1[1]], [dw2[1]]])
        line.add(chunk)
        return chunk

    def attn_chunk(dqkv, dwo, direct):
        first, second = attn_groups(dqkv, dwo)
        if tiled:
            streams = [
                Stream(part, part is first, chip_rows, direct=direct) for part in (first, second)
            ]
            line.add(streams)
            return streams
        chunk = Reduce(at, [first], [second])
        line.add(chunk)
        return chunk

    def table_chunk(tables):
        if tiled:
            streams = [Stream([table], number < 2, table_rows) for number, table in enumerate(tables)]
            line.add(streams)
            return Joined(streams)
        chunk = Reduce(at, [[table] for table in tables[:2]], [[table] for table in tables[2:]])
        line.add(chunk)
        return chunk

    sources, dw1, dw2 = backward_ffn(1, (grad_own, live_own))
    ffn1 = ffn_chunk(dw1, dw2)
    output = x * live_own
    sources = line.step(*sources, extra=output[cap:].astype(BF16) if tiled else None)
    sources, dqkv, dwo = backward_attn(1, sources)
    sources = line.close(*sources)
    output = from_chip(output, line.extra if tiled else send_back(output))
    att1 = attn_chunk(dqkv, dwo, False)
    sources = line.step(*sources)
    sources, dw1, dw2 = backward_ffn(0, sources)
    sources = line.close(*sources)
    ffn0 = ffn_chunk(dw1, dw2)
    sources = line.step(*sources)
    sources, dqkv, dwo = backward_attn(0, sources)
    sources = line.close(*sources)
    att0 = attn_chunk(dqkv, dwo, False)
    sources = line.step(*sources)
    grad_x = sources[0] + sources[1] + sources[2].astype(F32)
    grad_low = grad_x.astype(BF16)
    table_parts = table_grads(index, grad_low, at.swap(grad_low), chips * table_rows)
    table_parts = line.close(*table_parts)
    tab = table_chunk(table_parts)
    line.step(extra=grad_x[cap:].astype(BF16) if tiled else None)
    line.close()
    input_grad = from_chip(grad_x, line.extra if tiled else send_back(grad_x))
    zeros = jnp.zeros((2, HALF), F32)
    vectors = []
    for layer in range(LAYERS):
        mine = small_grads[layer][3][:2]
        vectors.append(by_core(core, mine, zeros, 1).reshape(2, D))
    vectors.append(jnp.stack([small_grads[layer][0][2] for layer in range(LAYERS)]))
    for row in range(2):
        for layer in range(LAYERS):
            vectors.append(jnp.stack([small_grads[layer][norm][row] for norm in range(2)]))
    vectors.append(jnp.stack([small_grads[layer][1][2] for layer in range(LAYERS)]))
    vectors = lax.optimization_barrier(jnp.concatenate(vectors)).reshape(SMALL_ROWS, devices, rows_dev).swapaxes(0, 1)
    ups_grad = jnp.stack([small_grads[layer][2][0] for layer in range(LAYERS)])
    ups_grad = ups_grad.reshape(LAYERS, 2, chips, ff_dev // 2).transpose(2, 0, 1, 3)
    ups_grad = by_core(core, ups_grad, jnp.zeros_like(ups_grad), 1)
    segments = jnp.concatenate(
        [vectors.reshape(devices, cut), ups_grad.reshape(devices, LAYERS * ff_dev)], axis=1
    )
    segments = lax.all_to_all(segments, ("page", "band"), 0, 0, tiled=True)


    def small_outputs(segments):
        segment = jnp.sum(segments, axis=0)
        rows = segment[:cut].reshape(SMALL_ROWS, rows_dev)
        return (
            rows[ROW_ATTN:ROW_OUT].reshape(LAYERS, 2, rows_dev),
            rows[ROW_OUT:ROW_GAIN],
            rows[ROW_GAIN:ROW_SHIFT].reshape(LAYERS, 2, rows_dev),
            rows[ROW_SHIFT:ROW_DOWN].reshape(LAYERS, 2, rows_dev),
            segment[cut:].reshape(LAYERS, ff_dev),
            rows[ROW_DOWN:SMALL_ROWS],
        )

    grads = None
    while line.busy():
        line.step()
        if tiled and grads is None and att0[0].total is not None:
            results = [
                [stream.total for stream in attn[:2] + ffn] for attn, ffn in ((att0, ffn0), (att1, ffn1))
            ]
            parts = []
            for qk, vo, up_a, down_a, up_b, down_b in results:
                mine, send = split(core_id, (qk, vo, up_a, up_b))
                parts += [mine, at.swap(send), down_a, down_b]
            grads = merge(core_id, parts)
            smalls = small_outputs(tie(segments, grads[0]))
            grads, smalls = line.close(grads, smalls)
        else:
            line.close()
    if not tiled:
        smalls = small_outputs(segments)
    if tiled:
        grad_tables = tab.total.reshape(4, table_rows, D)
    else:
        sums = [line.result(chunk) for chunk in (att0, ffn0, att1, ffn1)]
        grad_tables = jnp.stack(line.result(tab)).reshape(4, table_rows, D)
        results = []
        for attn_sum, ffn_sum in ((sums[0], sums[1]), (sums[2], sums[3])):
            attn = jnp.stack(attn_sum)
            ffn = jnp.stack(ffn_sum).reshape(4, chip_rows, D)
            results.append((attn, ffn, ffn))

    if not tiled:
        grads = [[], [], [], []]
        for layer in range(LAYERS):
            attn_sum, up_sum, down_sum = results[layer]
            both = jnp.stack([attn_sum[0], attn_sum[1], up_sum[0], up_sum[2]])
            by_owner = both.reshape(4, CORES, rows_dev, D)
            mine, theirs = pick(by_owner, core, 1), at.swap(pick(by_owner, 1 - core, 1))
            both = by_core(core, mine, theirs, 0).transpose(2, 0, 1, 3)
            attn = both[:, :, :2].reshape(rows_dev, CORES, 4, HALF).swapaxes(1, 2)
            grads[0].append(attn[:, :3].reshape(rows_dev, 3 * D))
            grads[1].append(attn[:, 3].reshape(rows_dev, D))
            ups = both[:, :, 2:].reshape(rows_dev, CORES, 2, chips, ff_dev // 2).transpose(0, 3, 1, 2, 4)
            grads[2].append(ups.reshape(rows_dev, FF))
            grads[3].append(jnp.concatenate([down_sum[1], down_sum[3]]))
        grads = [jnp.stack(pair) for pair in grads]

    return (
        output,
        input_grad,
        grad_tables,
        grads[0],
        smalls[0],
        grads[1],
        smalls[1],
        smalls[2],
        smalls[3],
        grads[2],
        smalls[4],
        grads[3],
        smalls[5],
    )


def solution(mesh):
    both = ("page", "band")
    tokens = P("page", "band", None, None)
    middle = P(None, both, None)
    last = P(None, both)
    third = P(None, None, both)
    return jax.shard_map(
        functools.partial(body, pages=mesh.shape["page"], bands=mesh.shape["band"]),
        mesh=mesh,
        in_specs=(
            tokens,
            P(None, "page", "band", None),
            P(None, "page"),
            P("page", "band"),
            middle,
            middle,
            third,
            middle,
            last,
            third,
            third,
            middle,
            last,
            middle,
            last,
            tokens,
        ),
        out_specs=(
            tokens,
            tokens,
            middle,
            middle,
            third,
            middle,
            last,
            third,
            third,
            middle,
            last,
            middle,
            last,
        ),
        check_vma=False,
    )
```

```python
import functools
import math

import jax
import jax.numpy as jnp
from jax import lax
from jax.experimental import pallas as pl
from jax.experimental.pallas import tpu as pltpu
from jax.sharding import PartitionSpec as P

D = 768
HEADS = 12
HEAD_DIM = 64
HALF = D // 2
PAIRS = HEADS // 4
FF = 3072
POS = 1024
GRID = 1000
LAYERS = 2
CORES = 2
LANES = 128
EPS = 1e-12
DEAD = -1000000000.0
SCALE = HEAD_DIM ** (-0.5)
VMEM = 52 * 1024 * 1024
F32 = jnp.float32
BF16 = jnp.bfloat16

ROW_ATTN, ROW_OUT, ROW_GAIN, ROW_SHIFT, ROW_DOWN = 0, 4, 6, 10, 14
SMALL_ROWS = 16


def dot(a, b, dims=((1,), (0,))):
    return lax.dot_general(a, b, (dims, ((), ())), preferred_element_type=F32)


def halves(core):
    first = core[0] * HALF
    return pl.ds(pl.multiple_of(first, LANES), HALF), pl.ds(pl.multiple_of(HALF - first, LANES), HALF)


NT = ((1,), (1,))
TN = ((0,), (0,))


def sds(shape, dtype):
    return jax.ShapeDtypeStruct(shape, dtype)


def whole(shape):
    return pl.BlockSpec(shape, lambda *_: (0,) * len(shape))


def cost(flops, nbytes, trans=0):
    return pl.CostEstimate(flops=flops, bytes_accessed=nbytes, transcendentals=trans)


def params():
    return pltpu.CompilerParams(vmem_limit_bytes=VMEM)


def embed_kernel(idx, t0, t1, t2, t3, out):
    rows = t0.shape[0]
    place = lax.broadcasted_iota(jnp.int32, (idx.shape[0], rows), 1)

    def hot(*cols):
        total = None
        for col in cols:
            one = jnp.where(place == idx[:, col : col + 1], 1.0, 0.0)
            total = one if total is None else total + one
        return total.astype(BF16)

    out[...] = (
        dot(hot(0, 2), t0[...])
        + dot(hot(1, 3), t1[...])
        + dot(hot(4), t2[...])
        + dot(hot(5), t3[...])
    )


def embed(idx, tables):
    tokens = idx.shape[0]
    block = 128
    rows = tables[0].shape[0]
    return pl.pallas_call(
        embed_kernel,
        name="embed",
        out_shape=sds((tokens, D), F32),
        grid=(tokens // block,),
        in_specs=[pl.BlockSpec((block, 8), lambda i: (i, 0))] + [whole((rows, D))] * 4,
        out_specs=pl.BlockSpec((block, D), lambda i: (i, 0)),
        compiler_params=params(),
        cost_estimate=cost(8 * tokens * rows * D, 8 * rows * D + 4 * tokens * D),
    )(idx, *tables)


def table_kernel(idx, own, sib, o0, o1, o2, o3):
    half = own.shape[0]
    block = o0.shape[0]
    first = pl.program_id(0) * block
    place = lax.broadcasted_iota(jnp.int32, (block, 2 * half), 0) + first

    def hot(*rows):
        total = None
        for row in rows:
            one = jnp.where(place == idx[row : row + 1, :], 1.0, 0.0)
            total = one if total is None else total + one
        return total.astype(BF16)

    for out, rows in ((o0, (0, 2)), (o1, (1, 3)), (o2, (4,)), (o3, (5,))):
        mark = hot(*rows)
        out[...] = (dot(mark[:, :half], own[...]) + dot(mark[:, half:], sib[...])).astype(BF16)


def table_grads(idx, own, sib, rows):
    half = own.shape[0]
    block = 256
    return pl.pallas_call(
        table_kernel,
        name="table_grads",
        out_shape=[sds((rows, D), BF16)] * 4,
        grid=(rows // block,),
        in_specs=[whole((8, 2 * half)), whole((half, D)), whole((half, D))],
        out_specs=[pl.BlockSpec((block, D), lambda i: (i, 0))] * 4,
        compiler_params=params(),
        cost_estimate=cost(16 * half * rows * D, 8 * rows * D),
    )(idx, own, sib)


def attn_fwd_kernel(core, xo, xs, wq, wk, wv, small, mask, q, k, v, mo, ms, *, layer):
    half = xo.shape[0]
    joined = jnp.concatenate([wq[...], wk[...], wv[...]], axis=1)
    row = ROW_ATTN + 2 * layer
    for first, rows in ((0, xo), (half, xs)):
        span = slice(first, first + half)
        qkv = dot(rows[...], joined)
        q[span, :] = (qkv[:, :LANES] + small[row : row + 1, :]).astype(BF16)
        k[span, :] = qkv[:, LANES : 2 * LANES].astype(BF16)
        v[span, :] = (qkv[:, 2 * LANES :] + small[row + 1 : row + 2, :]).astype(BF16)
    keys, values = k[...], v[...]
    low_lanes = lax.broadcasted_iota(jnp.int32, (1, LANES), 1) < HEAD_DIM
    for first, out in ((0, mo), (half, ms)):
        queries = q[first : first + half, :].astype(F32) * SCALE
        parts = []
        for head in range(2):
            lanes = low_lanes if head == 0 else jnp.logical_not(low_lanes)
            one = jnp.where(lanes, queries, 0.0).astype(BF16)
            scores = dot(one, keys, NT) + mask[...]
            expo = jnp.exp(scores - jnp.max(scores, axis=-1, keepdims=True))
            total = jnp.sum(expo, axis=-1, keepdims=True)
            parts.append(dot(expo.astype(BF16), values) / total)
        out[...] = jnp.where(low_lanes, parts[0], parts[1]).astype(BF16)


def weight_block(part):
    return pl.BlockSpec((D, LANES), lambda p, core: (0, part * PAIRS + p))


def attn_fwd(core, xo, xs, wa, small, mask, layer):
    half = xo.shape[0]
    tokens = 2 * half
    col = lambda p, core: (0, p)
    rows = pl.BlockSpec((tokens, LANES), col)
    return pl.pallas_call(
        functools.partial(attn_fwd_kernel, layer=layer),
        name="attn_fwd",
        out_shape=[sds((tokens, HALF), BF16)] * 3 + [sds((half, HALF), BF16)] * 2,
        grid_spec=pltpu.PrefetchScalarGridSpec(
            num_scalar_prefetch=1,
            grid=(PAIRS,),
            in_specs=[
                whole((half, D)),
                whole((half, D)),
                weight_block(0),
                weight_block(1),
                weight_block(2),
                pl.BlockSpec((SMALL_ROWS, LANES), lambda p, core: (0, core[0] * PAIRS + p)),
                whole((1, tokens)),
            ],
            out_specs=[rows] * 3 + [pl.BlockSpec((half, LANES), col)] * 2,
        ),
        compiler_params=params(),
        cost_estimate=cost(
            2 * tokens * D * 3 * HALF + 4 * PAIRS * 2 * tokens * tokens * LANES,
            2 * (tokens * D + 3 * D * HALF + 4 * tokens * HALF),
            PAIRS * 2 * tokens * tokens,
        ),
    )(core, xo, xs, wa, wa, wa, small, mask)


def attn_bwd_kernel(
    core, dao, das, wom, wot, q, k, v, mo, ms, xo, xs, wq, wk, wv, mask,
    dwq, dwk, dwv, dwo, dwo_sent, sums, dxo, dxs, acc, all_s, turned,
):
    half = xo.shape[0]
    step = pl.program_id(0)
    mine_cols, their_cols = halves(core)
    dq_s, dk_s, dv_s = [all_s.at[:, part * LANES : (part + 1) * LANES] for part in range(3)]

    @pl.when(step == 0)
    def _():
        turned[:, :half] = xo[...].T
        turned[:, half:] = xs[...].T

    keys, values = k[...], v[...]
    low_lanes = lax.broadcasted_iota(jnp.int32, (1, LANES), 1) < HEAD_DIM
    grad_keys = [None, None]
    grad_values = [None, None]
    for part, da in ((0, dao), (1, das)):
        first = part * half
        span = slice(first, first + half)
        grad_mix = dot(da[:, mine_cols], wom[...], NT) + dot(da[:, their_cols], wot[...], NT)
        queries = q[span, :].astype(F32) * SCALE
        grad_queries = []
        for head in range(2):
            lanes = low_lanes if head == 0 else jnp.logical_not(low_lanes)
            one = jnp.where(lanes, queries, 0.0).astype(BF16)
            scores = dot(one, keys, NT) + mask[...]
            expo = jnp.exp(scores - jnp.max(scores, axis=-1, keepdims=True))
            probs = expo * (1.0 / jnp.sum(expo, axis=-1, keepdims=True))
            grad_one = jnp.where(lanes, grad_mix, 0.0).astype(BF16)
            grad_probs = dot(grad_one, values, NT)
            weighted = probs * grad_probs
            delta = jnp.sum(weighted, axis=-1, keepdims=True)
            grad_scores = (weighted - probs * delta).astype(BF16)
            grad_queries.append(dot(grad_scores, keys))
            key_part = dot(grad_scores, one, TN)
            value_part = dot(probs.astype(BF16), grad_one, TN)
            if part == 0:
                grad_keys[head], grad_values[head] = key_part, value_part
            else:
                grad_keys[head] = grad_keys[head] + key_part
                grad_values[head] = grad_values[head] + value_part
        dq_s[span, :] = (jnp.where(low_lanes, grad_queries[0], grad_queries[1]) * SCALE).astype(BF16)
    dk_s[...] = (grad_keys[0] + grad_keys[1]).astype(BF16)
    dv_s[...] = (grad_values[0] + grad_values[1]).astype(BF16)
    sums[...] = jnp.zeros_like(sums)
    sums[0:1, :] = jnp.sum(dq_s[...].astype(F32), axis=0, keepdims=True)
    sums[1:2, :] = jnp.sum(dv_s[...].astype(F32), axis=0, keepdims=True)
    weight_grads = dot(turned[...], all_s[...]).astype(BF16)
    for part, out in enumerate((dwq, dwk, dwv)):
        out[...] = weight_grads[:, part * LANES : (part + 1) * LANES]
    out_rows = dot(mo[...], dao[...], TN) + dot(ms[...], das[...], TN)
    even = core[0] == 0
    dwo[...] = jnp.where(even, out_rows[:, :HALF], out_rows[:, HALF:]).astype(BF16)
    dwo_sent[...] = jnp.where(even, out_rows[:, HALF:], out_rows[:, :HALF]).astype(BF16)
    total = dot(all_s[...], jnp.concatenate([wq[...], wk[...], wv[...]], axis=1), NT)

    @pl.when(step == 0)
    def _():
        acc[...] = total

    @pl.when(step > 0)
    def _():
        acc[...] += total

    @pl.when(step == PAIRS - 1)
    def _():
        dxo[...] = acc[:half, :].astype(BF16)
        dxs[...] = acc[half:, :].astype(BF16)


def attn_bwd(core, dao, das, wom, wot, q, k, v, mo, ms, xo, xs, wa, mask):
    half = xo.shape[0]
    tokens = 2 * half
    col = lambda p, core: (0, p)
    weight = pl.BlockSpec((D, LANES), col)
    rows = pl.BlockSpec((tokens, LANES), col)
    part = pl.BlockSpec((half, LANES), col)
    out_rows = pl.BlockSpec((LANES, HALF), lambda p, core: (core[0] * PAIRS + p, 0))
    return pl.pallas_call(
        attn_bwd_kernel,
        name="attn_bwd",
        out_shape=[sds((D, HALF), BF16)] * 3
        + [
            sds((HALF, HALF), BF16),
            sds((HALF, HALF), BF16),
            sds((8, HALF), F32),
            sds((half, D), BF16),
            sds((half, D), BF16),
        ],
        grid_spec=pltpu.PrefetchScalarGridSpec(
            num_scalar_prefetch=1,
            grid=(PAIRS,),
            in_specs=[
                whole((half, D)),
                whole((half, D)),
                out_rows,
                out_rows,
                rows,
                rows,
                rows,
                part,
                part,
                whole((half, D)),
                whole((half, D)),
                weight_block(0),
                weight_block(1),
                weight_block(2),
                whole((1, tokens)),
            ],
            out_specs=[weight] * 3
            + [
                pl.BlockSpec((LANES, HALF), lambda p, core: (p, 0)),
                pl.BlockSpec((LANES, HALF), lambda p, core: (p, 0)),
                pl.BlockSpec((8, LANES), col),
                whole((half, D)),
                whole((half, D)),
            ],
            scratch_shapes=[
                pltpu.VMEM((tokens, D), F32),
                pltpu.VMEM((tokens, 3 * LANES), BF16),
                pltpu.VMEM((D, tokens), BF16),
            ],
        ),
        compiler_params=params(),
        cost_estimate=cost(
            8 * tokens * D * 3 * HALF // 2 + 10 * PAIRS * 2 * tokens * tokens * LANES,
            2 * (4 * tokens * D + 8 * D * HALF + 4 * tokens * HALF),
            PAIRS * 2 * tokens * tokens,
        ),
    )(core, dao, das, wom, wot, q, k, v, mo, ms, xo, xs, wa, wa, wa, mask)


def norm_rows(h, gain, shift, y, yb, n, rstd):
    mean = jnp.mean(h, axis=-1, keepdims=True)
    centred = h - mean
    scale = lax.rsqrt(jnp.mean(centred * centred, axis=-1, keepdims=True) + EPS)
    normal = centred * scale
    out = normal * gain + shift
    y[...] = out
    yb[...] = out.astype(BF16)
    n[...] = normal
    rstd[...] = scale


def norm_outs(half):
    return [sds((half, D), F32), sds((half, D), BF16), sds((half, D), F32), sds((half, 1), F32)]


def out_norm_kernel(core, mine, theirs, wom, wot, base, small, y, yb, n, rstd, *, layer):
    mine_rows, their_rows = halves(core)
    near = dot(mine[...], wom[mine_rows, :]) + dot(theirs[...], wom[their_rows, :])
    far = dot(mine[...], wot[mine_rows, :]) + dot(theirs[...], wot[their_rows, :])
    first = core[0] == 0
    mixed = jnp.concatenate([jnp.where(first, near, far), jnp.where(first, far, near)], axis=1)
    h = base[...] + mixed + small[ROW_OUT + layer : ROW_OUT + layer + 1, :]
    row = 2 * layer
    norm_rows(
        h, small[ROW_GAIN + row : ROW_GAIN + row + 1, :], small[ROW_SHIFT + row : ROW_SHIFT + row + 1, :],
        y, yb, n, rstd,
    )


def out_norm(core, mine, theirs, wom, wot, base, small, layer):
    half = base.shape[0]
    return pl.pallas_call(
        functools.partial(out_norm_kernel, layer=layer),
        name="out_norm",
        out_shape=norm_outs(half),
        in_specs=[pl.BlockSpec(memory_space=pltpu.SMEM)] + [pl.BlockSpec(memory_space=pltpu.VMEM)] * 6,
        out_specs=[pl.BlockSpec(memory_space=pltpu.VMEM)] * 4,
        compiler_params=params(),
        cost_estimate=cost(2 * half * D * D, 2 * D * D + 16 * half * D),
    )(core, mine, theirs, wom, wot, base, small)


def add_norm_kernel(base, part, recv, small, y, yb, n, rstd, *, layer):
    h = base[...] + part[...].astype(F32) + recv[...].astype(F32) + small[ROW_DOWN + layer : ROW_DOWN + layer + 1, :]
    row = 2 * layer + 1
    norm_rows(
        h, small[ROW_GAIN + row : ROW_GAIN + row + 1, :], small[ROW_SHIFT + row : ROW_SHIFT + row + 1, :],
        y, yb, n, rstd,
    )


def add_norm(base, part, recv, small, layer):
    half = base.shape[0]
    return pl.pallas_call(
        functools.partial(add_norm_kernel, layer=layer),
        name="add_norm",
        out_shape=norm_outs(half),
        in_specs=[pl.BlockSpec(memory_space=pltpu.VMEM)] * 4,
        out_specs=[pl.BlockSpec(memory_space=pltpu.VMEM)] * 4,
        compiler_params=params(),
        cost_estimate=cost(20 * half * D, 20 * half * D),
    )(base, part, recv, small)


def norm_bwd_kernel(*refs, row, summed):
    if summed:
        base, part, recv, n, rstd, small, gh, ghb, sums = refs
        gz = base[...] + part[...].astype(F32) + recv[...].astype(F32)
    else:
        base, live, n, rstd, small, gh, ghb, sums = refs
        gz = base[...].astype(F32) * live[...]
    normal = n[...]
    e = gz * small[ROW_GAIN + row : ROW_GAIN + row + 1, :]
    mean = jnp.mean(e, axis=-1, keepdims=True)
    slope = jnp.mean(e * normal, axis=-1, keepdims=True)
    grad = (e - mean - normal * slope) * rstd[...]
    low = grad.astype(BF16)
    gh[...] = grad
    ghb[...] = low
    sums[...] = jnp.zeros_like(sums)
    sums[0:1, :] = jnp.sum(gz * normal, axis=0, keepdims=True)
    sums[1:2, :] = jnp.sum(gz, axis=0, keepdims=True)
    sums[2:3, :] = jnp.sum(low.astype(F32), axis=0, keepdims=True)


def norm_bwd(sources, n, rstd, small, row):
    half = n.shape[0]
    operands = tuple(sources) + (n, rstd, small)
    return pl.pallas_call(
        functools.partial(norm_bwd_kernel, row=row, summed=len(sources) == 3),
        name="norm_bwd",
        out_shape=[sds((half, D), F32), sds((half, D), BF16), sds((8, D), F32)],
        in_specs=[pl.BlockSpec(memory_space=pltpu.VMEM)] * len(operands),
        out_specs=[pl.BlockSpec(memory_space=pltpu.VMEM)] * 3,
        compiler_params=params(),
        cost_estimate=cost(20 * half * D, 20 * half * D),
    )(*operands)


FF_BLOCK = 768
FF_STEPS = FF // CORES // FF_BLOCK


def ffn_fwd_kernel(yo, ys, w1, bias, w2, act, slope, po, ps, acc, *, layer):
    half = yo.shape[0]
    j = pl.program_id(0)
    for first, rows in ((0, yo), (half, ys)):
        span = slice(first, first + half)
        up = dot(rows[...], w1[...]) + bias[layer : layer + 1, :]
        cdf = 0.5 * (1.0 + lax.erf(up * (2.0**-0.5)))
        low = (up * cdf).astype(BF16)
        act[span, :] = low
        slope[span, :] = (cdf + up * (jnp.exp(-0.5 * up * up) * 0.3989422804014327)).astype(BF16)
        total = dot(low, w2[...])

        @pl.when(j == 0)
        def _():
            acc[span, :] = total

        @pl.when(j > 0)
        def _():
            acc[span, :] += total

    @pl.when(j == FF_STEPS - 1)
    def _():
        po[...] = acc[:half, :].astype(BF16)
        ps[...] = acc[half:, :].astype(BF16)


DOWN_STEPS = D // FF_BLOCK


def ffn_specs(tokens, col):
    return (
        pl.BlockSpec((D, FF_BLOCK), lambda j: (0, j)),
        pl.BlockSpec((FF_BLOCK, D), lambda j: (j % DOWN_STEPS, col // D + j // DOWN_STEPS)),
        pl.BlockSpec((tokens, FF_BLOCK), lambda j: (0, j)),
    )


def ffn_fwd(yo, ys, w1, w2, col, bias, layer):
    half = yo.shape[0]
    tokens = 2 * half
    width = FF // CORES
    cols, down, rows = ffn_specs(tokens, col)
    return pl.pallas_call(
        functools.partial(ffn_fwd_kernel, layer=layer),
        name="ffn_fwd",
        out_shape=[sds((tokens, width), BF16)] * 2 + [sds((half, D), BF16)] * 2,
        grid=(FF_STEPS,),
        in_specs=[
            whole((half, D)),
            whole((half, D)),
            cols,
            pl.BlockSpec((LAYERS, FF_BLOCK), lambda j: (0, j)),
            down,
        ],
        out_specs=[rows] * 2 + [whole((half, D))] * 2,
        scratch_shapes=[pltpu.VMEM((tokens, D), F32)],
        compiler_params=params(),
        cost_estimate=cost(4 * tokens * D * width, 4 * D * width + 4 * tokens * width, tokens * width),
    )(yo, ys, w1, bias, w2)


def ffn_bwd_kernel(dfo, dfs, w1, w2, act, slope, yo, ys, dw1, dw2, sums, po, ps, acc, du, turned):
    half = yo.shape[0]
    j = pl.program_id(0)

    @pl.when(j == 0)
    def _():
        turned[:, :half] = yo[...].T
        turned[:, half:] = ys[...].T

    for first, rows in ((0, dfo), (half, dfs)):
        span = slice(first, first + half)
        low = (slope[span, :].astype(F32) * dot(rows[...], w2[...], NT)).astype(BF16)
        du[span, :] = low
        total = dot(low, w1[...], NT)

        @pl.when(j == 0)
        def _():
            acc[span, :] = total

        @pl.when(j > 0)
        def _():
            acc[span, :] += total

    sums[...] = jnp.zeros_like(sums)
    sums[0:1, :] = jnp.sum(du[...].astype(F32), axis=0, keepdims=True)
    dw1[...] = dot(turned[...], du[...]).astype(BF16)
    dw2[...] = (dot(act[:half, :], dfo[...], TN) + dot(act[half:, :], dfs[...], TN)).astype(BF16)

    @pl.when(j == FF_STEPS - 1)
    def _():
        po[...] = acc[:half, :].astype(BF16)
        ps[...] = acc[half:, :].astype(BF16)


def ffn_bwd(dfo, dfs, w1, w2, col, act, slope, yo, ys):
    half = yo.shape[0]
    tokens = 2 * half
    width = FF // CORES
    cols, down, rows = ffn_specs(tokens, col)
    return pl.pallas_call(
        ffn_bwd_kernel,
        name="ffn_bwd",
        out_shape=[
            sds((2, D, D), BF16),
            sds((2, D, D), BF16),
            sds((8, width), F32),
            sds((half, D), BF16),
            sds((half, D), BF16),
        ],
        grid=(FF_STEPS,),
        in_specs=[whole((half, D))] * 2 + [cols, down, rows, rows] + [whole((half, D))] * 2,
        out_specs=[
            pl.BlockSpec((None, D, FF_BLOCK), lambda j: (j // DOWN_STEPS, 0, j % DOWN_STEPS)),
            pl.BlockSpec((None, FF_BLOCK, D), lambda j: (j // DOWN_STEPS, j % DOWN_STEPS, 0)),
            pl.BlockSpec((8, FF_BLOCK), lambda j: (0, j)),
        ]
        + [whole((half, D))] * 2,
        scratch_shapes=[
            pltpu.VMEM((tokens, D), F32),
            pltpu.VMEM((tokens, FF_BLOCK), BF16),
            pltpu.VMEM((D, tokens), BF16),
        ],
        compiler_params=params(),
        cost_estimate=cost(8 * tokens * D * width, 8 * D * width + 4 * tokens * width),
    )(dfo, dfs, w1, w2, act, slope, yo, ys)


def shuffle_kernel(table, *refs, moves, count):
    for out, to, to_col, source, at, at_col, width in moves:
        to = table[to[0]] if isinstance(to, list) else to
        at = table[at[0]] if isinstance(at, list) else at
        ref, cols = refs[source], slice(at_col, at_col + width)
        rows = refs[count + out].shape[1]
        block = ref[at : at + rows, cols] if len(ref.shape) == 2 else ref[at, :, cols]
        refs[count + out][to, :, to_col : to_col + width] = block


def shuffle(table, sources, shapes, moves):
    nbytes = sum(4 * source.size for source in sources)
    return pl.pallas_call(
        functools.partial(shuffle_kernel, moves=moves, count=len(sources)),
        name="shuffle",
        out_shape=shapes,
        in_specs=[pl.BlockSpec(memory_space=pltpu.SMEM)]
        + [pl.BlockSpec(memory_space=pltpu.VMEM)] * len(sources),
        out_specs=[pl.BlockSpec(memory_space=pltpu.VMEM)] * len(shapes),
        compiler_params=params(),
        cost_estimate=cost(0, nbytes),
    )(table, *sources)


def pack_kernel(core, qkv, out, up, mine, send):
    chips = FF // (2 * CORES * FF_CHUNK)
    ups = up[0].astype(F32)
    parts = []
    for parity in range(CORES):
        starts = [
            ((chip * CORES + parity) * 2 + part) * FF_CHUNK for part in range(2) for chip in range(chips)
        ]
        parts.append(jnp.concatenate([ups[:, start : start + FF_CHUNK] for start in starts], axis=1))
    even = core[0] == 0
    for ref, cols, ff in (
        (mine, halves(core)[0], jnp.where(even, parts[0], parts[1])),
        (send, halves(core)[1], jnp.where(even, parts[1], parts[0])),
    ):
        for part in range(3):
            whole_part = qkv.at[0, :, part * D : (part + 1) * D]
            ref[:, part * HALF : (part + 1) * HALF] = whole_part[:, cols]
        ref[:, 3 * HALF : 4 * HALF] = out.at[0][:, cols]
        ref[:, 4 * HALF :] = ff.astype(BF16)


FF_CHUNK = 48
PACKED = 4 * HALF + FF // CORES


def layer_block(shape, layer):
    return pl.BlockSpec((1,) + shape, lambda *_: (layer, 0, 0))


def pack(core, attn_in, attn_out, ffn_in, layer):
    rows = attn_in.shape[1]
    return pl.pallas_call(
        pack_kernel,
        name="pack",
        out_shape=[sds((rows, PACKED), BF16)] * 2,
        grid=(1,),
        in_specs=[
            pl.BlockSpec(memory_space=pltpu.SMEM),
            layer_block((rows, 3 * D), layer),
            layer_block((rows, D), layer),
            layer_block((rows, FF), layer),
        ],
        out_specs=[whole((rows, PACKED))] * 2,
        compiler_params=params(),
        cost_estimate=cost(0, 8 * rows * PACKED),
    )(core, attn_in, attn_out, ffn_in)


def join_kernel(core, mine, recv, down, *outs):
    rows = mine.shape[0]
    even = core[0] == 0
    near, far = mine[...].astype(F32), recv[...].astype(F32)
    both = jnp.concatenate([jnp.where(even, near, far), jnp.where(even, far, near)], axis=0).astype(BF16)
    downs = [down[0, part * CORES * rows : (part + 1) * CORES * rows, :] for part in range(2)]
    attn, ffn = outs
    for unit in range(2):
        attn[unit] = both[:, unit * D : (unit + 1) * D]
        ffn[2 * unit] = both[:, (2 + unit) * D : (3 + unit) * D]
        ffn[2 * unit + 1] = downs[unit]


def join(core, mine, recv, ffn_out, layer, shapes):
    rows = mine.shape[0]
    down = ffn_out.shape[1]
    return pl.pallas_call(
        join_kernel,
        name="join",
        out_shape=[sds(shape, BF16) for shape in shapes],
        grid=(1,),
        in_specs=[
            pl.BlockSpec(memory_space=pltpu.SMEM),
            whole((rows, PACKED)),
            whole((rows, PACKED)),
            layer_block((down, D), layer),
        ],
        out_specs=[whole(shape) for shape in shapes],
        compiler_params=params(),
        cost_estimate=cost(0, 8 * rows * PACKED),
    )(core, mine, recv, ffn_out)


def split_kernel(core, *refs):
    mine, send = refs[-2:]
    rows = mine.shape[0]
    even = core[0] == 0
    for part, block in enumerate(refs[:-2]):
        top, bottom = block[:rows, :], block[rows:, :]
        mine[:, part * D : (part + 1) * D] = jnp.where(even, top, bottom)
        send[:, part * D : (part + 1) * D] = jnp.where(even, bottom, top)


def split(core, units):
    rows = units[0].shape[0] // CORES
    return pl.pallas_call(
        split_kernel,
        name="split",
        out_shape=[sds((rows, PACKED), F32)] * 2,
        in_specs=[pl.BlockSpec(memory_space=pltpu.SMEM)] + [pl.BlockSpec(memory_space=pltpu.VMEM)] * len(units),
        out_specs=[pl.BlockSpec(memory_space=pltpu.VMEM)] * 2,
        compiler_params=params(),
        cost_estimate=cost(0, 16 * rows * PACKED),
    )(core, *units)


def merge_kernel(core, *refs):
    qkv, out, up, down = refs[4 * LAYERS :]
    chips = FF // (2 * CORES * FF_CHUNK)
    even = core[0] == 0
    for layer in range(LAYERS):
        mine, recv, first_down, second_down = refs[4 * layer : 4 * layer + 4]
        near, far = mine[...], recv[...]
        first, second = jnp.where(even, near, far), jnp.where(even, far, near)
        for part in range(3):
            span = slice(part * HALF, (part + 1) * HALF)
            qkv[layer, :, part * D : part * D + HALF] = first[:, span]
            qkv[layer, :, part * D + HALF : (part + 1) * D] = second[:, span]
        out[layer, :, :HALF] = first[:, 3 * HALF : 4 * HALF]
        out[layer, :, HALF:] = second[:, 3 * HALF : 4 * HALF]
        chunks = []
        for chip in range(chips):
            for source in (first, second):
                for part in range(2):
                    start = 4 * HALF + part * D + chip * FF_CHUNK
                    chunks.append(source[:, start : start + FF_CHUNK])
        up[layer] = jnp.concatenate(chunks, axis=1)
        rows = first_down.shape[0]
        down[layer, :rows, :] = first_down[...]
        down[layer, rows:, :] = second_down[...]


def merge(core, parts):
    rows = parts[0].shape[0]
    down = 2 * parts[2].shape[0]
    return pl.pallas_call(
        merge_kernel,
        name="merge",
        out_shape=[
            sds((LAYERS, rows, 3 * D), F32),
            sds((LAYERS, rows, D), F32),
            sds((LAYERS, rows, FF), F32),
            sds((LAYERS, down, D), F32),
        ],
        in_specs=[pl.BlockSpec(memory_space=pltpu.SMEM)] + [pl.BlockSpec(memory_space=pltpu.VMEM)] * len(parts),
        out_specs=[pl.BlockSpec(memory_space=pltpu.VMEM)] * 4,
        compiler_params=params(),
        cost_estimate=cost(0, 32 * rows * PACKED),
    )(core, *parts)


class Places:
    def __init__(self, pages, bands):
        self.ny = bands // CORES
        self.nx = self.ny if pages % self.ny == 0 else 1
        self.nz = pages // self.nx
        self.chips = pages * self.ny
        page, band = lax.axis_index("page"), lax.axis_index("band")
        self.z, self.x = page // self.nx, page % self.nx
        self.y, self.core = band // CORES, band % CORES
        self.sizes = (self.nz, self.nx, self.ny, CORES)

    def move(self, value, axis, step, flip=False):
        pairs = []
        nz, nx, ny, nc = self.sizes
        for device in range(nz * nx * ny * nc):
            place = [device // (nx * ny * nc), device // (ny * nc) % nx, device // nc % ny, device % nc]
            place[axis] = place[axis] ^ step if flip else (place[axis] + step) % self.sizes[axis]
            pairs.append((device, ((place[0] * nx + place[1]) * ny + place[2]) * nc + place[3]))
        return lax.ppermute(value, ("page", "band"), pairs)

    def payloads(self, wants):
        keys = []
        for axis, step, _ in wants:
            keys.append((axis, step if axis == 0 else step % self.sizes[axis]))
        merged, places = {}, [None] * len(wants)
        for key in dict.fromkeys(keys):
            numbers = [i for i, other in enumerate(keys) if other == key]
            flat = [wants[i][2].reshape(-1, wants[i][2].shape[-1]) for i in numbers]
            merged[key] = jnp.concatenate(flat) if len(flat) > 1 else flat[0]
            first = 0
            for i, part in zip(numbers, flat):
                places[i] = (key, first, wants[i][2].shape)
                first += part.shape[0]
        return merged, places

    def swap(self, value):
        return self.move(value, 3, 1)

    def chip_of(self, kz, kx, ky):
        z, x, y = self.z ^ kz, (self.x - kx) % self.nx, (self.y - ky) % self.ny
        return (z * self.nx + x) * self.ny + y

    def flips(self):
        return [1 << bit for bit in reversed(range(self.nz.bit_length() - 1))]


def tie(values, *others):
    return lax.optimization_barrier((values, others))[0]


class Gather:
    def __init__(self, at, local, shapes, place):
        self.at, self.local = at, local
        self.half = local.shape[0] // 2
        self.shapes, self.place = shapes, place
        self.stages = [functools.partial(self.flip, step) for step in at.flips()]
        self.stages += [self.first, self.second]
        self.held = local[None]
        self.spots = [0]

    def flip(self, step, got):
        if got:
            self.held = jnp.concatenate([self.held] + list(got))
        self.spots = self.spots + [spot ^ step for spot in self.spots]
        return [(0, step, self.held)]

    def near(self, axis, part):
        return [(axis, k, part) for k in range(1, self.at.sizes[axis])]

    def first(self, got):
        held = jnp.concatenate([self.held] + list(got))
        self.sent = [held[:, : self.half], held[:, self.half :]]
        return self.near(1, self.sent[0]) + self.near(2, self.sent[1])

    def second(self, got):
        cut = self.at.nx - 1
        self.sent = [jnp.stack([part] + got) for part, got in zip(self.sent, (got[:cut], got[cut:]))]
        return self.near(2, self.sent[0]) + self.near(1, self.sent[1])

    def finish(self, got, mine):
        at = self.at
        rows = self.local.shape[1]
        sources, moves, table = [], [], []
        cut = at.ny - 1
        for axes, pieces, start in (
            ((1, 2), mine[:1] + got[:cut], 0),
            ((2, 1), mine[cut : cut + 1] + got[cut:], self.half),
        ):
            for far, piece in enumerate(pieces):
                source, spot, stride = piece.source(sources, rows)
                for near in range(at.sizes[axes[0]]):
                    kx, ky = (near, far) if axes[0] == 1 else (far, near)
                    for kz in self.spots:
                        chip = at.chip_of(kz, kx, ky)
                        for unit in range(start, start + self.half):
                            for out, step, offset, to_col, at_col, width in self.place[unit]:
                                moves.append((out, [len(table)], to_col, source, spot, at_col, width))
                                table.append(chip * step + offset)
                            spot += stride
        outs = shuffle(jnp.stack(table), sources, [sds(shape, BF16) for shape in self.shapes], moves)
        return [out.reshape(-1, out.shape[-1]) for out in outs]


class LateGather(Gather):
    def __init__(self, at, local, shapes, place, idle):
        self.at, self.local = at, local
        self.half = local.shape[0] // 2
        self.shapes, self.place = shapes, place
        self.stages = [self.first, self.second] + [self.rest] * idle
        self.stages += [functools.partial(self.flip, step) for step in at.flips()]
        self.spots = [0]
        self.got = None

    def first(self, got):
        self.sent = [self.local[None, : self.half], self.local[None, self.half :]]
        return self.near(1, self.sent[0]) + self.near(2, self.sent[1])

    def rest(self, got):
        if got:
            self.got = got
        return []

    def flip(self, step, got):
        if self.got is not None:
            got = self.got
        if len(self.spots) == 1:
            cut = self.at.ny - 1
            self.held = jnp.concatenate(
                [jnp.stack([part] + list(other)).reshape((-1,) + part.shape[-3:])
                 for part, other in zip(self.sent, (got[:cut], got[cut:]))],
                axis=1,
            )[None]
        else:
            self.held = jnp.concatenate([self.held] + list(got))
        self.got = None
        self.spots = self.spots + [spot ^ step for spot in self.spots]
        return [(0, step, self.held)]

    def finish(self, got, mine):
        at = self.at
        rows = self.local.shape[1]
        sources, moves, table = [], [], []
        spots = len(self.spots) // 2
        for number, piece in enumerate((mine[0], got[0])):
            source, block, stride = piece.source(sources, rows)
            for spot in self.spots[number * spots : (number + 1) * spots]:
                for far in range(at.nx):
                    for near in range(at.ny):
                        for unit in range(2 * self.half):
                            kx, ky = (near, far) if unit < self.half else (far, near)
                            for out, step, offset, to_col, at_col, width in self.place[unit]:
                                moves.append((out, [len(table)], to_col, source, block, at_col, width))
                                table.append(at.chip_of(spot, kx, ky) * step + offset)
                            block += stride
        outs = shuffle(jnp.stack(table), sources, [sds(shape, BF16) for shape in self.shapes], moves)
        return [out.reshape(-1, out.shape[-1]) for out in outs]


class Reduce:
    def __init__(self, at, first, second):
        self.at, self.halves = at, (first, second)
        self.stages = [self.first, self.second]
        self.stages += [functools.partial(self.flip, number) for number in range(len(at.flips()))]

    def picked(self, groups, axis, index):
        at = self.at
        rows = []
        for group in groups:
            parts = []
            for part in group:
                blocks = part.reshape(at.nz, at.nx, at.ny, part.shape[0] // at.chips, part.shape[1])
                parts.append(pick(blocks, index, axis))
            rows.append(jnp.concatenate(parts, axis=-1) if len(parts) > 1 else parts[0])
        return jnp.concatenate(rows, axis=2) if len(rows) > 1 else rows[0]

    def first(self, got):
        at = self.at
        wants = [(2, -k, self.picked(self.halves[0], 2, (at.y - k) % at.ny)) for k in range(1, at.ny)]
        return wants + [
            (1, -k, self.picked(self.halves[1], 1, (at.x - k) % at.nx)) for k in range(1, at.nx)
        ]

    def second(self, got):
        at = self.at
        cut = at.ny - 1
        self.lows = []
        for mine, other in (
            (self.picked(self.halves[0], 2, at.y), got[:cut]),
            (self.picked(self.halves[1], 1, at.x), got[cut:]),
        ):
            self.lows.append(self.total(mine, other).astype(BF16))
        wants = [(1, -k, pick(self.lows[0], (at.x - k) % at.nx, 1)) for k in range(1, at.nx)]
        return wants + [(2, -k, pick(self.lows[1], (at.y - k) % at.ny, 1)) for k in range(1, at.ny)]

    def total(self, mine, other):
        mine = mine.astype(F32)
        for term in other:
            mine = mine + term.astype(F32)
        return mine

    def flip(self, number, got):
        at = self.at
        bit = 1 << number
        if number == 0:
            cut = at.nx - 1
            first = self.total(pick(self.lows[0], at.x, 1), got[:cut])
            second = self.total(pick(self.lows[1], at.y, 1), got[cut:])
            self.cut = first.shape[1]
            low = jnp.concatenate([first, second], axis=1).astype(BF16)
        else:
            low = self.total(self.low, got).astype(BF16)
        low = low.reshape((low.shape[0] // 2, 2) + low.shape[1:])
        side = at.z // bit % 2
        self.low = pick(low, side, 1)
        return [(0, bit, pick(low, 1 - side, 1))]

    def finish(self, got):
        total = self.total(self.low, got)[0]
        return total[: self.cut], total[self.cut :]


class Piece:
    def __init__(self, array, first, shape):
        self.array, self.first, self.shape = array, first, shape

    def value(self):
        rows = math.prod(self.shape[:-1])
        return self.array[self.first : self.first + rows].reshape(self.shape)

    def source(self, sources, rows):
        if rows % 16:
            sources.append(self.value().reshape(-1, rows, self.shape[-1]))
            return len(sources) - 1, 0, 1
        for number, array in enumerate(sources):
            if array is self.array:
                return number, self.first, rows
        sources.append(self.array)
        return len(sources) - 1, self.first, rows


class Line:
    def __init__(self, at):
        self.at, self.chunks, self.age, self.got, self.mine = at, [], [], [], []

    def add(self, chunk):
        self.chunks.append(chunk)
        self.age.append(0)
        self.got.append([])
        self.mine.append([])

    def step(self, *others, extra=None):
        wants, spans = [], []
        for number, chunk in enumerate(self.chunks):
            if self.age[number] < len(chunk.stages):
                new = chunk.stages[self.age[number]]([piece.value() for piece in self.got[number]])
                spans.append((number, len(wants), len(wants) + len(new)))
                wants += new
                self.age[number] += 1
        merged, self.places = self.at.payloads(wants)
        values, others = lax.optimization_barrier((list(merged.values()), others))
        merged = dict(zip(merged, values))
        self.moved = {key: self.at.move(value, *key, flip=key[0] == 0) for key, value in merged.items()}
        self.spans = spans
        for number, start, stop in spans:
            self.mine[number] = [Piece(merged[key], *place) for key, *place in self.places[start:stop]]
        return others

    def close(self, *others):
        self.moved, others = lax.optimization_barrier((self.moved, others))
        for number, start, stop in self.spans:
            self.got[number] = [Piece(self.moved[key], *place) for key, *place in self.places[start:stop]]
        return others

    def busy(self):
        return not all(self.done(chunk) for chunk in self.chunks)

    def done(self, chunk):
        number = self.chunks.index(chunk)
        return self.age[number] == len(chunk.stages)

    def fresh(self, chunk):
        return self.done(chunk) and any(span[0] == self.chunks.index(chunk) for span in self.spans)

    def result(self, chunk):
        number = self.chunks.index(chunk)
        if isinstance(chunk, Gather):
            return chunk.finish(self.got[number], self.mine[number])
        return chunk.finish([piece.value() for piece in self.got[number]])


def blocks_kernel(scalars, *refs, counts, loads, jobs):
    sources, outs = refs[: counts[0]], refs[counts[0] : counts[0] + counts[1]]
    buffers = refs[counts[0] + counts[1] : -2]
    load_sems, out_sems = refs[-2:]

    def rows(place, height):
        start, slopes = place
        for number, slope in slopes:
            start = start + scalars[number] * slope
        return pl.ds(pl.multiple_of(start, 16) if slopes else start, height)

    copies = []
    for number, (source, place, height, buffer, row, col, width) in enumerate(loads):
        copies.append(
            pltpu.make_async_copy(
                sources[source].at[rows(place, height), :],
                buffers[buffer].at[row : row + height, col : col + width],
                load_sems.at[number],
            )
        )
    for copy in copies:
        copy.start()
    waited = set()

    def wait(numbers):
        for number in numbers:
            if number not in waited:
                waited.add(number)
                copies[number].wait()

    stores = []
    for out, (needs, sums) in enumerate(jobs):
        for to, height, terms in sums:
            total = None
            for buffer, place, numbers in terms:
                wait(numbers)
                value = buffers[buffer][rows(place, height), :].astype(buffers[out].dtype)
                total = value if total is None else total + value
            buffers[out][to : to + height, :] = total.astype(buffers[out].dtype)
        wait(needs)
        stores.append(pltpu.make_async_copy(buffers[out], outs[out], out_sems.at[out]))
        stores[-1].start()
    for store in stores:
        store.wait()


class Stream:
    def __init__(self, parts, first_y, rows, base=0, direct=False):
        self.parts, self.first_y, self.rows, self.base = parts, first_y, rows, base
        self.age, self.direct, self.last = 0, direct, False
        self.keep = self.recv = self.total = self.joined = None


class Joined:
    def __init__(self, streams):
        self.streams, self.out, self.total = streams, None, None
        self.rows = sum(stream.rows for stream in streams)
        for stream in streams:
            stream.joined = self

    def start(self, stream):
        return sum(other.rows for other in self.streams[: self.streams.index(stream)])


class Pipe:
    def __init__(self, at):
        self.at, self.groups = at, []
        self.bits = at.nz.bit_length() - 1
        scalars = [at.x, at.y] + [at.z // (1 << bit) % 2 for bit in range(self.bits)]
        self.scalars = jnp.stack(scalars).astype(jnp.int32)

    def add(self, streams):
        self.groups.append(streams)

    def pieces(self, stream, rows):
        nz = self.at.nz
        first = 1 if stream.first_y else 0
        strides = (2, 1)

        def chip(z, coords):
            start, slopes = stream.base + 4 * z * rows, []
            for axis, (fixed, slope) in enumerate(coords):
                start += fixed * strides[axis] * rows
                if slope:
                    slopes.append((axis, slope * strides[axis] * rows))
            return start, slopes

        def spot(fixed, number, slope, scale, base=0):
            return (base + fixed * scale, [(number, slope * scale)])

        other, same = (1, -1), (0, 1)
        sent, kept = [], []
        if stream.age == 0:
            for z in range(nz):
                for far in range(2):
                    coords = [None, None]
                    coords[first], coords[1 - first] = other, (far, 0)
                    sent.append([(stream.parts, chip(z, coords))])
        elif stream.age == 1:
            ((ref, base),) = stream.recv
            for out, side in ((sent, other), (kept, same)):
                for z in range(nz):
                    coords = [None, None]
                    coords[first], coords[1 - first] = same, side
                    place = spot(2 * z + side[0], 1 - first, side[1], rows, base)
                    out.append([(stream.parts, chip(z, coords)), ([ref], place)])
        elif stream.direct and stream.age == 2:
            ((ref, base),) = stream.recv
            for flip in range(nz):
                start, slopes = 0, []
                for bit in range(self.bits):
                    fixed, slope = other if flip >> bit & 1 else same
                    start += (fixed << bit) * rows
                    slopes.append((2 + bit, (slope << bit) * rows))
                out = sent if flip else kept
                out.append([([stream.keep], (start, slopes)), ([ref], (base + start, slopes))])
        elif not self.final(stream):
            bit = stream.age - 2
            ((ref, base),) = stream.recv
            for out, side in ((sent, other), (kept, same)):
                for high in range(nz >> (bit + 1)):
                    fixed = 2 * high + side[0]
                    keep = spot(fixed, 2 + bit, side[1], rows)
                    out.append([([stream.keep], keep), ([ref], spot(fixed, 2 + bit, side[1], rows, base))])
        else:
            kept.append([([stream.keep], (0, []))] + [([ref], (base, [])) for ref, base in stream.recv])
        return sent, kept

    def final(self, stream):
        return stream.age == (3 if stream.direct else 2 + self.bits)

    def step(self, *others, extra=None):
        heights, keeps, todo, self.sent = {}, [], [], []
        spots, self.joined = [], None
        for streams in self.groups:
            for stream in streams:
                if stream.last:
                    continue
                rows = stream.rows
                sent, kept = self.pieces(stream, rows)
                axis = (2, 1) if stream.first_y else (1, 2)
                blocks, spans = [], []
                if stream.age < 2:
                    spans = [(axis[stream.age], len(sent))]
                elif sent:
                    spans = [(-flip, 1) for flip in range(1, len(sent) + 1)]
                    if not stream.direct:
                        spans = [(-(1 << (stream.age - 2)), len(sent))]
                for key, many in spans:
                    start = heights.get(key, 0)
                    heights[key] = start + many * rows
                    self.sent.append((stream, key, start))
                    blocks += [(key, start + block * rows) for block in range(many)]
                todo.append((stream, blocks, sent, kept, rows))
        if extra is not None:
            span = (heights.get(2, 0), extra.shape[0])
            heights[2] = sum(span)
        order = list(heights)
        shapes = [sds((heights[key], D), BF16) for key in order]
        jobs = [([], []) for _ in order]
        arrays, loads, buffers, held = [], [], [], {}

        def source(array):
            for i, known in enumerate(arrays):
                if known is array:
                    return i
            arrays.append(array)
            return len(arrays) - 1

        for stream, blocks, sent, kept, rows in todo:
            if kept:
                last = self.final(stream)
                if last and stream.joined is not None:
                    if stream.joined.out is None:
                        stream.joined.out = len(shapes)
                        shapes.append(sds((stream.joined.rows, D), F32))
                        jobs.append(([], []))
                        self.joined = stream.joined
                    spots.append((stream.joined.out, stream.joined.start(stream)))
                    continue
                keeps.append((stream, len(shapes)))
                spots.append((len(shapes), 0))
                shapes.append(sds((len(kept) * rows, D), F32 if last else BF16))
                jobs.append(([], []))
        buffers = list(shapes)
        if extra is not None:
            jobs[order.index(2)][0].append(len(loads))
            loads.append((source(extra), (0, []), span[1], order.index(2), span[0], 0, D))
        spare = len(buffers)
        buffers.append(None)
        spare_rows = 0

        def term(parts, place, height):
            nonlocal spare_rows
            if len(parts) == 1 and not any(part is parts[0] for part in stream.parts):
                array = source(parts[0])
                if array not in held:
                    held[array] = (len(buffers), len(loads))
                    loads.append((array, (0, []), parts[0].shape[0], len(buffers), 0, 0, D))
                    buffers.append(sds(parts[0].shape, parts[0].dtype))
                return held[array][0], place, [held[array][1]]
            row, numbers = spare_rows, []
            spare_rows += height
            for number, part in enumerate(parts):
                width = D // len(parts)
                numbers.append(len(loads))
                loads.append((source(part), place, height, spare, row, number * width, width))
            return spare, (row, []), numbers

        for stream, blocks, sent, kept, rows in todo:
            for (key, to), terms in zip(blocks, sent):
                out = order.index(key)
                if len(terms) == 1:
                    ((parts, place),) = terms
                    for number, part in enumerate(parts):
                        width = D // len(parts)
                        jobs[out][0].append(len(loads))
                        loads.append((source(part), place, rows, out, to, number * width, width))
                else:
                    jobs[out][1].append((to, rows, [term(parts, place, rows) for parts, place in terms]))
        spots = iter(spots)
        for stream, blocks, sent, kept, rows in todo:
            if kept:
                out, first = next(spots)
                for block, terms in enumerate(kept):
                    terms = [term(parts, place, rows) for parts, place in terms]
                    jobs[out][1].append((first + block * rows, rows, terms))
        buffers[spare] = sds((max(spare_rows, 16), D), BF16)
        outs = pl.pallas_call(
            functools.partial(
                blocks_kernel, counts=(len(arrays), len(shapes)), loads=loads, jobs=jobs
            ),
            name="blocks",
            out_shape=shapes,
            in_specs=[pl.BlockSpec(memory_space=pltpu.SMEM)]
            + [pl.BlockSpec(memory_space=pltpu.HBM)] * len(arrays),
            out_specs=[pl.BlockSpec(memory_space=pltpu.HBM)] * len(shapes),
            scratch_shapes=[pltpu.VMEM(buffer.shape, buffer.dtype) for buffer in buffers]
            + [pltpu.SemaphoreType.DMA((len(loads),)), pltpu.SemaphoreType.DMA((len(shapes),))],
            compiler_params=params(),
            cost_estimate=cost(0, sum(3 * array.size for array in arrays)),
        )(self.scalars, *arrays)
        if self.joined is not None:
            self.joined.total = outs[self.joined.out]
        for stream, out in keeps:
            stream.keep = outs[out]
            if self.final(stream):
                stream.total = outs[out]
        for stream, *_ in todo:
            stream.last = self.final(stream)
            stream.age += 1
        payloads, others = lax.optimization_barrier((outs[: len(order)], others))
        self.moved = {}
        self.span = None if extra is None else span
        for key, payload in zip(order, payloads):
            if key > 0:
                self.moved[key] = self.at.move(payload, key, 1)
            else:
                self.moved[key] = self.at.move(payload, 0, -key, flip=True)
        return others

    def close(self, *others):
        self.moved, others = lax.optimization_barrier((self.moved, others))
        for stream, key, start in self.sent:
            stream.recv = []
        for stream, key, start in self.sent:
            stream.recv.append((self.moved[key], start))
        if self.span is not None:
            self.extra = [self.moved[2][self.span[0] : sum(self.span)]]
        return others

    def busy(self):
        return not all(stream.last for streams in self.groups for stream in streams)


def pick(stacked, index, axis=0):
    return lax.dynamic_index_in_dim(stacked, index, axis, keepdims=False)


def by_core(core, mine, theirs, axis):
    return jnp.where(core == 0, jnp.stack([mine, theirs], axis), jnp.stack([theirs, mine], axis))


def body(
    hidden,
    boxes,
    page_size,
    band_count,
    layout_tables,
    attn_in,
    attn_bias,
    attn_out,
    out_bias,
    norm_gain,
    norm_bias,
    ffn_in,
    ffn_in_bias,
    ffn_out,
    ffn_out_bias,
    out_grad,
    *,
    pages,
    bands,
):
    at = Places(pages, bands)
    core = at.core
    core_id = core.astype(jnp.int32).reshape(1)
    devices = pages * bands
    ny, chips = at.ny, at.chips
    cap = hidden.shape[2]
    rows_dev = attn_in.shape[1]
    table_rows = layout_tables.shape[1]
    ff_dev = ffn_out.shape[1]
    chip_rows = CORES * rows_dev
    tiled = rows_dev % 8 == 0 and ff_dev == 2 * FF_CHUNK and at.nx == ny == 2

    def local_weights(layer):
        if tiled:
            mine, send = pack(core_id, attn_in, attn_out, ffn_in, layer)
            shapes = ((2, chip_rows, D), (4, chip_rows, D))
            return join(core_id, mine, at.swap(send), ffn_out, layer, shapes)
        columns = jnp.concatenate(
            [attn_in[layer].reshape(rows_dev, 3, CORES, HALF), attn_out[layer].reshape(rows_dev, 1, CORES, HALF)],
            axis=1,
        ).transpose(2, 0, 1, 3)
        ups = ffn_in[layer].reshape(rows_dev, chips, CORES, 2, ff_dev // 2).transpose(2, 0, 3, 1, 4)
        packed = jnp.concatenate(
            [columns.reshape(CORES, rows_dev, 4 * HALF), ups.reshape(CORES, rows_dev, FF // CORES)], axis=2
        )
        both = by_core(core, pick(packed, core), at.swap(pick(packed, 1 - core)), 0)
        both = both.reshape(chip_rows, PACKED)
        down = ffn_out[layer].reshape(2, chip_rows, D)
        both = both.reshape(chip_rows, 4, D).swapaxes(0, 1)
        return both[:2], jnp.stack([both[2], down[0], both[3], down[1]])

    attn_place = ([(0, 1, 0, 0, 0, D)], [(0, 1, 0, D, 0, D), (1, 1, 0, 0, HALF, HALF)])
    attn_shapes = ((chips, chip_rows, 2 * D), (chips, chip_rows, HALF))
    ffn_place = [[(0, 1, 0, col * D, 0, D)] for col in (0, 2, 1, 3)]
    ffn_shapes = ((chips, chip_rows, 4 * D),)
    table_place = [[(table, 1, 0, 0, 0, D)] for table in range(4)]
    table_shapes = ((chips, table_rows, D),) * 4

    def to_chip(stacked):
        own = [pick(stacked, at.y)]
        for k in range(1, ny):
            own.append(at.move(pick(stacked, (at.y + k) % ny), 2, k))
        return own

    def send_back(rows):
        parts = rows.reshape((ny, cap) + rows.shape[1:])
        return [at.move(parts[k].astype(BF16), 2, -k) for k in range(1, ny)]

    def from_chip(rows, back):
        back = [rows[:cap]] + [part.astype(F32) for part in back]
        back = jnp.stack(back)
        return jnp.stack([pick(back, (page - at.y) % ny) for page in range(ny)])[:, None]

    def token_facts(hidden, out_grad, boxes, page_size, band_count):
        widths, heights = page_size[0][:, None], page_size[1][:, None]
        left = boxes[0, :, 0] * GRID // widths
        top = boxes[1, :, 0] * GRID // heights
        right = boxes[2, :, 0] * GRID // widths
        bottom = boxes[3, :, 0] * GRID // heights
        live = (lax.broadcasted_iota(jnp.int32, left.shape, 1) < band_count).astype(jnp.int32)
        facts = jnp.stack([left, top, right, bottom, bottom - top, right - left, live, live], axis=1)
        facts_own = jnp.concatenate(to_chip(facts), axis=-1)
        facts_all = jnp.concatenate([facts_own, at.swap(facts_own)], axis=-1)
        owner = facts_all // table_rows
        index = jnp.where(
            owner % CORES == core, owner // CORES * table_rows + facts_all % table_rows, -1
        )
        mask = jnp.where(facts_all[6:7] > 0, 0.0, DEAD).astype(F32)
        live_own = facts_own[6].astype(F32)[:, None]
        hidden_own = jnp.concatenate(to_chip(hidden[:, 0]), axis=0)
        grad_own = jnp.concatenate(to_chip(out_grad[:, 0]), axis=0)
        return index, mask, live_own, hidden_own, grad_own

    cut = SMALL_ROWS * rows_dev

    def small_params(attn_bias, out_bias, norm_gain, norm_bias, ffn_out_bias, ffn_in_bias):
        segment = jnp.concatenate(
            [
                attn_bias.reshape(-1),
                out_bias.reshape(-1),
                norm_gain.reshape(-1),
                norm_bias.reshape(-1),
                ffn_out_bias.reshape(-1),
                ffn_in_bias.reshape(-1),
            ]
        )
        smalls = lax.all_to_all(
            jnp.broadcast_to(segment, (devices, segment.shape[0])), ("page", "band"), 0, 0, tiled=True
        ).astype(F32)
        small = smalls[:, :cut].reshape(devices, SMALL_ROWS, rows_dev).swapaxes(0, 1).reshape(SMALL_ROWS, D)
        up_bias = pick(smalls[:, cut:].reshape(chips, CORES, LAYERS, 2, ff_dev // 2), core, 1)
        up_bias = up_bias.transpose(1, 2, 0, 3).reshape(LAYERS, FF // CORES)
        return small, up_bias

    saved = [[], []]
    weights = [[], []]

    def look_up(state):
        tables = line.result(chunks[0])
        looked_up = embed(index.T, tables)
        mine = hidden_own.astype(F32) + looked_up[:half]
        x = mine + at.swap(looked_up[half:].astype(BF16)).astype(F32)
        return x, x.astype(BF16)

    def attend(layer, state):
        x, x_low = state
        wa, wom = line.result(chunks[1 + 2 * layer])
        wot, x_other = at.swap(wom), at.swap(x_low)
        weights[layer] += [wa, wom, wot]
        q, k, v, mix_own, mix_other = attn_fwd(core_id, x_low, x_other, wa, small, mask, layer)
        y1, y1_low, n1, r1 = out_norm(core_id, mix_own, at.swap(mix_other), wom, wot, x, small, layer)
        saved[layer] += [x_low, x_other, q, k, v, mix_own, mix_other, n1, r1]
        return y1, y1_low

    def feed(layer, state):
        y1, y1_low = state
        (w1,) = line.result(chunks[2 + 2 * layer])
        w2, col = (w1, 2 * D) if layer == 0 else (downs[0], 0)
        y1_other = at.swap(y1_low)
        weights[layer] += [w1, w2, col]
        act, slope, part, part_other = ffn_fwd(y1_low, y1_other, w1, w2, col, up_bias, layer)
        x, x_low, n2, r2 = add_norm(y1, part, at.swap(part_other), small, layer)
        saved[layer] += [y1_low, y1_other, act, slope, n2, r2]
        return x, x_low

    half = ny * cap
    line = Line(at)
    chunks = [Gather(at, layout_tables, table_shapes, table_place)]
    parts = [look_up]
    line.add(chunks[0])
    down_chunk = LateGather(
        at,
        ffn_out[LAYERS - 1].reshape(2, chip_rows, D),
        ((chips, chip_rows, 2 * D),),
        ([(0, 1, 0, 0, 0, D)], [(0, 1, 0, D, 0, D)]),
        3,
    )
    line.add(down_chunk)
    line.step()
    locals0 = local_weights(0)
    token_args = (hidden, out_grad, boxes, page_size, band_count)
    small_args = (attn_bias, out_bias, norm_gain, norm_bias, ffn_out_bias, ffn_in_bias)
    locals0, token_args = line.close(locals0, token_args)
    state, downs = (), []
    running = None
    waiting = []
    for layer in range(LAYERS):
        waiting += [(layer, 0), (layer, 1)]
        parts += [functools.partial(attend, layer), functools.partial(feed, layer)]
    local = locals0
    while waiting or running is not None or not line.done(chunks[-1]):
        if waiting:
            layer, number = waiting.pop(0)
            if layer > 0 and number == 0:
                local = local_weights(layer)
            if layer > 0 and number == 1:
                shard = jnp.stack([local[1][0], local[1][2]])
                shapes, place = ((chips, chip_rows, 2 * D),), ([(0, 1, 0, 0, 0, D)], [(0, 1, 0, D, 0, D)])
            else:
                shard = local[number]
                shapes, place = (attn_shapes, ffn_shapes)[number], (attn_place, ffn_place)[number]
            chunks.append(Gather(at, shard, shapes, place))
            line.add(chunks[-1])
        if all(line.done(chunk) for chunk in chunks):
            state = running(state)
            break
        state = line.step(*state)
        if line.done(down_chunk) and not downs and not line.fresh(down_chunk):
            downs.append(line.result(down_chunk)[0])
        if running is not None:
            state = running(state)
        if len(chunks) == 2:
            tokens, small_args, late = line.close(
                token_facts(*token_args), small_args, (attn_in, attn_out, ffn_in)
            )
            index, mask, live_own, hidden_own, grad_own = tokens
            attn_in, attn_out, ffn_in = late
        elif len(chunks) == 3:
            (small_args,) = line.close(small_args)
        elif len(chunks) == 4:
            small, up_bias = line.close(*small_params(*small_args))
        elif downs:
            state, downs = line.close(state, downs)
        else:
            state = line.close(*state)
        ready = [number for number, chunk in enumerate(chunks) if line.fresh(chunk)]
        running = parts[ready[0]] if ready else None
    x = state[0]

    small_grads = [None] * LAYERS

    def backward_ffn(layer, sources):
        w1, w2, col = weights[layer][3:]
        y1_low, y1_other, act, slope, n2, r2 = saved[layer][9:]
        gh2, df, sums2 = norm_bwd(sources, n2, r2, small, 2 * layer + 1)
        dw1, dw2, up_sums, part, part_other = ffn_bwd(df, at.swap(df), w1, w2, col, act, slope, y1_low, y1_other)
        small_grads[layer] = [sums2, up_sums]
        return (gh2, part, at.swap(part_other)), dw1, dw2

    def backward_attn(layer, sources):
        wa, wom, wot = weights[layer][:3]
        x_low, x_other, q, k, v, mix_own, mix_other, n1, r1 = saved[layer][:9]
        gh1, da, sums1 = norm_bwd(sources, n1, r1, small, 2 * layer)
        dwq, dwk, dwv, dwo, dwo_sent, attn_sums, part, part_other = attn_bwd(
            core_id, da, at.swap(da), wom, wot, q, k, v, mix_own, mix_other, x_low, x_other, wa, mask
        )
        small_grads[layer] = [sums1] + small_grads[layer] + [attn_sums]
        return (gh1, part, at.swap(part_other)), (dwq, dwk, dwv), (dwo, at.swap(dwo_sent))

    def attn_groups(dqkv, dwo):
        dwq, dwk, dwv = dqkv
        return [dwq, dwk], [dwv, by_core(core, *dwo, 0).reshape(D, HALF)]

    line = Pipe(at) if tiled else Line(at)

    def ffn_chunk(dw1, dw2):
        if tiled:
            flat = [dw.reshape(2 * D, D) for dw in (dw1, dw2)]
            streams = [Stream([unit], part == 0, chip_rows, part * D) for part in range(2) for unit in flat]
            line.add(streams)
            return streams
        chunk = Reduce(at, [[dw1[0]], [dw2[0]]], [[dw1[1]], [dw2[1]]])
        line.add(chunk)
        return chunk

    def attn_chunk(dqkv, dwo, direct):
        first, second = attn_groups(dqkv, dwo)
        if tiled:
            streams = [
                Stream(part, part is first, chip_rows, direct=direct) for part in (first, second)
            ]
            line.add(streams)
            return streams
        chunk = Reduce(at, [first], [second])
        line.add(chunk)
        return chunk

    def table_chunk(tables):
        if tiled:
            streams = [Stream([table], number < 2, table_rows) for number, table in enumerate(tables)]
            line.add(streams)
            return Joined(streams)
        chunk = Reduce(at, [[table] for table in tables[:2]], [[table] for table in tables[2:]])
        line.add(chunk)
        return chunk

    sources, dw1, dw2 = backward_ffn(1, (grad_own, live_own))
    ffn1 = ffn_chunk(dw1, dw2)
    output = x * live_own
    sources = line.step(*sources, extra=output[cap:].astype(BF16) if tiled else None)
    sources, dqkv, dwo = backward_attn(1, sources)
    sources = line.close(*sources)
    output = from_chip(output, line.extra if tiled else send_back(output))
    att1 = attn_chunk(dqkv, dwo, False)
    sources = line.step(*sources)
    sources, dw1, dw2 = backward_ffn(0, sources)
    sources = line.close(*sources)
    ffn0 = ffn_chunk(dw1, dw2)
    sources = line.step(*sources)
    sources, dqkv, dwo = backward_attn(0, sources)
    sources = line.close(*sources)
    att0 = attn_chunk(dqkv, dwo, False)
    sources = line.step(*sources)
    grad_x = sources[0] + sources[1].astype(F32) + sources[2].astype(F32)
    grad_low = grad_x.astype(BF16)
    table_parts = table_grads(index, grad_low, at.swap(grad_low), chips * table_rows)
    table_parts = line.close(*table_parts)
    tab = table_chunk(table_parts)
    line.step(extra=grad_x[cap:].astype(BF16) if tiled else None)
    line.close()
    input_grad = from_chip(grad_x, line.extra if tiled else send_back(grad_x))
    zeros = jnp.zeros((2, HALF), F32)
    vectors = []
    for layer in range(LAYERS):
        mine = small_grads[layer][3][:2]
        vectors.append(by_core(core, mine, zeros, 1).reshape(2, D))
    vectors.append(jnp.stack([small_grads[layer][0][2] for layer in range(LAYERS)]))
    for row in range(2):
        for layer in range(LAYERS):
            vectors.append(jnp.stack([small_grads[layer][norm][row] for norm in range(2)]))
    vectors.append(jnp.stack([small_grads[layer][1][2] for layer in range(LAYERS)]))
    vectors = lax.optimization_barrier(jnp.concatenate(vectors)).reshape(SMALL_ROWS, devices, rows_dev).swapaxes(0, 1)
    ups_grad = jnp.stack([small_grads[layer][2][0] for layer in range(LAYERS)])
    ups_grad = ups_grad.reshape(LAYERS, 2, chips, ff_dev // 2).transpose(2, 0, 1, 3)
    ups_grad = by_core(core, ups_grad, jnp.zeros_like(ups_grad), 1)
    segments = jnp.concatenate(
        [vectors.reshape(devices, cut), ups_grad.reshape(devices, LAYERS * ff_dev)], axis=1
    )
    segments = lax.all_to_all(segments, ("page", "band"), 0, 0, tiled=True)


    def small_outputs(segments):
        segment = jnp.sum(segments, axis=0)
        rows = segment[:cut].reshape(SMALL_ROWS, rows_dev)
        return (
            rows[ROW_ATTN:ROW_OUT].reshape(LAYERS, 2, rows_dev),
            rows[ROW_OUT:ROW_GAIN],
            rows[ROW_GAIN:ROW_SHIFT].reshape(LAYERS, 2, rows_dev),
            rows[ROW_SHIFT:ROW_DOWN].reshape(LAYERS, 2, rows_dev),
            segment[cut:].reshape(LAYERS, ff_dev),
            rows[ROW_DOWN:SMALL_ROWS],
        )

    grads = None
    while line.busy():
        line.step()
        if tiled and grads is None and att0[0].total is not None:
            results = [
                [stream.total for stream in attn[:2] + ffn] for attn, ffn in ((att0, ffn0), (att1, ffn1))
            ]
            parts = []
            for qk, vo, up_a, down_a, up_b, down_b in results:
                mine, send = split(core_id, (qk, vo, up_a, up_b))
                parts += [mine, at.swap(send), down_a, down_b]
            grads = merge(core_id, parts)
            smalls = small_outputs(tie(segments, grads[0]))
            grads, smalls = line.close(grads, smalls)
        else:
            line.close()
    if not tiled:
        smalls = small_outputs(segments)
    if tiled:
        grad_tables = tab.total.reshape(4, table_rows, D)
    else:
        sums = [line.result(chunk) for chunk in (att0, ffn0, att1, ffn1)]
        grad_tables = jnp.stack(line.result(tab)).reshape(4, table_rows, D)
        results = []
        for attn_sum, ffn_sum in ((sums[0], sums[1]), (sums[2], sums[3])):
            attn = jnp.stack(attn_sum)
            ffn = jnp.stack(ffn_sum).reshape(4, chip_rows, D)
            results.append((attn, ffn, ffn))

    if not tiled:
        grads = [[], [], [], []]
        for layer in range(LAYERS):
            attn_sum, up_sum, down_sum = results[layer]
            both = jnp.stack([attn_sum[0], attn_sum[1], up_sum[0], up_sum[2]])
            by_owner = both.reshape(4, CORES, rows_dev, D)
            mine, theirs = pick(by_owner, core, 1), at.swap(pick(by_owner, 1 - core, 1))
            both = by_core(core, mine, theirs, 0).transpose(2, 0, 1, 3)
            attn = both[:, :, :2].reshape(rows_dev, CORES, 4, HALF).swapaxes(1, 2)
            grads[0].append(attn[:, :3].reshape(rows_dev, 3 * D))
            grads[1].append(attn[:, 3].reshape(rows_dev, D))
            ups = both[:, :, 2:].reshape(rows_dev, CORES, 2, chips, ff_dev // 2).transpose(0, 3, 1, 2, 4)
            grads[2].append(ups.reshape(rows_dev, FF))
            grads[3].append(jnp.concatenate([down_sum[1], down_sum[3]]))
        grads = [jnp.stack(pair) for pair in grads]

    return (
        output,
        input_grad,
        grad_tables,
        grads[0],
        smalls[0],
        grads[1],
        smalls[1],
        smalls[2],
        smalls[3],
        grads[2],
        smalls[4],
        grads[3],
        smalls[5],
    )


def solution(mesh):
    both = ("page", "band")
    tokens = P("page", "band", None, None)
    middle = P(None, both, None)
    last = P(None, both)
    third = P(None, None, both)
    return jax.shard_map(
        functools.partial(body, pages=mesh.shape["page"], bands=mesh.shape["band"]),
        mesh=mesh,
        in_specs=(
            tokens,
            P(None, "page", "band", None),
            P(None, "page"),
            P("page", "band"),
            middle,
            middle,
            third,
            middle,
            last,
            third,
            third,
            middle,
            last,
            middle,
            last,
            tokens,
        ),
        out_specs=(
            tokens,
            tokens,
            middle,
            middle,
            third,
            middle,
            last,
            third,
            third,
            middle,
            last,
            middle,
            last,
        ),
        check_vma=False,
    )
```
